256 devices in a mesh: tm: 16 (over z, core), mp: 8 (over y, x_hi), batch: 2 (over x_lo).
Axes of the slice: x: 4 (x_hi: 2, x_lo: 2; x = x_hi * 2 + x_lo), y: 4, z: 8, core: 2. Of those that a mesh axis runs over, the one named last changes fastest.
Arguments:
- frames: bfloat16 [32768, 1024], P(('batch', 'tm')), parts along dimension 0, may hold values from -40 to 40
- norm_gain: float32 [1024], replicated, may hold values from 0.5 to 1.5
- qkv_weight: bfloat16 [3, 1024, 1024], P(None, None, 'mp'), may hold values from -2 to 2
- out_weight: bfloat16 [1024, 1024], P('mp'), may hold values from -0.1875 to 0.1875
- cotangent: bfloat16 [32768, 1024], P(('batch', 'tm')), parts along dimension 0, may hold values from -6 to 6
- pad_mask: int32 [32768], P('batch'), parts along dimension 0, may hold values from 0 to 1, as said below
- utt_lengths: int32 [16], P('batch'), parts along dimension 0, may hold values from 1 to 4096, 16384 in all
Outputs:
- frame_grad: bfloat16 [32768, 1024], P(('batch', 'tm'), 'mp'), parts along dimension 0
- qkv_grad: float32 [6, 1024, 1024], P('batch', 'tm', 'mp'), parts along dimension 0
- out_grad: float32 [2048, 1024], P(('batch', 'mp'), 'tm'), parts along dimension 0
The draws below stay inside these ranges and needn't reach their ends.
There are 2 independent parts, one for each index of `batch`. The reference program is written for one: setup_inputs(seed, part) draws one part's arguments, and reference() takes and returns one part's arrays. A program takes and returns all parts, laid end to end along the dimension named above; an argument that names none is the same for every part. Nothing has to cross between parts.
Inputs may be any that keep to these rules, and one draw needn't show every extreme that they name: `pad_mask`: in each aligned block of 256 frames, the padding frames form the tail of the block, fewer than 128 of them. `utt_lengths`: 8 lengths that sum to 16384; the largest is exactly 4096.
All inputs are finite; a program needn't handle non-finite values.
Results may differ from the reference program's by a relative error of at most 0.012.
The reference program's roundings to bfloat16 on the way count: a program that leaves them out, or rounds other values in their place, can miss the bound.
Values may be sent and summed in bfloat16 or wider, within the bound.
No kernel may reach another device: no remote copies, remote signals or barrier semaphores. Data moves between devices by JAX's collectives and lax.ppermute only.
A program may use at most 64 MiB of HBM per device.

```python
import math
import jax
import jax.numpy as jnp
import numpy as np
from jax import lax

D = 1024
HEADS = 8
HS = 128
CH = 32
UTTS = 8
FRAMES = 16384
MAXLEN = 4096


def draw_frames(key, part):
    base = jax.random.normal(key, (FRAMES, D), jnp.float32)
    return jnp.clip(base, -40.0, 40.0).astype(jnp.bfloat16)


def draw_qkv_weight(key, part):
    noise = jax.random.normal(key, (3, D, D), jnp.float32) * D ** (-0.5)
    return jnp.clip(noise, -2.0, 2.0).astype(jnp.bfloat16)


def draw_pad_mask(key, part):
    block_len = 8 * CH
    tails = jax.random.randint(key, (FRAMES // block_len,), 0, block_len // 2)
    positions = jnp.arange(block_len, dtype=jnp.int32)
    keep = (positions[None, :] < block_len - tails[:, None]).astype(jnp.int32)
    return keep.reshape(FRAMES)


def block_scale(own_key, shape, split, least, top_value):
    gain = 1.0
    for axis_at, blocks in split:
        draws = jax.random.uniform(jax.random.fold_in(jax.random.fold_in(own_key, 6), axis_at), (blocks,), jnp.float32, least / len(split), top_value / len(split))
        gain = gain * jnp.repeat(jnp.exp(draws), shape[axis_at] // blocks).reshape((-1,) + (1,) * (len(shape) - 1 - axis_at))
    return gain


def split_up(amount, total, reach, lean):
    portions = [(1 << 20) // math.isqrt(rank ** lean) + 1 for rank in range(2, amount + 1)]
    surplus, counts = total - reach - (amount - 1), [1] * (amount - 1)
    while surplus > 0:
        movable = [i for i in range(amount - 1) if counts[i] < reach]
        pool, remaining = sum([portions[i] for i in movable]), surplus
        for i in movable:
            addition = min(reach - counts[i], max(1, remaining * portions[i] // pool), surplus)
            counts[i] = counts[i] + addition
            surplus = surplus - addition
    return np.array([reach] + counts)


def uneven(rng, number_of, total, reach, skew):
    if number_of == 2:
        one = jax.random.randint(rng, (), max(1, total - reach), min(reach, total - 1) + 1)
        return jnp.stack([one, total - one])
    lengths = jnp.asarray(split_up(number_of, total, reach, skew), jnp.int32)
    couples = (number_of - 1) // 2
    source_of, taker = lengths[1:1 + 2 * couples:2], lengths[2:2 + 2 * couples:2]
    slack = jnp.minimum(source_of - 1, reach - taker)
    moved = jax.random.randint(jax.random.fold_in(rng, 1), (couples,), 0, 1 << 20) % (slack + 1)
    lengths = lengths.at[1:1 + 2 * couples:2].set(source_of - moved).at[2:2 + 2 * couples:2].set(taker + moved)
    return lengths[jax.random.permutation(jax.random.fold_in(rng, 2), number_of)]


def normal_values(stream_key, dims, width, bound, cuts=(), kind=jnp.bfloat16):
    gain = block_scale(stream_key, dims, cuts, -0.22, 0.18) if cuts else 1.0
    array = jax.random.normal(stream_key, dims, jnp.float32) * width * gain
    return jnp.minimum(jnp.maximum(array, -bound), bound).astype(kind)


def setup_inputs(seed: int = 0, part: int = 0) -> dict:
    seeds = jax.random.split(jax.random.key(seed), 8)
    own_keys = jax.random.split(jax.random.fold_in(seeds[7], part), 8)
    frames = draw_frames(jax.random.fold_in(jax.random.fold_in(seeds[7], part), 71), part)
    norm_gain = jnp.clip(1.0 + 0.1 * jax.random.normal(seeds[1], (D,), jnp.float32), 0.5, 1.5)
    qkv_weight = draw_qkv_weight(jax.random.fold_in(seeds[7], 71), part)
    out_weight = normal_values(seeds[3], (D, D), D ** -0.5, 0.1875, ((0, 8),))
    cotangent = normal_values(own_keys[4], (FRAMES, D), 1.0, 6.0, ((0, 16),))
    pad_mask = draw_pad_mask(jax.random.fold_in(jax.random.fold_in(seeds[7], part), 71), part)
    utt_lengths = uneven(own_keys[6], UTTS, FRAMES, MAXLEN, 2).astype(jnp.int32)
    return {"frames": frames, "norm_gain": norm_gain, "qkv_weight": qkv_weight, "out_weight": out_weight, "cotangent": cotangent, "pad_mask": pad_mask, "utt_lengths": utt_lengths}


EPSILON = 1e-05

def layer_norm(frames, norm_gain):
    values = frames.astype(jnp.float32)
    center = values - lax.optimization_barrier(jnp.mean(values, axis=-1, keepdims=True))
    inverse = lax.rsqrt(lax.optimization_barrier(jnp.mean(center * center, axis=-1, keepdims=True)) + EPSILON)
    normal_form = center * inverse
    return (normal_form, inverse, (normal_form * norm_gain).astype(jnp.bfloat16))

def norm_backward(incoming, normal_form, inverse, norm_gain):
    scaled = incoming * norm_gain
    mean_grad = lax.optimization_barrier(jnp.mean(scaled, axis=-1, keepdims=True))
    mean_proj = lax.optimization_barrier(jnp.mean(scaled * normal_form, axis=-1, keepdims=True))
    return inverse * (scaled - mean_grad - normal_form * mean_proj)

def windows(block_rows):
    block_count = block_rows.shape[0] - 2
    return jnp.concatenate([block_rows[:block_count], block_rows[1:block_count + 1], block_rows[2:]], axis=1)

def fold_keys(window):
    block_width = window.shape[1] // 3
    trailing = [(0, 0)] * (window.ndim - 1)
    pieces = [jnp.pad(window[:, offset * block_width:(offset + 1) * block_width], [(offset, 2 - offset)] + trailing) for offset in range(3)]
    return pieces[0] + pieces[1] + pieces[2]

def permitted(query_start, query_count, key_start, key_count, pad_mask, utt_lengths):
    utt_ends = jnp.cumsum(utt_lengths).astype(jnp.int32)
    query_pos = query_start + jnp.arange(query_count, dtype=jnp.int32)
    key_pos = key_start + jnp.arange(key_count, dtype=jnp.int32)

    def segment(positions):
        return lax.optimization_barrier(jnp.sum((utt_ends[None, :] <= positions[:, None]).astype(jnp.int32), axis=1))
    padded = jnp.pad(pad_mask, 2 * CH)
    live_keys = lax.dynamic_slice(padded, (jnp.asarray(key_start + 2 * CH, jnp.int32),), (key_count,))
    query_cells = query_pos.reshape(-1, CH)
    query_seg = segment(query_pos).reshape(-1, CH)
    key_cells = windows(key_pos.reshape(-1, CH))
    key_seg = windows(segment(key_pos).reshape(-1, CH))
    key_live = windows(live_keys.reshape(-1, CH))
    same_utt = query_seg[:, :, None] == key_seg[:, None, :]
    return same_utt & ((key_live[:, None, :] == 1) | (query_cells[:, :, None] == key_cells[:, None, :]))

def product(form, left, right):
    return jnp.einsum(form, left.astype(jnp.float32), right.astype(jnp.float32), precision=lax.Precision.HIGHEST)

def attend(queries, grad_rows, key_blocks, value_blocks, allowed):
    score_scale = HS ** (-0.5)
    key_win = windows(key_blocks)
    value_win = windows(value_blocks)
    scores = product('cihd,cjhd->chij', queries, key_win) * score_scale
    scores = jnp.where(allowed[:, None], scores, -1e+30)
    row_max = lax.optimization_barrier(jnp.max(scores, axis=-1, keepdims=True))
    weights = jnp.exp(scores - row_max)
    attn_probs = weights / lax.optimization_barrier(jnp.sum(weights, axis=-1, keepdims=True))
    rounded = attn_probs.astype(jnp.bfloat16)
    mixed_out = product('chij,cjhd->cihd', rounded, value_win).astype(jnp.bfloat16)
    prob_grad = product('cihd,cjhd->chij', grad_rows, value_win)
    centre = lax.optimization_barrier(jnp.sum(attn_probs * prob_grad, axis=-1, keepdims=True))
    score_grad = (attn_probs * (prob_grad - centre) * score_scale).astype(jnp.bfloat16)
    query_grad = product('chij,cjhd->cihd', score_grad, key_win)
    key_grad = fold_keys(product('chij,cihd->cjhd', score_grad, queries))
    value_grad = fold_keys(product('chij,cihd->cjhd', rounded, grad_rows))
    return (mixed_out, query_grad, key_grad, value_grad)

def reference(frames, norm_gain, qkv_weight, out_weight, cotangent, pad_mask, utt_lengths):
    normal_form, inverse, normed = layer_norm(frames, norm_gain)
    projected = [jnp.dot(normed, qkv_weight[piece], preferred_element_type=jnp.float32).astype(jnp.bfloat16) for piece in range(3)]
    masked = cotangent * pad_mask.astype(jnp.bfloat16)[:, None]
    grad_heads = jnp.dot(masked, out_weight.T, preferred_element_type=jnp.float32).astype(jnp.bfloat16)
    block_count = FRAMES // CH

    def blocks(tensor):
        return tensor.reshape(block_count, CH, HEADS, HS)

    def extend(tensor):
        return jnp.pad(blocks(tensor), ((1, 1), (0, 0), (0, 0), (0, 0)))
    allowed = permitted(0, FRAMES, -CH, FRAMES + 2 * CH, pad_mask, utt_lengths)
    mixed_out, query_grad, key_ext, value_ext = attend(blocks(projected[0]), blocks(grad_heads), extend(projected[1]), extend(projected[2]), allowed)
    all_grads = [gradient.reshape(FRAMES, D).astype(jnp.bfloat16) for gradient in (query_grad, key_ext[1:-1], value_ext[1:-1])]
    qkv_grad = jnp.stack([jnp.dot(normed.T, gradient, preferred_element_type=jnp.float32) for gradient in all_grads])
    out_grad = jnp.dot(mixed_out.reshape(FRAMES, D).T, masked, preferred_element_type=jnp.float32)
    incoming = jnp.dot(all_grads[0], qkv_weight[0].T, preferred_element_type=jnp.float32)
    incoming = incoming + jnp.dot(all_grads[1], qkv_weight[1].T, preferred_element_type=jnp.float32)
    incoming = incoming + jnp.dot(all_grads[2], qkv_weight[2].T, preferred_element_type=jnp.float32)
    frame_grad = norm_backward(incoming, normal_form, inverse, norm_gain).astype(jnp.bfloat16)
    return (frame_grad, qkv_grad, out_grad)
```

```python
import jax
import jax.numpy as jnp
from jax import lax
from jax.experimental import pallas as pl
from jax.experimental.pallas import tpu as pltpu
from jax.sharding import PartitionSpec as P

HS = 128
CH = 32
HALO = 64
EPSILON = 1e-05
SCALE = HS ** (-0.5)
F32 = jnp.float32
BF16 = jnp.bfloat16


def rows_by_rows(left, right):
    return lax.dot_general(left, right, (((1,), (1,)), ((), ())), preferred_element_type=F32)


def cols_by_cols(left, right):
    return lax.dot_general(left, right, (((0,), (0,)), ((), ())), preferred_element_type=F32)


def plain(left, right):
    return jnp.dot(left, right, preferred_element_type=F32)


def normalised(values):
    values = values.astype(F32)
    center = values - jnp.mean(values, axis=-1, keepdims=True)
    inverse = lax.rsqrt(jnp.mean(center * center, axis=-1, keepdims=True) + EPSILON)
    return center * inverse, inverse


def pad_rows(pad_ref, first, count):
    total = pad_ref.shape[0]
    return [pad_ref[pl.ds(jnp.clip(first + i, 0, total - 1), 1), :] for i in range(count)]


def as_columns(rows):
    height = -(-len(rows) // 8) * 8
    full = jnp.concatenate(rows + [jnp.zeros_like(rows[0])] * (height - len(rows)), axis=0)
    return full.T


def project_body(frames_ref, gain_ref, qkv_ref, out_ref, cot_ref, pad_ref, proj_ref, normed_ref, w_scr):
    step = pl.program_id(0)
    rows = frames_ref.shape[0]

    @pl.when(step == 0)
    def _():
        for m in range(3):
            w_scr[:, m * HS : (m + 1) * HS] = qkv_ref[m]

    normal_form, _ = normalised(frames_ref[...])
    normed = (normal_form * gain_ref[...]).astype(BF16)
    normed_ref[...] = normed
    qkv = plain(normed, w_scr[...]).astype(BF16)
    for m in range(3):
        proj_ref[m] = qkv[:, m * HS : (m + 1) * HS]
    per_step = rows // 128
    first = (lax.axis_index("tm") * pl.num_programs(0) + step) * per_step
    live = as_columns([r.astype(F32) for r in pad_rows(pad_ref, first, per_step)])
    live = jnp.concatenate([live[:, i : i + 1] for i in range(per_step)], axis=0)
    grads = rows_by_rows(cot_ref[...], out_ref[...])
    proj_ref[3] = jnp.where(live == 1.0, grads, 0.0).astype(BF16)


def project(frames, gain, qkv_weight, out_weight, cotangent, pad2d):
    count, width = frames.shape
    rows = 256
    whole = lambda *shape: pl.BlockSpec(shape, lambda i: (0,) * len(shape))
    return pl.pallas_call(
        project_body,
        grid=(count // rows,),
        in_specs=[
            pl.BlockSpec((rows, width), lambda i: (i, 0)),
            whole(1, width),
            whole(*qkv_weight.shape),
            whole(*out_weight.shape),
            pl.BlockSpec((rows, width), lambda i: (i, 0)),
            whole(*pad2d.shape),
        ],
        out_specs=[
            pl.BlockSpec((4, rows, HS), lambda i: (0, i, 0)),
            pl.BlockSpec((rows, width), lambda i: (i, 0)),
        ],
        out_shape=[
            jax.ShapeDtypeStruct((4, count, HS), BF16),
            jax.ShapeDtypeStruct((count, width), BF16),
        ],
        scratch_shapes=[pltpu.VMEM((width, 3 * HS), BF16)],
        compiler_params=pltpu.CompilerParams(vmem_limit_bytes=48 << 20),
        name="project",
    )(frames, gain, qkv_weight, out_weight, cotangent, pad2d)


def attend_body(len_ref, proj_ref, halo_ref, gain_ref, qkv_ref, out_ref, pad_ref, grads_ref, mixed_ref, x_scr):
    count = proj_ref.shape[1]
    tiles = count // 128 + 1
    shard = lax.axis_index("tm")
    first_block = shard * (count // 128) - 1
    normal_form, _ = normalised(halo_ref[0])
    normed = (normal_form * gain_ref[...]).astype(BF16)
    blocks = tiles + 1
    live_rows = [r.astype(F32) for r in pad_rows(pad_ref, first_block, blocks)]
    live_cols = as_columns(live_rows)
    halo_live = jnp.concatenate([live_cols[HALO:, 0:1], live_cols[:HALO, blocks - 1 : blocks]], axis=0)
    zeros = jnp.zeros((HALO, HS), BF16)
    for m in range(4):
        if m < 3:
            part = plain(normed, qkv_ref[m])
        else:
            part = jnp.where(halo_live == 1.0, rows_by_rows(halo_ref[1], out_ref[...]), 0.0)
        part = part.astype(BF16)
        x_scr[m, 0:HALO, :] = zeros
        x_scr[m, HALO : 2 * HALO, :] = part[:HALO]
        x_scr[m, 2 * HALO : 2 * HALO + count, :] = proj_ref[m]
        x_scr[m, 2 * HALO + count : 3 * HALO + count, :] = part[HALO:]
        x_scr[m, 3 * HALO + count :, :] = zeros

    ends = []
    total = 0
    for u in range(len_ref.shape[0]):
        total = total + len_ref[u]
        ends.append(total)

    def segment(positions):
        found = jnp.zeros(positions.shape, jnp.int32)
        for end in ends:
            found = found + jnp.where(positions >= end, 1, 0)
        return found.astype(F32)

    lane = lax.broadcasted_iota(jnp.int32, (1, 128), 1)
    codes = []
    for b in range(blocks):
        at = (first_block + b) * 128 + lane
        codes.append(jnp.where((live_rows[b] == 1.0) & (at >= 0), segment(at), -1.0))
    code_cols = as_columns(codes)

    keys = 192
    key_at = lax.broadcasted_iota(jnp.int32, (keys, 128), 0)
    query_at = lax.broadcasted_iota(jnp.int32, (keys, 128), 1)
    apart = key_at // CH - query_at // CH
    in_band = (apart >= 0) & (apart <= 2)
    same = key_at == query_at + CH

    carry_k = carry_v = None
    for t in range(tiles):
        base = 128 * t
        q = x_scr[0, base + HALO : base + HALO + 128, :]
        g = x_scr[3, base + HALO : base + HALO + 128, :]
        k = x_scr[1, base + CH : base + CH + keys, :]
        v = x_scr[2, base + CH : base + CH + keys, :]
        query_seg = segment((first_block + t) * 128 + HALO + lane)
        code = jnp.concatenate([code_cols[CH:, t : t + 1], code_cols[: keys - 96, t + 1 : t + 2]], axis=0)
        allowed = in_band & ((code == query_seg) | same)
        scores = jnp.where(allowed, rows_by_rows(k, q) * SCALE, -1e30)
        weights = jnp.exp(scores - jnp.max(scores, axis=0, keepdims=True))
        probs = weights * (1.0 / jnp.sum(weights, axis=0, keepdims=True))
        rounded = probs.astype(BF16)
        prob_grad = rows_by_rows(v, g)
        centre = jnp.sum(probs * prob_grad, axis=0, keepdims=True)
        score_grad = (probs * (prob_grad - centre) * SCALE).astype(BF16)
        mixed = cols_by_cols(rounded, v).astype(BF16)
        query_grad = cols_by_cols(score_grad, k).astype(BF16)
        key_grad = plain(score_grad, q)
        value_grad = plain(rounded, g)
        live = jnp.concatenate([live_cols[HALO:, t : t + 1], live_cols[:HALO, t + 1 : t + 2]], axis=0)
        mixed = jnp.where(live == 1.0, mixed, jnp.zeros_like(mixed))
        lo, hi = (HALO if t == 0 else 0), (HALO if t == tiles - 1 else 128)
        at = base - HALO
        mixed_ref[at + lo : at + hi, :] = mixed[lo:hi]
        grads_ref[at + lo : at + hi, 0:HS] = query_grad[lo:hi]
        if t > 0:
            key_grad = jnp.concatenate([key_grad[:64] + carry_k, key_grad[64:]], axis=0)
            value_grad = jnp.concatenate([value_grad[:64] + carry_v, value_grad[64:]], axis=0)
        carry_k, carry_v = key_grad[128:], value_grad[128:]
        lo, hi = (96 if t == 0 else 0), (96 if t == tiles - 1 else 128)
        at = base - 96
        grads_ref[at + lo : at + hi, HS : 2 * HS] = key_grad[lo:hi].astype(BF16)
        grads_ref[at + lo : at + hi, 2 * HS : 3 * HS] = value_grad[lo:hi].astype(BF16)


def attend(lengths, proj, halo, gain, qkv_weight, out_weight, pad2d):
    count = proj.shape[1]
    vmem = pl.BlockSpec(memory_space=pltpu.VMEM)
    return pl.pallas_call(
        attend_body,
        in_specs=[pl.BlockSpec(memory_space=pltpu.SMEM)] + [vmem] * 6,
        out_specs=[vmem, vmem],
        out_shape=[
            jax.ShapeDtypeStruct((count, 3 * HS), BF16),
            jax.ShapeDtypeStruct((count, HS), BF16),
        ],
        scratch_shapes=[pltpu.VMEM((4, count + 4 * HALO, HS), BF16)],
        compiler_params=pltpu.CompilerParams(vmem_limit_bytes=48 << 20),
        name="attend",
    )(lengths, proj, halo, gain, qkv_weight, out_weight, pad2d)


def input_body(frames_ref, gain_ref, qkv_ref, grads_ref, term_ref, w_scr):
    @pl.when(pl.program_id(0) == 0)
    def _():
        for m in range(3):
            w_scr[:, m * HS : (m + 1) * HS] = qkv_ref[m]

    incoming = rows_by_rows(grads_ref[...], w_scr[...])
    normal_form, inverse = normalised(frames_ref[...])
    scaled = incoming * gain_ref[...]
    mean_grad = jnp.mean(scaled, axis=-1, keepdims=True)
    mean_proj = jnp.mean(scaled * normal_form, axis=-1, keepdims=True)
    result = (inverse * (scaled - mean_grad - normal_form * mean_proj)).astype(BF16)
    for p in range(term_ref.shape[0]):
        term_ref[p] = result[:, p * 128 : (p + 1) * 128]


def input_terms(frames, gain, qkv_weight, grads):
    count, width = frames.shape
    rows = 256
    whole = lambda *shape: pl.BlockSpec(shape, lambda i: (0,) * len(shape))
    return pl.pallas_call(
        input_body,
        grid=(count // rows,),
        in_specs=[
            pl.BlockSpec((rows, width), lambda i: (i, 0)),
            whole(1, width),
            whole(*qkv_weight.shape),
            pl.BlockSpec((rows, 3 * HS), lambda i: (i, 0)),
        ],
        out_specs=pl.BlockSpec((width // 128, rows, 128), lambda i: (0, i, 0)),
        out_shape=jax.ShapeDtypeStruct((width // 128, count, 128), BF16),
        scratch_shapes=[pltpu.VMEM((width, 3 * HS), BF16)],
        compiler_params=pltpu.CompilerParams(vmem_limit_bytes=48 << 20),
        name="input_terms",
    )(frames, gain, qkv_weight, grads)


def weight_body(normed_ref, cot_ref, grads_ref, mixed_ref, term_ref):
    shards, _, part, _ = term_ref.shape
    qkv = cols_by_cols(normed_ref[...], grads_ref[...]).astype(BF16)
    out = cols_by_cols(cot_ref[...], mixed_ref[...]).astype(BF16)
    for s in range(shards):
        for m in range(3):
            term_ref[s, m] = qkv[s * part : (s + 1) * part, m * HS : (m + 1) * HS]
        term_ref[s, 3] = out[s * part : (s + 1) * part]


def weight_terms(normed, cotangent, grads, mixed, shards):
    count, width = normed.shape
    vmem = pl.BlockSpec(memory_space=pltpu.VMEM)
    return pl.pallas_call(
        weight_body,
        in_specs=[vmem] * 4,
        out_specs=vmem,
        out_shape=jax.ShapeDtypeStruct((shards, 4, width // shards, HS), BF16),
        compiler_params=pltpu.CompilerParams(vmem_limit_bytes=48 << 20),
        name="weight_terms",
    )(normed, cotangent, grads, mixed)


def on_device(frames, norm_gain, qkv_weight, out_weight, cotangent, pad_mask, utt_lengths):
    shards = lax.axis_size("tm")
    up = [(i, i + 1) for i in range(shards - 1)]
    down = [(i + 1, i) for i in range(shards - 1)]
    ends = jnp.stack([frames[-HALO:], cotangent[-HALO:]])
    starts = jnp.stack([frames[:HALO], cotangent[:HALO]])
    halo = jnp.concatenate([lax.ppermute(ends, "tm", up), lax.ppermute(starts, "tm", down)], axis=1)
    gain = norm_gain[None, :]
    pad2d = pad_mask.reshape(-1, 128)
    proj, normed = project(frames, gain, qkv_weight, out_weight, cotangent, pad2d)
    grads, mixed = attend(utt_lengths, proj, halo, gain, qkv_weight, out_weight, pad2d)
    terms = input_terms(frames, gain, qkv_weight, grads)
    weights = weight_terms(normed, cotangent, grads, mixed, shards)
    terms = lax.all_to_all(terms, "mp", 0, 0, tiled=True)
    weights = lax.all_to_all(weights, "tm", 0, 0, tiled=True)
    frame_grad = terms.astype(F32).sum(axis=0).astype(BF16)
    summed = weights.astype(F32).sum(axis=0)
    return frame_grad, summed[:3], summed[3].T


def solution(mesh):
    placed = (
        P(("batch", "tm"), None),
        P(),
        P(None, None, "mp"),
        P("mp", None),
        P(("batch", "tm"), None),
        P("batch"),
        P("batch"),
    )
    return jax.shard_map(
        on_device,
        mesh=mesh,
        in_specs=placed,
        out_specs=(P(("batch", "tm"), "mp"), P("batch", "tm", "mp"), P(("batch", "mp"), "tm")),
        check_vma=False,
    )
```

```python
import jax
import jax.numpy as jnp
from jax import lax
from jax.experimental import pallas as pl
from jax.experimental.pallas import tpu as pltpu
from jax.sharding import PartitionSpec as P

HS = 128
CH = 32
HALO = 64
EPSILON = 1e-05
SCALE = HS ** (-0.5)
F32 = jnp.float32
BF16 = jnp.bfloat16


def rows_by_rows(left, right):
    return lax.dot_general(left, right, (((1,), (1,)), ((), ())), preferred_element_type=F32)


def cols_by_cols(left, right):
    return lax.dot_general(left, right, (((0,), (0,)), ((), ())), preferred_element_type=F32)


def plain(left, right):
    return jnp.dot(left, right, preferred_element_type=F32)


def normalised(values):
    values = values.astype(F32)
    center = values - jnp.mean(values, axis=-1, keepdims=True)
    inverse = lax.rsqrt(jnp.mean(center * center, axis=-1, keepdims=True) + EPSILON)
    return center * inverse, inverse


def pad_rows(pad_ref, first, count):
    total = pad_ref.shape[0]
    return [pad_ref[pl.ds(jnp.clip(first + i, 0, total - 1), 1), :] for i in range(count)]


def as_columns(rows):
    height = -(-len(rows) // 8) * 8
    full = jnp.concatenate(rows + [jnp.zeros_like(rows[0])] * (height - len(rows)), axis=0)
    return full.T


def project_body(frames_ref, gain_ref, qkv_ref, out_ref, cot_ref, pad_ref, proj_ref, normed_ref, w_scr):
    step = pl.program_id(0)
    rows = frames_ref.shape[0]

    @pl.when(step == 0)
    def _():
        for m in range(3):
            w_scr[:, m * HS : (m + 1) * HS] = qkv_ref[m]

    normal_form, _ = normalised(frames_ref[...])
    normed = (normal_form * gain_ref[...]).astype(BF16)
    normed_ref[...] = normed
    qkv = plain(normed, w_scr[...]).astype(BF16)
    for m in range(3):
        proj_ref[m] = qkv[:, m * HS : (m + 1) * HS]
    per_step = rows // 128
    first = (lax.axis_index("tm") * pl.num_programs(0) + step) * per_step
    live = as_columns([r.astype(F32) for r in pad_rows(pad_ref, first, per_step)])
    live = jnp.concatenate([live[:, i : i + 1] for i in range(per_step)], axis=0)
    grads = rows_by_rows(cot_ref[...], out_ref[...])
    proj_ref[3] = jnp.where(live == 1.0, grads, 0.0).astype(BF16)


def project(frames, gain, qkv_weight, out_weight, cotangent, pad2d):
    count, width = frames.shape
    rows = 256
    whole = lambda *shape: pl.BlockSpec(shape, lambda i: (0,) * len(shape))
    return pl.pallas_call(
        project_body,
        grid=(count // rows,),
        in_specs=[
            pl.BlockSpec((rows, width), lambda i: (i, 0)),
            whole(1, width),
            whole(*qkv_weight.shape),
            whole(*out_weight.shape),
            pl.BlockSpec((rows, width), lambda i: (i, 0)),
            whole(*pad2d.shape),
        ],
        out_specs=[
            pl.BlockSpec((4, rows, HS), lambda i: (0, i, 0)),
            pl.BlockSpec((rows, width), lambda i: (i, 0)),
        ],
        out_shape=[
            jax.ShapeDtypeStruct((4, count, HS), BF16),
            jax.ShapeDtypeStruct((count, width), BF16),
        ],
        scratch_shapes=[pltpu.VMEM((width, 3 * HS), BF16)],
        compiler_params=pltpu.CompilerParams(vmem_limit_bytes=48 << 20),
        name="project",
    )(frames, gain, qkv_weight, out_weight, cotangent, pad2d)


def attend_body(len_ref, proj_ref, halo_ref, gain_ref, qkv_ref, out_ref, pad_ref, grads_ref, mixed_ref, x_scr):
    count = proj_ref.shape[1]
    tiles = count // 128 + 1
    shard = lax.axis_index("tm")
    first_block = shard * (count // 128) - 1
    normal_form, _ = normalised(halo_ref[0])
    normed = (normal_form * gain_ref[...]).astype(BF16)
    blocks = tiles + 1
    live_rows = [r.astype(F32) for r in pad_rows(pad_ref, first_block, blocks)]
    live_cols = as_columns(live_rows)
    halo_live = jnp.concatenate([live_cols[HALO:, 0:1], live_cols[:HALO, blocks - 1 : blocks]], axis=0)
    zeros = jnp.zeros((HALO, HS), BF16)
    for m in range(4):
        if m < 3:
            part = plain(normed, qkv_ref[m])
        else:
            part = jnp.where(halo_live == 1.0, rows_by_rows(halo_ref[1], out_ref[...]), 0.0)
        part = part.astype(BF16)
        x_scr[m, 0:HALO, :] = zeros
        x_scr[m, HALO : 2 * HALO, :] = part[:HALO]
        x_scr[m, 2 * HALO : 2 * HALO + count, :] = proj_ref[m]
        x_scr[m, 2 * HALO + count : 3 * HALO + count, :] = part[HALO:]
        x_scr[m, 3 * HALO + count :, :] = zeros

    ends = []
    total = 0
    for u in range(len_ref.shape[0]):
        total = total + len_ref[u]
        ends.append(total)

    def segment(positions):
        found = jnp.zeros(positions.shape, jnp.int32)
        for end in ends:
            found = found + jnp.where(positions >= end, 1, 0)
        return found.astype(F32)

    lane = lax.broadcasted_iota(jnp.int32, (1, 128), 1)
    codes = []
    for b in range(blocks):
        at = (first_block + b) * 128 + lane
        codes.append(jnp.where((live_rows[b] == 1.0) & (at >= 0), segment(at), -1.0))
    code_cols = as_columns(codes)

    keys = 192
    key_at = lax.broadcasted_iota(jnp.int32, (keys, 128), 0)
    query_at = lax.broadcasted_iota(jnp.int32, (keys, 128), 1)
    apart = key_at // CH - query_at // CH
    in_band = (apart >= 0) & (apart <= 2)
    same = key_at == query_at + CH

    carry_k = carry_v = None
    for t in range(tiles):
        base = 128 * t
        q = x_scr[0, base + HALO : base + HALO + 128, :]
        g = x_scr[3, base + HALO : base + HALO + 128, :]
        k = x_scr[1, base + CH : base + CH + keys, :]
        v = x_scr[2, base + CH : base + CH + keys, :]
        query_seg = segment((first_block + t) * 128 + HALO + lane)
        code = jnp.concatenate([code_cols[CH:, t : t + 1], code_cols[: keys - 96, t + 1 : t + 2]], axis=0)
        allowed = in_band & ((code == query_seg) | same)
        scores = jnp.where(allowed, rows_by_rows(k, q) * SCALE, -1e30)
        weights = jnp.exp(scores - jnp.max(scores, axis=0, keepdims=True))
        probs = weights * (1.0 / jnp.sum(weights, axis=0, keepdims=True))
        rounded = probs.astype(BF16)
        prob_grad = rows_by_rows(v, g)
        centre = jnp.sum(probs * prob_grad, axis=0, keepdims=True)
        score_grad = (probs * (prob_grad - centre) * SCALE).astype(BF16)
        mixed = cols_by_cols(rounded, v).astype(BF16)
        query_grad = cols_by_cols(score_grad, k).astype(BF16)
        key_grad = plain(score_grad, q)
        value_grad = plain(rounded, g)
        live = jnp.concatenate([live_cols[HALO:, t : t + 1], live_cols[:HALO, t + 1 : t + 2]], axis=0)
        mixed = jnp.where(live == 1.0, mixed, jnp.zeros_like(mixed))
        lo, hi = (HALO if t == 0 else 0), (HALO if t == tiles - 1 else 128)
        at = base - HALO
        mixed_ref[at + lo : at + hi, :] = mixed[lo:hi]
        grads_ref[at + lo : at + hi, 0:HS] = query_grad[lo:hi]
        if t > 0:
            key_grad = jnp.concatenate([key_grad[:64] + carry_k, key_grad[64:]], axis=0)
            value_grad = jnp.concatenate([value_grad[:64] + carry_v, value_grad[64:]], axis=0)
        carry_k, carry_v = key_grad[128:], value_grad[128:]
        lo, hi = (96 if t == 0 else 0), (96 if t == tiles - 1 else 128)
        at = base - 96
        grads_ref[at + lo : at + hi, HS : 2 * HS] = key_grad[lo:hi].astype(BF16)
        grads_ref[at + lo : at + hi, 2 * HS : 3 * HS] = value_grad[lo:hi].astype(BF16)


def attend(lengths, proj, halo, gain, qkv_weight, out_weight, pad2d):
    count = proj.shape[1]
    vmem = pl.BlockSpec(memory_space=pltpu.VMEM)
    return pl.pallas_call(
        attend_body,
        in_specs=[pl.BlockSpec(memory_space=pltpu.SMEM)] + [vmem] * 6,
        out_specs=[vmem, vmem],
        out_shape=[
            jax.ShapeDtypeStruct((count, 3 * HS), BF16),
            jax.ShapeDtypeStruct((count, HS), BF16),
        ],
        scratch_shapes=[pltpu.VMEM((4, count + 4 * HALO, HS), BF16)],
        compiler_params=pltpu.CompilerParams(vmem_limit_bytes=48 << 20),
        name="attend",
    )(lengths, proj, halo, gain, qkv_weight, out_weight, pad2d)


def input_body(frames_ref, gain_ref, qkv_ref, grads_ref, *rest):
    outs, w_scr = rest[:-1], rest[-1]
    place = lax.axis_index("mp")
    y, xh = place // 2, place % 2

    @pl.when(pl.program_id(0) == 0)
    def _():
        for m in range(3):
            w_scr[:, m * HS : (m + 1) * HS] = qkv_ref[m]

    incoming = rows_by_rows(grads_ref[...], w_scr[...])
    normal_form, inverse = normalised(frames_ref[...])
    scaled = incoming * gain_ref[...]
    mean_grad = jnp.mean(scaled, axis=-1, keepdims=True)
    mean_proj = jnp.mean(scaled * normal_form, axis=-1, keepdims=True)
    result = (inverse * (scaled - mean_grad - normal_form * mean_proj)).astype(BF16)
    if len(outs) == 4:
        for p in range(4):
            for k in range(4):

                @pl.when((p - y) % 4 == k)
                def _():
                    for h in range(2):
                        at = (2 * p + h) * 128
                        outs[k][h] = result[:, at : at + 128]
    else:
        for p in range(4):
            low = result[:, 256 * p : 256 * p + 128]
            high = result[:, 256 * p + 128 : 256 * p + 256]
            away = (p - y + 4) % 4
            outs[0][away] = jnp.where(xh == 0, low, high)
            outs[1][away] = jnp.where(xh == 0, high, low)


def input_terms(frames, gain, qkv_weight, grads, half, pair_first):
    count, width = frames.shape
    rows = 256
    steps = count // rows // 2
    first = half * steps
    whole = lambda *shape: pl.BlockSpec(shape, lambda i: (0,) * len(shape))
    lead, n_outs = (4, 2) if pair_first else (2, 4)
    return pl.pallas_call(
        input_body,
        grid=(steps,),
        in_specs=[
            pl.BlockSpec((rows, width), lambda i: (i + first, 0)),
            whole(1, width),
            whole(*qkv_weight.shape),
            pl.BlockSpec((rows, 3 * HS), lambda i: (i + first, 0)),
        ],
        out_specs=[pl.BlockSpec((lead, rows, 128), lambda i: (0, i, 0))] * n_outs,
        out_shape=[jax.ShapeDtypeStruct((lead, count // 2, 128), BF16)] * n_outs,
        scratch_shapes=[pltpu.VMEM((width, 3 * HS), BF16)],
        compiler_params=pltpu.CompilerParams(vmem_limit_bytes=48 << 20),
        name="input_terms_pair" if pair_first else "input_terms_ring",
    )(frames, gain, qkv_weight, grads)


def weight_body(normed_ref, cot_ref, grads_ref, mixed_ref, keep_ref, send_ref):
    place = lax.axis_index("tm")
    core, zl, zh = place % 2, (place // 2) % 2, place // 4
    qkv = cols_by_cols(normed_ref[...], grads_ref[...]).astype(BF16)
    out = cols_by_cols(cot_ref[...], mixed_ref[...]).astype(BF16)
    full = jnp.concatenate([qkv, out], axis=1)
    for h in range(4):
        away = (h - zh + 4) % 4
        for l in range(2):
            side = (l - zl + 2) % 2
            at = (2 * h + l) * 128
            low, high = full[at : at + 64], full[at + 64 : at + 128]
            keep = jnp.where(core == 0, low, high)
            send = jnp.where(core == 0, high, low)
            for m in range(4):
                keep_ref[side, away, m] = keep[:, m * HS : (m + 1) * HS]
                send_ref[side, away, m] = send[:, m * HS : (m + 1) * HS]


def weight_terms(normed, cotangent, grads, mixed):
    count, width = normed.shape
    vmem = pl.BlockSpec(memory_space=pltpu.VMEM)
    part = jax.ShapeDtypeStruct((2, 4, 4, width // 16, HS), BF16)
    return pl.pallas_call(
        weight_body,
        in_specs=[vmem] * 4,
        out_specs=[vmem] * 2,
        out_shape=[part] * 2,
        compiler_params=pltpu.CompilerParams(vmem_limit_bytes=48 << 20),
        name="weight_terms",
    )(normed, cotangent, grads, mixed)


def shifted(x, axis, by):
    size = lax.axis_size(axis)
    return lax.ppermute(x, axis, [(i, (i + by) % size) for i in range(size)])


def swapped(x, axis, bit):
    return lax.ppermute(x, axis, [(i, i ^ bit) for i in range(lax.axis_size(axis))])


def total(*parts):
    summed = parts[0].astype(F32)
    for part in parts[1:]:
        summed = summed + part.astype(F32)
    return summed


def on_device(frames, norm_gain, qkv_weight, out_weight, cotangent, pad_mask, utt_lengths):
    shards = lax.axis_size("tm")
    up = [(i, i + 1) for i in range(shards - 1)]
    down = [(i + 1, i) for i in range(shards - 1)]
    ends = jnp.stack([frames[-HALO:], cotangent[-HALO:]])
    starts = jnp.stack([frames[:HALO], cotangent[:HALO]])
    halo = jnp.concatenate([lax.ppermute(ends, "tm", up), lax.ppermute(starts, "tm", down)], axis=1)
    gain = norm_gain[None, :]
    pad2d = pad_mask.reshape(-1, 128)
    proj, normed = project(frames, gain, qkv_weight, out_weight, cotangent, pad2d)
    grads, mixed = attend(utt_lengths, proj, halo, gain, qkv_weight, out_weight, pad2d)
    keep, send = weight_terms(normed, cotangent, grads, mixed)
    other = swapped(send, "tm", 1)
    (frames_b, grads_b), _ = lax.optimization_barrier(((frames, grads), send))
    near, across = input_terms(frames_b, gain, qkv_weight, grads_b, 1, True)
    across = swapped(across, "mp", 1)
    ring = input_terms(frames_b, gain, qkv_weight, grads_b, 0, False)
    ring_in = [shifted(ring[k], "mp", 2 * k) for k in (2, 1, 3)]
    stay = total(keep[0], other[0]).astype(BF16)
    cross = swapped(total(keep[1], other[1]).astype(BF16), "tm", 2)
    pair = [total(stay[k], cross[k]) for k in range(4)]
    far = [shifted(pair[k].astype(BF16), "tm", 4 * k) for k in (2, 1, 3)]
    col = [total(near[k], across[k]) for k in range(4)]
    col_in = [shifted(col[k].astype(BF16), "mp", 2 * k) for k in (2, 1, 3)]
    xh = lax.axis_index("mp") % 2
    both = total(ring[0], *ring_in).astype(BF16)
    mine = lax.dynamic_index_in_dim(both, xh, 0, False)
    theirs = swapped(lax.dynamic_index_in_dim(both, 1 - xh, 0, False), "mp", 1)
    first_half = total(mine, theirs).astype(BF16)
    second_half = total(col[0], *col_in).astype(BF16)
    frame_grad = jnp.concatenate([first_half, second_half], axis=0)
    summed = total(pair[0], *far)
    return frame_grad, summed[:3], summed[3].T


def solution(mesh):
    placed = (
        P(("batch", "tm"), None),
        P(),
        P(None, None, "mp"),
        P("mp", None),
        P(("batch", "tm"), None),
        P("batch"),
        P("batch"),
    )
    return jax.shard_map(
        on_device,
        mesh=mesh,
        in_specs=placed,
        out_specs=(P(("batch", "tm"), "mp"), P("batch", "tm", "mp"), P(("batch", "mp"), "tm")),
        check_vma=False,
    )
```

```python
import jax
import jax.numpy as jnp
from jax import lax
from jax.experimental import pallas as pl
from jax.experimental.pallas import tpu as pltpu
from jax.sharding import PartitionSpec as P

HS = 128
CH = 32
HALO = 64
EPSILON = 1e-05
SCALE = HS ** (-0.5)
F32 = jnp.float32
BF16 = jnp.bfloat16


def rows_by_rows(left, right):
    return lax.dot_general(left, right, (((1,), (1,)), ((), ())), preferred_element_type=F32)


def cols_by_cols(left, right):
    return lax.dot_general(left, right, (((0,), (0,)), ((), ())), preferred_element_type=F32)


def plain(left, right):
    return jnp.dot(left, right, preferred_element_type=F32)


def normalised(values):
    values = values.astype(F32)
    center = values - jnp.mean(values, axis=-1, keepdims=True)
    inverse = lax.rsqrt(jnp.mean(center * center, axis=-1, keepdims=True) + EPSILON)
    return center * inverse, inverse


def pad_rows(pad_ref, first, count):
    total = pad_ref.shape[0]
    return [pad_ref[pl.ds(jnp.clip(first + i, 0, total - 1), 1), :] for i in range(count)]


def as_columns(rows):
    height = -(-len(rows) // 8) * 8
    full = jnp.concatenate(rows + [jnp.zeros_like(rows[0])] * (height - len(rows)), axis=0)
    return full.T


def project_body(frames_ref, gain_ref, qkv_ref, out_ref, cot_ref, pad_ref, proj_ref, normed_ref, w_scr):
    step = pl.program_id(0)
    rows = frames_ref.shape[0]

    @pl.when(step == 0)
    def _():
        for m in range(3):
            w_scr[:, m * HS : (m + 1) * HS] = qkv_ref[m]

    normal_form, _ = normalised(frames_ref[...])
    normed = (normal_form * gain_ref[...]).astype(BF16)
    normed_ref[...] = normed
    qkv = plain(normed, w_scr[...]).astype(BF16)
    for m in range(3):
        proj_ref[m] = qkv[:, m * HS : (m + 1) * HS]
    per_step = rows // 128
    first = (lax.axis_index("tm") * pl.num_programs(0) + step) * per_step
    live = as_columns([r.astype(F32) for r in pad_rows(pad_ref, first, per_step)])
    live = jnp.concatenate([live[:, i : i + 1] for i in range(per_step)], axis=0)
    grads = rows_by_rows(cot_ref[...], out_ref[...])
    proj_ref[3] = jnp.where(live == 1.0, grads, 0.0).astype(BF16)


def project(frames, gain, qkv_weight, out_weight, cotangent, pad2d):
    count, width = frames.shape
    rows = 256
    whole = lambda *shape: pl.BlockSpec(shape, lambda i: (0,) * len(shape))
    return pl.pallas_call(
        project_body,
        grid=(count // rows,),
        in_specs=[
            pl.BlockSpec((rows, width), lambda i: (i, 0)),
            whole(1, width),
            whole(*qkv_weight.shape),
            whole(*out_weight.shape),
            pl.BlockSpec((rows, width), lambda i: (i, 0)),
            whole(*pad2d.shape),
        ],
        out_specs=[
            pl.BlockSpec((4, rows, HS), lambda i: (0, i, 0)),
            pl.BlockSpec((rows, width), lambda i: (i, 0)),
        ],
        out_shape=[
            jax.ShapeDtypeStruct((4, count, HS), BF16),
            jax.ShapeDtypeStruct((count, width), BF16),
        ],
        scratch_shapes=[pltpu.VMEM((width, 3 * HS), BF16)],
        compiler_params=pltpu.CompilerParams(vmem_limit_bytes=48 << 20),
        name="project",
    )(frames, gain, qkv_weight, out_weight, cotangent, pad2d)


def attend_body(len_ref, proj_ref, halo_ref, gain_ref, qkv_ref, out_ref, pad_ref, grads_ref, mixed_ref, x_scr):
    count = proj_ref.shape[1]
    tiles = count // 128 + 1
    shard = lax.axis_index("tm")
    first_block = shard * (count // 128) - 1
    normal_form, _ = normalised(halo_ref[0])
    normed = (normal_form * gain_ref[...]).astype(BF16)
    blocks = tiles + 1
    live_rows = [r.astype(F32) for r in pad_rows(pad_ref, first_block, blocks)]
    live_cols = as_columns(live_rows)
    halo_live = jnp.concatenate([live_cols[HALO:, 0:1], live_cols[:HALO, blocks - 1 : blocks]], axis=0)
    zeros = jnp.zeros((HALO, HS), BF16)
    for m in range(4):
        if m < 3:
            part = plain(normed, qkv_ref[m])
        else:
            part = jnp.where(halo_live == 1.0, rows_by_rows(halo_ref[1], out_ref[...]), 0.0)
        part = part.astype(BF16)
        x_scr[m, 0:HALO, :] = zeros
        x_scr[m, HALO : 2 * HALO, :] = part[:HALO]
        x_scr[m, 2 * HALO : 2 * HALO + count, :] = proj_ref[m]
        x_scr[m, 2 * HALO + count : 3 * HALO + count, :] = part[HALO:]
        x_scr[m, 3 * HALO + count :, :] = zeros

    ends = []
    total = 0
    for u in range(len_ref.shape[0]):
        total = total + len_ref[u]
        ends.append(total)

    def segment(positions):
        found = jnp.zeros(positions.shape, jnp.int32)
        for end in ends:
            found = found + jnp.where(positions >= end, 1, 0)
        return found.astype(F32)

    lane = lax.broadcasted_iota(jnp.int32, (1, 128), 1)
    codes = []
    for b in range(blocks):
        at = (first_block + b) * 128 + lane
        codes.append(jnp.where((live_rows[b] == 1.0) & (at >= 0), segment(at), -1.0))
    code_cols = as_columns(codes)

    keys = 192
    key_at = lax.broadcasted_iota(jnp.int32, (keys, 128), 0)
    query_at = lax.broadcasted_iota(jnp.int32, (keys, 128), 1)
    apart = key_at // CH - query_at // CH
    in_band = (apart >= 0) & (apart <= 2)
    same = key_at == query_at + CH

    carry_k = carry_v = None
    for t in range(tiles):
        base = 128 * t
        q = x_scr[0, base + HALO : base + HALO + 128, :]
        g = x_scr[3, base + HALO : base + HALO + 128, :]
        k = x_scr[1, base + CH : base + CH + keys, :]
        v = x_scr[2, base + CH : base + CH + keys, :]
        query_seg = segment((first_block + t) * 128 + HALO + lane)
        code = jnp.concatenate([code_cols[CH:, t : t + 1], code_cols[: keys - 96, t + 1 : t + 2]], axis=0)
        allowed = in_band & ((code == query_seg) | same)
        scores = jnp.where(allowed, rows_by_rows(k, q) * SCALE, -1e30)
        weights = jnp.exp(scores - jnp.max(scores, axis=0, keepdims=True))
        probs = weights * (1.0 / jnp.sum(weights, axis=0, keepdims=True))
        rounded = probs.astype(BF16)
        prob_grad = rows_by_rows(v, g)
        centre = jnp.sum(probs * prob_grad, axis=0, keepdims=True)
        score_grad = (probs * (prob_grad - centre) * SCALE).astype(BF16)
        mixed = cols_by_cols(rounded, v).astype(BF16)
        query_grad = cols_by_cols(score_grad, k).astype(BF16)
        key_grad = plain(score_grad, q)
        value_grad = plain(rounded, g)
        live = jnp.concatenate([live_cols[HALO:, t : t + 1], live_cols[:HALO, t + 1 : t + 2]], axis=0)
        mixed = jnp.where(live == 1.0, mixed, jnp.zeros_like(mixed))
        lo, hi = (HALO if t == 0 else 0), (HALO if t == tiles - 1 else 128)
        at = base - HALO
        mixed_ref[at + lo : at + hi, :] = mixed[lo:hi]
        grads_ref[at + lo : at + hi, 0:HS] = query_grad[lo:hi]
        if t > 0:
            key_grad = jnp.concatenate([key_grad[:64] + carry_k, key_grad[64:]], axis=0)
            value_grad = jnp.concatenate([value_grad[:64] + carry_v, value_grad[64:]], axis=0)
        carry_k, carry_v = key_grad[128:], value_grad[128:]
        lo, hi = (96 if t == 0 else 0), (96 if t == tiles - 1 else 128)
        at = base - 96
        grads_ref[at + lo : at + hi, HS : 2 * HS] = key_grad[lo:hi].astype(BF16)
        grads_ref[at + lo : at + hi, 2 * HS : 3 * HS] = value_grad[lo:hi].astype(BF16)


def attend(lengths, proj, halo, gain, qkv_weight, out_weight, pad2d):
    count = proj.shape[1]
    vmem = pl.BlockSpec(memory_space=pltpu.VMEM)
    return pl.pallas_call(
        attend_body,
        in_specs=[pl.BlockSpec(memory_space=pltpu.SMEM)] + [vmem] * 6,
        out_specs=[vmem, vmem],
        out_shape=[
            jax.ShapeDtypeStruct((count, 3 * HS), BF16),
            jax.ShapeDtypeStruct((count, HS), BF16),
        ],
        scratch_shapes=[pltpu.VMEM((4, count + 4 * HALO, HS), BF16)],
        compiler_params=pltpu.CompilerParams(vmem_limit_bytes=48 << 20),
        name="attend",
    )(lengths, proj, halo, gain, qkv_weight, out_weight, pad2d)


def input_body(frames_ref, gain_ref, qkv_ref, grads_ref, *rest):
    outs, w_scr = rest[:-1], rest[-1]
    y = lax.axis_index("mp") // 2

    @pl.when(pl.program_id(0) == 0)
    def _():
        for m in range(3):
            w_scr[:, m * HS : (m + 1) * HS] = qkv_ref[m]

    incoming = rows_by_rows(grads_ref[...], w_scr[...])
    normal_form, inverse = normalised(frames_ref[...])
    scaled = incoming * gain_ref[...]
    mean_grad = jnp.mean(scaled, axis=-1, keepdims=True)
    mean_proj = jnp.mean(scaled * normal_form, axis=-1, keepdims=True)
    result = (inverse * (scaled - mean_grad - normal_form * mean_proj)).astype(BF16)
    for p in range(4):
        for k in range(4):

            @pl.when((p - y + 4) % 4 == k)
            def _():
                for h in range(2):
                    at = (2 * p + h) * 128
                    outs[k][h] = result[:, at : at + 128]


def input_terms(frames, gain, qkv_weight, grads):
    count, width = frames.shape
    rows = 256
    whole = lambda *shape: pl.BlockSpec(shape, lambda i: (0,) * len(shape))
    return pl.pallas_call(
        input_body,
        grid=(count // rows,),
        in_specs=[
            pl.BlockSpec((rows, width), lambda i: (i, 0)),
            whole(1, width),
            whole(*qkv_weight.shape),
            pl.BlockSpec((rows, 3 * HS), lambda i: (i, 0)),
        ],
        out_specs=[pl.BlockSpec((2, rows, 128), lambda i: (0, i, 0))] * 4,
        out_shape=[jax.ShapeDtypeStruct((2, count, 128), BF16)] * 4,
        scratch_shapes=[pltpu.VMEM((width, 3 * HS), BF16)],
        compiler_params=pltpu.CompilerParams(vmem_limit_bytes=48 << 20),
        name="input_terms",
    )(frames, gain, qkv_weight, grads)


def weight_body(normed_ref, cot_ref, grads_ref, mixed_ref, keep_ref, send_ref):
    core = lax.axis_index("tm") % 2
    qkv = cols_by_cols(grads_ref[...], normed_ref[...]).astype(BF16)
    out = cols_by_cols(mixed_ref[...], cot_ref[...]).astype(BF16)
    full = jnp.concatenate([qkv, out], axis=0)
    for z in range(8):
        both = full[:, z * 128 : (z + 1) * 128].T
        low, high = both[:64], both[64:]
        keep = jnp.where(core == 0, low, high)
        send = jnp.where(core == 0, high, low)
        for m in range(4):
            keep_ref[z, m] = keep[:, m * HS : (m + 1) * HS]
            send_ref[z, m] = send[:, m * HS : (m + 1) * HS]


def weight_terms(normed, cotangent, grads, mixed):
    count, width = normed.shape
    vmem = pl.BlockSpec(memory_space=pltpu.VMEM)
    part = jax.ShapeDtypeStruct((8, 4, width // 16, HS), BF16)
    return pl.pallas_call(
        weight_body,
        in_specs=[vmem] * 4,
        out_specs=[vmem] * 2,
        out_shape=[part] * 2,
        compiler_params=pltpu.CompilerParams(vmem_limit_bytes=48 << 20),
        name="weight_terms",
    )(normed, cotangent, grads, mixed)


def finish_body(parts_ref, qkv_ref, out_ref):
    for m in range(4):
        summed = parts_ref[0, m].astype(F32)
        for z in range(1, 8):
            summed = summed + parts_ref[z, m].astype(F32)
        if m < 3:
            qkv_ref[m] = summed
        else:
            out_ref[...] = summed.T


def finish(parts):
    vmem = pl.BlockSpec(memory_space=pltpu.VMEM)
    part = parts.shape[2]
    return pl.pallas_call(
        finish_body,
        in_specs=[vmem],
        out_specs=[vmem] * 2,
        out_shape=[jax.ShapeDtypeStruct((3, part, HS), F32), jax.ShapeDtypeStruct((HS, part), F32)],
        name="finish",
    )(parts)


def shifted(x, axis, by):
    size = lax.axis_size(axis)
    return lax.ppermute(x, axis, [(i, (i + by) % size) for i in range(size)])


def swapped(x, axis, bit):
    return lax.ppermute(x, axis, [(i, i ^ bit) for i in range(lax.axis_size(axis))])


def total(*parts):
    summed = parts[0].astype(F32)
    for part in parts[1:]:
        summed = summed + part.astype(F32)
    return summed


def on_device(frames, norm_gain, qkv_weight, out_weight, cotangent, pad_mask, utt_lengths):
    shards = lax.axis_size("tm")
    up = [(i, i + 1) for i in range(shards - 1)]
    down = [(i + 1, i) for i in range(shards - 1)]
    ends = jnp.stack([frames[-HALO:], cotangent[-HALO:]])
    starts = jnp.stack([frames[:HALO], cotangent[:HALO]])
    halo = jnp.concatenate([lax.ppermute(ends, "tm", up), lax.ppermute(starts, "tm", down)], axis=1)
    gain = norm_gain[None, :]
    pad2d = pad_mask.reshape(-1, 128)
    proj, normed = project(frames, gain, qkv_weight, out_weight, cotangent, pad2d)
    grads, mixed = attend(utt_lengths, proj, halo, gain, qkv_weight, out_weight, pad2d)
    keep, send = weight_terms(normed, cotangent, grads, mixed)
    other = swapped(send, "tm", 1)
    (frames_b, grads_b), _ = lax.optimization_barrier(((frames, grads), keep))
    ring = input_terms(frames_b, gain, qkv_weight, grads_b)
    ring_in = [shifted(ring[k], "mp", 2 * k) for k in (2, 1, 3)]
    (keep, other), _ = lax.optimization_barrier(((keep, other), ring[0]))
    chip = total(keep, other).astype(BF16)
    same_core = [[c + 2 * z for z in range(shards // 2)] for c in range(2)]
    weights = lax.all_to_all(chip, "tm", 0, 0, tiled=True, axis_index_groups=same_core)
    xh = lax.axis_index("mp") % 2
    both = total(ring[0], *ring_in).astype(BF16)
    mine = lax.dynamic_index_in_dim(both, xh, 0, False)
    theirs = swapped(lax.dynamic_index_in_dim(both, 1 - xh, 0, False), "mp", 1)
    frame_grad = total(mine, theirs).astype(BF16)
    qkv_grad, out_grad = finish(weights)
    return frame_grad, qkv_grad, out_grad


def solution(mesh):
    placed = (
        P(("batch", "tm"), None),
        P(),
        P(None, None, "mp"),
        P("mp", None),
        P(("batch", "tm"), None),
        P("batch"),
        P("batch"),
    )
    return jax.shard_map(
        on_device,
        mesh=mesh,
        in_specs=placed,
        out_specs=(P(("batch", "tm"), "mp"), P("batch", "tm", "mp"), P(("batch", "mp"), "tm")),
        check_vma=False,
    )
```

```python
import jax
import jax.numpy as jnp
from jax import lax
from jax.experimental import pallas as pl
from jax.experimental.pallas import tpu as pltpu
from jax.sharding import PartitionSpec as P

HS = 128
CH = 32
HALO = 64
EPSILON = 1e-05
SCALE = HS ** (-0.5)
F32 = jnp.float32
BF16 = jnp.bfloat16


def rows_by_rows(left, right):
    return lax.dot_general(left, right, (((1,), (1,)), ((), ())), preferred_element_type=F32)


def cols_by_cols(left, right):
    return lax.dot_general(left, right, (((0,), (0,)), ((), ())), preferred_element_type=F32)


def plain(left, right):
    return jnp.dot(left, right, preferred_element_type=F32)


def normalised(values):
    values = values.astype(F32)
    center = values - jnp.mean(values, axis=-1, keepdims=True)
    inverse = lax.rsqrt(jnp.mean(center * center, axis=-1, keepdims=True) + EPSILON)
    return center * inverse, inverse


def pad_rows(pad_ref, first, count):
    total = pad_ref.shape[0]
    return [pad_ref[pl.ds(jnp.clip(first + i, 0, total - 1), 1), :] for i in range(count)]


def as_columns(rows):
    height = -(-len(rows) // 8) * 8
    full = jnp.concatenate(rows + [jnp.zeros_like(rows[0])] * (height - len(rows)), axis=0)
    return full.T


def project_body(frames_ref, gain_ref, qkv_ref, out_ref, cot_ref, pad_ref, proj_ref, normed_ref, w_scr):
    step = pl.program_id(0)
    rows = frames_ref.shape[0]

    @pl.when(step == 0)
    def _():
        for m in range(3):
            w_scr[:, m * HS : (m + 1) * HS] = qkv_ref[m]

    normal_form, _ = normalised(frames_ref[...])
    normed = (normal_form * gain_ref[...]).astype(BF16)
    normed_ref[...] = normed
    qkv = plain(normed, w_scr[...]).astype(BF16)
    for m in range(3):
        proj_ref[m] = qkv[:, m * HS : (m + 1) * HS]
    per_step = rows // 128
    first = (lax.axis_index("tm") * pl.num_programs(0) + step) * per_step
    live = as_columns([r.astype(F32) for r in pad_rows(pad_ref, first, per_step)])
    live = jnp.concatenate([live[:, i : i + 1] for i in range(per_step)], axis=0)
    grads = rows_by_rows(cot_ref[...], out_ref[...])
    proj_ref[3] = jnp.where(live == 1.0, grads, 0.0).astype(BF16)


def project(frames, gain, qkv_weight, out_weight, cotangent, pad2d):
    count, width = frames.shape
    rows = 256
    whole = lambda *shape: pl.BlockSpec(shape, lambda i: (0,) * len(shape))
    return pl.pallas_call(
        project_body,
        grid=(count // rows,),
        in_specs=[
            pl.BlockSpec((rows, width), lambda i: (i, 0)),
            whole(1, width),
            whole(*qkv_weight.shape),
            whole(*out_weight.shape),
            pl.BlockSpec((rows, width), lambda i: (i, 0)),
            whole(*pad2d.shape),
        ],
        out_specs=[
            pl.BlockSpec((4, rows, HS), lambda i: (0, i, 0)),
            pl.BlockSpec((rows, width), lambda i: (i, 0)),
        ],
        out_shape=[
            jax.ShapeDtypeStruct((4, count, HS), BF16),
            jax.ShapeDtypeStruct((count, width), BF16),
        ],
        scratch_shapes=[pltpu.VMEM((width, 3 * HS), BF16)],
        compiler_params=pltpu.CompilerParams(vmem_limit_bytes=48 << 20),
        name="project",
    )(frames, gain, qkv_weight, out_weight, cotangent, pad2d)


def attend_body(len_ref, proj_ref, halo_ref, gain_ref, qkv_ref, out_ref, pad_ref, grads_ref, mixed_ref, x_scr):
    count = proj_ref.shape[1]
    tiles = count // 128 + 1
    shard = lax.axis_index("tm")
    first_block = shard * (count // 128) - 1
    normal_form, _ = normalised(halo_ref[0])
    normed = (normal_form * gain_ref[...]).astype(BF16)
    blocks = tiles + 1
    live_rows = [r.astype(F32) for r in pad_rows(pad_ref, first_block, blocks)]
    live_cols = as_columns(live_rows)
    halo_live = jnp.concatenate([live_cols[HALO:, 0:1], live_cols[:HALO, blocks - 1 : blocks]], axis=0)
    zeros = jnp.zeros((HALO, HS), BF16)
    for m in range(4):
        if m < 3:
            part = plain(normed, qkv_ref[m])
        else:
            part = jnp.where(halo_live == 1.0, rows_by_rows(halo_ref[1], out_ref[...]), 0.0)
        part = part.astype(BF16)
        x_scr[m, 0:HALO, :] = zeros
        x_scr[m, HALO : 2 * HALO, :] = part[:HALO]
        x_scr[m, 2 * HALO : 2 * HALO + count, :] = proj_ref[m]
        x_scr[m, 2 * HALO + count : 3 * HALO + count, :] = part[HALO:]
        x_scr[m, 3 * HALO + count :, :] = zeros

    ends = []
    total = 0
    for u in range(len_ref.shape[0]):
        total = total + len_ref[u]
        ends.append(total)

    def segment(positions):
        found = jnp.zeros(positions.shape, jnp.int32)
        for end in ends:
            found = found + jnp.where(positions >= end, 1, 0)
        return found.astype(F32)

    lane = lax.broadcasted_iota(jnp.int32, (1, 128), 1)
    codes = []
    for b in range(blocks):
        at = (first_block + b) * 128 + lane
        codes.append(jnp.where((live_rows[b] == 1.0) & (at >= 0), segment(at), -1.0))
    code_cols = as_columns(codes)

    keys = 192
    key_at = lax.broadcasted_iota(jnp.int32, (keys, 128), 0)
    query_at = lax.broadcasted_iota(jnp.int32, (keys, 128), 1)
    apart = key_at // CH - query_at // CH
    in_band = (apart >= 0) & (apart <= 2)
    same = key_at == query_at + CH

    carry_k = carry_v = None
    for t in range(tiles):
        base = 128 * t
        q = x_scr[0, base + HALO : base + HALO + 128, :]
        g = x_scr[3, base + HALO : base + HALO + 128, :]
        k = x_scr[1, base + CH : base + CH + keys, :]
        v = x_scr[2, base + CH : base + CH + keys, :]
        query_seg = segment((first_block + t) * 128 + HALO + lane)
        code = jnp.concatenate([code_cols[CH:, t : t + 1], code_cols[: keys - 96, t + 1 : t + 2]], axis=0)
        allowed = in_band & ((code == query_seg) | same)
        scores = jnp.where(allowed, rows_by_rows(k, q) * SCALE, -1e30)
        weights = jnp.exp(scores - jnp.max(scores, axis=0, keepdims=True))
        probs = weights * (1.0 / jnp.sum(weights, axis=0, keepdims=True))
        rounded = probs.astype(BF16)
        prob_grad = rows_by_rows(v, g)
        centre = jnp.sum(probs * prob_grad, axis=0, keepdims=True)
        score_grad = (probs * (prob_grad - centre) * SCALE).astype(BF16)
        mixed = cols_by_cols(rounded, v).astype(BF16)
        query_grad = cols_by_cols(score_grad, k).astype(BF16)
        key_grad = plain(score_grad, q)
        value_grad = plain(rounded, g)
        live = jnp.concatenate([live_cols[HALO:, t : t + 1], live_cols[:HALO, t + 1 : t + 2]], axis=0)
        mixed = jnp.where(live == 1.0, mixed, jnp.zeros_like(mixed))
        lo, hi = (HALO if t == 0 else 0), (HALO if t == tiles - 1 else 128)
        at = base - HALO
        mixed_ref[at + lo : at + hi, :] = mixed[lo:hi]
        grads_ref[at + lo : at + hi, 0:HS] = query_grad[lo:hi]
        if t > 0:
            key_grad = jnp.concatenate([key_grad[:64] + carry_k, key_grad[64:]], axis=0)
            value_grad = jnp.concatenate([value_grad[:64] + carry_v, value_grad[64:]], axis=0)
        carry_k, carry_v = key_grad[128:], value_grad[128:]
        lo, hi = (96 if t == 0 else 0), (96 if t == tiles - 1 else 128)
        at = base - 96
        grads_ref[at + lo : at + hi, HS : 2 * HS] = key_grad[lo:hi].astype(BF16)
        grads_ref[at + lo : at + hi, 2 * HS : 3 * HS] = value_grad[lo:hi].astype(BF16)


def attend(lengths, proj, halo, gain, qkv_weight, out_weight, pad2d):
    count = proj.shape[1]
    vmem = pl.BlockSpec(memory_space=pltpu.VMEM)
    return pl.pallas_call(
        attend_body,
        in_specs=[pl.BlockSpec(memory_space=pltpu.SMEM)] + [vmem] * 6,
        out_specs=[vmem, vmem],
        out_shape=[
            jax.ShapeDtypeStruct((count, 3 * HS), BF16),
            jax.ShapeDtypeStruct((count, HS), BF16),
        ],
        scratch_shapes=[pltpu.VMEM((4, count + 4 * HALO, HS), BF16)],
        compiler_params=pltpu.CompilerParams(vmem_limit_bytes=48 << 20),
        name="attend",
    )(lengths, proj, halo, gain, qkv_weight, out_weight, pad2d)


def input_body(frames_ref, gain_ref, qkv_ref, grads_ref, *rest):
    outs, w_scr = rest[:-1], rest[-1]
    place = lax.axis_index("mp")
    y, xh = place // 2, place % 2

    @pl.when(pl.program_id(0) == 0)
    def _():
        for m in range(3):
            w_scr[:, m * HS : (m + 1) * HS] = qkv_ref[m]

    incoming = rows_by_rows(grads_ref[...], w_scr[...])
    normal_form, inverse = normalised(frames_ref[...])
    scaled = incoming * gain_ref[...]
    mean_grad = jnp.mean(scaled, axis=-1, keepdims=True)
    mean_proj = jnp.mean(scaled * normal_form, axis=-1, keepdims=True)
    result = (inverse * (scaled - mean_grad - normal_form * mean_proj)).astype(BF16)
    if len(outs) == 4:
        for p in range(4):
            for k in range(4):

                @pl.when((p - y) % 4 == k)
                def _():
                    for h in range(2):
                        at = (2 * p + h) * 128
                        outs[k][h] = result[:, at : at + 128]
    else:
        for p in range(4):
            low = result[:, 256 * p : 256 * p + 128]
            high = result[:, 256 * p + 128 : 256 * p + 256]
            away = (p - y + 4) % 4
            outs[0][away] = jnp.where(xh == 0, low, high)
            outs[1][away] = jnp.where(xh == 0, high, low)


def input_terms(frames, gain, qkv_weight, grads, half, pair_first):
    count, width = frames.shape
    rows = 256
    steps = count // rows // 2
    first = half * steps
    whole = lambda *shape: pl.BlockSpec(shape, lambda i: (0,) * len(shape))
    lead, n_outs = (4, 2) if pair_first else (2, 4)
    return pl.pallas_call(
        input_body,
        grid=(steps,),
        in_specs=[
            pl.BlockSpec((rows, width), lambda i: (i + first, 0)),
            whole(1, width),
            whole(*qkv_weight.shape),
            pl.BlockSpec((rows, 3 * HS), lambda i: (i + first, 0)),
        ],
        out_specs=[pl.BlockSpec((lead, rows, 128), lambda i: (0, i, 0))] * n_outs,
        out_shape=[jax.ShapeDtypeStruct((lead, count // 2, 128), BF16)] * n_outs,
        scratch_shapes=[pltpu.VMEM((width, 3 * HS), BF16)],
        compiler_params=pltpu.CompilerParams(vmem_limit_bytes=48 << 20),
        name="input_terms_pair" if pair_first else "input_terms_ring",
    )(frames, gain, qkv_weight, grads)


def weight_body(normed_ref, cot_ref, grads_ref, mixed_ref, keep_ref, send_ref):
    core = lax.axis_index("tm") % 2
    qkv = cols_by_cols(grads_ref[...], normed_ref[...]).astype(BF16)
    out = cols_by_cols(mixed_ref[...], cot_ref[...]).astype(BF16)
    full = jnp.concatenate([qkv, out], axis=0)
    for z in range(8):
        both = full[:, z * 128 : (z + 1) * 128].T
        low, high = both[:64], both[64:]
        keep = jnp.where(core == 0, low, high)
        send = jnp.where(core == 0, high, low)
        for m in range(4):
            keep_ref[z, m] = keep[:, m * HS : (m + 1) * HS]
            send_ref[z, m] = send[:, m * HS : (m + 1) * HS]


def weight_terms(normed, cotangent, grads, mixed):
    count, width = normed.shape
    vmem = pl.BlockSpec(memory_space=pltpu.VMEM)
    part = jax.ShapeDtypeStruct((8, 4, width // 16, HS), BF16)
    return pl.pallas_call(
        weight_body,
        in_specs=[vmem] * 4,
        out_specs=[vmem] * 2,
        out_shape=[part] * 2,
        compiler_params=pltpu.CompilerParams(vmem_limit_bytes=48 << 20),
        name="weight_terms",
    )(normed, cotangent, grads, mixed)


def shifted(x, axis, by):
    size = lax.axis_size(axis)
    return lax.ppermute(x, axis, [(i, (i + by) % size) for i in range(size)])


def swapped(x, axis, bit):
    return lax.ppermute(x, axis, [(i, i ^ bit) for i in range(lax.axis_size(axis))])


def total(*parts):
    summed = parts[0].astype(F32)
    for part in parts[1:]:
        summed = summed + part.astype(F32)
    return summed


def on_device(frames, norm_gain, qkv_weight, out_weight, cotangent, pad_mask, utt_lengths):
    shards = lax.axis_size("tm")
    up = [(i, i + 1) for i in range(shards - 1)]
    down = [(i + 1, i) for i in range(shards - 1)]
    ends = jnp.stack([frames[-HALO:], cotangent[-HALO:]])
    starts = jnp.stack([frames[:HALO], cotangent[:HALO]])
    halo = jnp.concatenate([lax.ppermute(ends, "tm", up), lax.ppermute(starts, "tm", down)], axis=1)
    gain = norm_gain[None, :]
    pad2d = pad_mask.reshape(-1, 128)
    proj, normed = project(frames, gain, qkv_weight, out_weight, cotangent, pad2d)
    grads, mixed = attend(utt_lengths, proj, halo, gain, qkv_weight, out_weight, pad2d)
    keep, send = weight_terms(normed, cotangent, grads, mixed)
    other = swapped(send, "tm", 1)
    (frames_p, grads_p), _ = lax.optimization_barrier(((frames, grads), keep))
    near, across = input_terms(frames_p, gain, qkv_weight, grads_p, 1, True)
    across = swapped(across, "mp", 1)
    (frames_r, grads_r), _ = lax.optimization_barrier(((frames, grads), near))
    ring = input_terms(frames_r, gain, qkv_weight, grads_r, 0, False)
    ring_in = [shifted(ring[k], "mp", 2 * k) for k in (2, 1, 3)]
    (keep, other), _ = lax.optimization_barrier(((keep, other), ring[0]))
    chip = total(keep, other).astype(BF16)
    same_core = [[c + 2 * z for z in range(shards // 2)] for c in range(2)]
    weights = lax.all_to_all(chip, "tm", 0, 0, tiled=True, axis_index_groups=same_core)
    col = [total(near[k], across[k]) for k in range(4)]
    col_in = [shifted(col[k].astype(BF16), "mp", 2 * k) for k in (2, 1, 3)]
    ring_in, _ = lax.optimization_barrier((ring_in, [c.astype(BF16) for c in col[1:]]))
    xh = lax.axis_index("mp") % 2

    def both(side):
        return total(*[lax.dynamic_index_in_dim(r, side, 0, False) for r in (ring[0], *ring_in)])

    theirs = swapped(both(1 - xh).astype(BF16), "mp", 1)
    first_half = total(both(xh), theirs).astype(BF16)
    second_half = total(col[0], *col_in).astype(BF16)
    frame_grad = jnp.concatenate([first_half, second_half], axis=0)
    qkv_grad = weights[:, :3].astype(F32).sum(axis=0)
    out_grad = weights[:, 3].astype(F32).sum(axis=0)
    return frame_grad, qkv_grad, out_grad.T


def solution(mesh):
    placed = (
        P(("batch", "tm"), None),
        P(),
        P(None, None, "mp"),
        P("mp", None),
        P(("batch", "tm"), None),
        P("batch"),
        P("batch"),
    )
    return jax.shard_map(
        on_device,
        mesh=mesh,
        in_specs=placed,
        out_specs=(P(("batch", "tm"), "mp"), P("batch", "tm", "mp"), P(("batch", "mp"), "tm")),
        check_vma=False,
    )
```

```python
import jax
import jax.numpy as jnp
from jax import lax
from jax.experimental import pallas as pl
from jax.experimental.pallas import tpu as pltpu
from jax.sharding import PartitionSpec as P

HS = 128
CH = 32
HALO = 64
EPSILON = 1e-05
SCALE = HS ** (-0.5)
F32 = jnp.float32
BF16 = jnp.bfloat16


def rows_by_rows(left, right):
    return lax.dot_general(left, right, (((1,), (1,)), ((), ())), preferred_element_type=F32)


def cols_by_cols(left, right):
    return lax.dot_general(left, right, (((0,), (0,)), ((), ())), preferred_element_type=F32)


def plain(left, right):
    return jnp.dot(left, right, preferred_element_type=F32)


def normalised(values):
    values = values.astype(F32)
    center = values - jnp.mean(values, axis=-1, keepdims=True)
    inverse = lax.rsqrt(jnp.mean(center * center, axis=-1, keepdims=True) + EPSILON)
    return center * inverse, inverse


def pad_rows(pad_ref, first, count):
    total = pad_ref.shape[0]
    return [pad_ref[pl.ds(jnp.clip(first + i, 0, total - 1), 1), :] for i in range(count)]


def as_columns(rows):
    height = -(-len(rows) // 8) * 8
    full = jnp.concatenate(rows + [jnp.zeros_like(rows[0])] * (height - len(rows)), axis=0)
    return full.T


def project_body(frames_ref, gain_ref, qkv_ref, out_ref, cot_ref, pad_ref, proj_ref, normed_ref, w_scr):
    step = pl.program_id(0)
    rows = frames_ref.shape[0]

    @pl.when(step == 0)
    def _():
        for m in range(3):
            w_scr[:, m * HS : (m + 1) * HS] = qkv_ref[m]

    normal_form, _ = normalised(frames_ref[...])
    normed = (normal_form * gain_ref[...]).astype(BF16)
    normed_ref[...] = normed
    qkv = plain(normed, w_scr[...]).astype(BF16)
    for m in range(3):
        proj_ref[m] = qkv[:, m * HS : (m + 1) * HS]
    per_step = rows // 128
    first = (lax.axis_index("tm") * pl.num_programs(0) + step) * per_step
    live = as_columns([r.astype(F32) for r in pad_rows(pad_ref, first, per_step)])
    live = jnp.concatenate([live[:, i : i + 1] for i in range(per_step)], axis=0)
    grads = rows_by_rows(cot_ref[...], out_ref[...])
    proj_ref[3] = jnp.where(live == 1.0, grads, 0.0).astype(BF16)


def project(frames, gain, qkv_weight, out_weight, cotangent, pad2d):
    count, width = frames.shape
    rows = 256
    whole = lambda *shape: pl.BlockSpec(shape, lambda i: (0,) * len(shape))
    return pl.pallas_call(
        project_body,
        grid=(count // rows,),
        in_specs=[
            pl.BlockSpec((rows, width), lambda i: (i, 0)),
            whole(1, width),
            whole(*qkv_weight.shape),
            whole(*out_weight.shape),
            pl.BlockSpec((rows, width), lambda i: (i, 0)),
            whole(*pad2d.shape),
        ],
        out_specs=[
            pl.BlockSpec((4, rows, HS), lambda i: (0, i, 0)),
            pl.BlockSpec((rows, width), lambda i: (i, 0)),
        ],
        out_shape=[
            jax.ShapeDtypeStruct((4, count, HS), BF16),
            jax.ShapeDtypeStruct((count, width), BF16),
        ],
        scratch_shapes=[pltpu.VMEM((width, 3 * HS), BF16)],
        compiler_params=pltpu.CompilerParams(vmem_limit_bytes=20 << 20),
        name="project",
    )(frames, gain, qkv_weight, out_weight, cotangent, pad2d)


def attend_body(len_ref, proj_ref, halo_ref, gain_ref, qkv_ref, out_ref, pad_ref, grads_ref, mixed_ref, x_scr):
    count = proj_ref.shape[1]
    tiles = count // 128 + 1
    shard = lax.axis_index("tm")
    first_block = shard * (count // 128) - 1
    normal_form, _ = normalised(halo_ref[0])
    normed = (normal_form * gain_ref[...]).astype(BF16)
    blocks = tiles + 1
    live_rows = [r.astype(F32) for r in pad_rows(pad_ref, first_block, blocks)]
    live_cols = as_columns(live_rows)
    halo_live = jnp.concatenate([live_cols[HALO:, 0:1], live_cols[:HALO, blocks - 1 : blocks]], axis=0)
    zeros = jnp.zeros((HALO, HS), BF16)
    for m in range(4):
        if m < 3:
            part = plain(normed, qkv_ref[m])
        else:
            part = jnp.where(halo_live == 1.0, rows_by_rows(halo_ref[1], out_ref[...]), 0.0)
        part = part.astype(BF16)
        x_scr[m, 0:HALO, :] = zeros
        x_scr[m, HALO : 2 * HALO, :] = part[:HALO]
        x_scr[m, 2 * HALO : 2 * HALO + count, :] = proj_ref[m]
        x_scr[m, 2 * HALO + count : 3 * HALO + count, :] = part[HALO:]
        x_scr[m, 3 * HALO + count :, :] = zeros

    ends = []
    total = 0
    for u in range(len_ref.shape[0]):
        total = total + len_ref[u]
        ends.append(total)

    def segment(positions):
        found = jnp.zeros(positions.shape, jnp.int32)
        for end in ends:
            found = found + jnp.where(positions >= end, 1, 0)
        return found.astype(F32)

    lane = lax.broadcasted_iota(jnp.int32, (1, 128), 1)
    codes = []
    for b in range(blocks):
        at = (first_block + b) * 128 + lane
        codes.append(jnp.where((live_rows[b] == 1.0) & (at >= 0), segment(at), -1.0))
    code_cols = as_columns(codes)

    keys = 192
    key_at = lax.broadcasted_iota(jnp.int32, (keys, 128), 0)
    query_at = lax.broadcasted_iota(jnp.int32, (keys, 128), 1)
    apart = key_at // CH - query_at // CH
    in_band = (apart >= 0) & (apart <= 2)
    same = key_at == query_at + CH

    carry_k = carry_v = None
    for t in range(tiles):
        base = 128 * t
        q = x_scr[0, base + HALO : base + HALO + 128, :]
        g = x_scr[3, base + HALO : base + HALO + 128, :]
        k = x_scr[1, base + CH : base + CH + keys, :]
        v = x_scr[2, base + CH : base + CH + keys, :]
        query_seg = segment((first_block + t) * 128 + HALO + lane)
        code = jnp.concatenate([code_cols[CH:, t : t + 1], code_cols[: keys - 96, t + 1 : t + 2]], axis=0)
        allowed = in_band & ((code == query_seg) | same)
        scores = jnp.where(allowed, rows_by_rows(k, q) * SCALE, -1e30)
        weights = jnp.exp(scores - jnp.max(scores, axis=0, keepdims=True))
        probs = weights * (1.0 / jnp.sum(weights, axis=0, keepdims=True))
        rounded = probs.astype(BF16)
        prob_grad = rows_by_rows(v, g)
        centre = jnp.sum(probs * prob_grad, axis=0, keepdims=True)
        score_grad = (probs * (prob_grad - centre) * SCALE).astype(BF16)
        mixed = cols_by_cols(rounded, v).astype(BF16)
        query_grad = cols_by_cols(score_grad, k).astype(BF16)
        key_grad = plain(score_grad, q)
        value_grad = plain(rounded, g)
        live = jnp.concatenate([live_cols[HALO:, t : t + 1], live_cols[:HALO, t + 1 : t + 2]], axis=0)
        mixed = jnp.where(live == 1.0, mixed, jnp.zeros_like(mixed))
        lo, hi = (HALO if t == 0 else 0), (HALO if t == tiles - 1 else 128)
        at = base - HALO
        mixed_ref[at + lo : at + hi, :] = mixed[lo:hi]
        grads_ref[at + lo : at + hi, 0:HS] = query_grad[lo:hi]
        if t > 0:
            key_grad = jnp.concatenate([key_grad[:64] + carry_k, key_grad[64:]], axis=0)
            value_grad = jnp.concatenate([value_grad[:64] + carry_v, value_grad[64:]], axis=0)
        carry_k, carry_v = key_grad[128:], value_grad[128:]
        lo, hi = (96 if t == 0 else 0), (96 if t == tiles - 1 else 128)
        at = base - 96
        grads_ref[at + lo : at + hi, HS : 2 * HS] = key_grad[lo:hi].astype(BF16)
        grads_ref[at + lo : at + hi, 2 * HS : 3 * HS] = value_grad[lo:hi].astype(BF16)


def attend(lengths, proj, halo, gain, qkv_weight, out_weight, pad2d):
    count = proj.shape[1]
    vmem = pl.BlockSpec(memory_space=pltpu.VMEM)
    return pl.pallas_call(
        attend_body,
        in_specs=[pl.BlockSpec(memory_space=pltpu.SMEM)] + [vmem] * 6,
        out_specs=[vmem, vmem],
        out_shape=[
            jax.ShapeDtypeStruct((count, 3 * HS), BF16),
            jax.ShapeDtypeStruct((count, HS), BF16),
        ],
        scratch_shapes=[pltpu.VMEM((4, count + 4 * HALO, HS), BF16)],
        compiler_params=pltpu.CompilerParams(vmem_limit_bytes=20 << 20),
        name="attend",
    )(lengths, proj, halo, gain, qkv_weight, out_weight, pad2d)


def input_body(frames_ref, gain_ref, qkv_ref, grads_ref, near_ref, across_ref, w_scr):
    place = lax.axis_index("mp")
    y, xh = place // 2, place % 2

    @pl.when(pl.program_id(0) == 0)
    def _():
        for m in range(3):
            w_scr[:, m * HS : (m + 1) * HS] = qkv_ref[m]

    incoming = rows_by_rows(grads_ref[...], w_scr[...])
    normal_form, inverse = normalised(frames_ref[...])
    scaled = incoming * gain_ref[...]
    mean_grad = jnp.mean(scaled, axis=-1, keepdims=True)
    mean_proj = jnp.mean(scaled * normal_form, axis=-1, keepdims=True)
    result = (inverse * (scaled - mean_grad - normal_form * mean_proj)).astype(BF16)
    for p in range(4):
        low = result[:, 256 * p : 256 * p + 128]
        high = result[:, 256 * p + 128 : 256 * p + 256]
        away = (p - y + 4) % 4
        near_ref[away] = jnp.where(xh == 0, low, high)
        across_ref[away] = jnp.where(xh == 0, high, low)


def input_terms(frames, gain, qkv_weight, grads):
    count, width = frames.shape
    rows = 256
    whole = lambda *shape: pl.BlockSpec(shape, lambda i: (0,) * len(shape))
    return pl.pallas_call(
        input_body,
        grid=(count // rows,),
        in_specs=[
            pl.BlockSpec((rows, width), lambda i: (i, 0)),
            whole(1, width),
            whole(*qkv_weight.shape),
            pl.BlockSpec((rows, 3 * HS), lambda i: (i, 0)),
        ],
        out_specs=[pl.BlockSpec((4, rows, 128), lambda i: (0, i, 0))] * 2,
        out_shape=[jax.ShapeDtypeStruct((4, count, 128), BF16)] * 2,
        scratch_shapes=[pltpu.VMEM((width, 3 * HS), BF16)],
        compiler_params=pltpu.CompilerParams(vmem_limit_bytes=20 << 20),
        name="input_terms",
    )(frames, gain, qkv_weight, grads)


def weight_body(normed_ref, cot_ref, grads_ref, mixed_ref, keep_ref, send_ref):
    core = lax.axis_index("tm") % 2
    qkv = cols_by_cols(grads_ref[...], normed_ref[...]).astype(BF16)
    out = cols_by_cols(mixed_ref[...], cot_ref[...]).astype(BF16)
    full = jnp.concatenate([qkv, out], axis=0)
    for z in range(8):
        both = full[:, z * 128 : (z + 1) * 128].T
        low, high = both[:64], both[64:]
        keep = jnp.where(core == 0, low, high)
        send = jnp.where(core == 0, high, low)
        for m in range(4):
            keep_ref[z, m] = keep[:, m * HS : (m + 1) * HS]
            send_ref[z, m] = send[:, m * HS : (m + 1) * HS]


def weight_terms(normed, cotangent, grads, mixed):
    count, width = normed.shape
    vmem = pl.BlockSpec(memory_space=pltpu.VMEM)
    part = jax.ShapeDtypeStruct((8, 4, width // 16, HS), BF16)
    return pl.pallas_call(
        weight_body,
        in_specs=[vmem] * 4,
        out_specs=[vmem] * 2,
        out_shape=[part] * 2,
        compiler_params=pltpu.CompilerParams(vmem_limit_bytes=20 << 20),
        name="weight_terms",
    )(normed, cotangent, grads, mixed)


def shifted(x, axis, by):
    size = lax.axis_size(axis)
    return lax.ppermute(x, axis, [(i, (i + by) % size) for i in range(size)])


def swapped(x, axis, bit):
    return lax.ppermute(x, axis, [(i, i ^ bit) for i in range(lax.axis_size(axis))])


def total(*parts):
    summed = parts[0].astype(F32)
    for part in parts[1:]:
        summed = summed + part.astype(F32)
    return summed


def on_device(frames, norm_gain, qkv_weight, out_weight, cotangent, pad_mask, utt_lengths):
    shards = lax.axis_size("tm")
    up = [(i, i + 1) for i in range(shards - 1)]
    down = [(i + 1, i) for i in range(shards - 1)]
    ends = jnp.stack([frames[-HALO:], cotangent[-HALO:]])
    starts = jnp.stack([frames[:HALO], cotangent[:HALO]])
    halo = jnp.concatenate([lax.ppermute(ends, "tm", up), lax.ppermute(starts, "tm", down)], axis=1)
    gain = norm_gain[None, :]
    pad2d = pad_mask.reshape(-1, 128)
    proj, normed = project(frames, gain, qkv_weight, out_weight, cotangent, pad2d)
    grads, mixed = attend(utt_lengths, proj, halo, gain, qkv_weight, out_weight, pad2d)
    near, across = input_terms(frames, gain, qkv_weight, grads)
    across = swapped(across, "mp", 1)
    (normed, cotangent, grads, mixed), _ = lax.optimization_barrier(((normed, cotangent, grads, mixed), near))
    keep, send = weight_terms(normed, cotangent, grads, mixed)
    other = swapped(send, "tm", 1)
    chip = total(keep, other).astype(BF16)
    same_core = [[c + 2 * z for z in range(shards // 2)] for c in range(2)]
    weights = lax.all_to_all(chip, "tm", 0, 0, tiled=True, axis_index_groups=same_core)
    (near, across), _ = lax.optimization_barrier(((near, across), chip))
    col = [total(near[k], across[k]) for k in range(4)]
    col_in = [shifted(col[k].astype(BF16), "mp", 2 * k) for k in (2, 1, 3)]
    frame_grad = total(col[0], *col_in).astype(BF16)
    qkv_grad = weights[:, :3].astype(F32).sum(axis=0)
    out_grad = weights[:, 3].astype(F32).sum(axis=0)
    return frame_grad, qkv_grad, out_grad.T


def solution(mesh):
    placed = (
        P(("batch", "tm"), None),
        P(),
        P(None, None, "mp"),
        P("mp", None),
        P(("batch", "tm"), None),
        P("batch"),
        P("batch"),
    )
    return jax.shard_map(
        on_device,
        mesh=mesh,
        in_specs=placed,
        out_specs=(P(("batch", "tm"), "mp"), P("batch", "tm", "mp"), P(("batch", "mp"), "tm")),
        check_vma=False,
    )
```

```python
import jax
import jax.numpy as jnp
from jax import lax
from jax.experimental import pallas as pl
from jax.experimental.pallas import tpu as pltpu
from jax.sharding import PartitionSpec as P

HS = 128
CH = 32
HALO = 64
EPSILON = 1e-05
SCALE = HS ** (-0.5)
F32 = jnp.float32
BF16 = jnp.bfloat16


def rows_by_rows(left, right):
    return lax.dot_general(left, right, (((1,), (1,)), ((), ())), preferred_element_type=F32)


def cols_by_cols(left, right):
    return lax.dot_general(left, right, (((0,), (0,)), ((), ())), preferred_element_type=F32)


def plain(left, right):
    return jnp.dot(left, right, preferred_element_type=F32)


def normalised(values):
    values = values.astype(F32)
    center = values - jnp.mean(values, axis=-1, keepdims=True)
    inverse = lax.rsqrt(jnp.mean(center * center, axis=-1, keepdims=True) + EPSILON)
    return center * inverse, inverse


def pad_rows(pad_ref, first, count):
    total = pad_ref.shape[0]
    return [pad_ref[pl.ds(jnp.clip(first + i, 0, total - 1), 1), :] for i in range(count)]


def as_columns(rows):
    height = -(-len(rows) // 8) * 8
    full = jnp.concatenate(rows + [jnp.zeros_like(rows[0])] * (height - len(rows)), axis=0)
    return full.T


def project_body(frames_ref, gain_ref, qkv_ref, out_ref, cot_ref, pad_ref, proj_ref, normed_ref, w_scr):
    step = pl.program_id(0)
    rows = frames_ref.shape[0]

    @pl.when(step == 0)
    def _():
        for m in range(3):
            w_scr[:, m * HS : (m + 1) * HS] = qkv_ref[m]

    normal_form, _ = normalised(frames_ref[...])
    normed = (normal_form * gain_ref[...]).astype(BF16)
    normed_ref[...] = normed
    qkv = plain(normed, w_scr[...]).astype(BF16)
    for m in range(3):
        proj_ref[m] = qkv[:, m * HS : (m + 1) * HS]
    per_step = rows // 128
    first = (lax.axis_index("tm") * pl.num_programs(0) + step) * per_step
    live = as_columns([r.astype(F32) for r in pad_rows(pad_ref, first, per_step)])
    live = jnp.concatenate([live[:, i : i + 1] for i in range(per_step)], axis=0)
    grads = rows_by_rows(cot_ref[...], out_ref[...])
    proj_ref[3] = jnp.where(live == 1.0, grads, 0.0).astype(BF16)


def project(frames, gain, qkv_weight, out_weight, cotangent, pad2d):
    count, width = frames.shape
    rows = 256
    whole = lambda *shape: pl.BlockSpec(shape, lambda i: (0,) * len(shape))
    return pl.pallas_call(
        project_body,
        grid=(count // rows,),
        in_specs=[
            pl.BlockSpec((rows, width), lambda i: (i, 0)),
            whole(1, width),
            whole(*qkv_weight.shape),
            whole(*out_weight.shape),
            pl.BlockSpec((rows, width), lambda i: (i, 0)),
            whole(*pad2d.shape),
        ],
        out_specs=[
            pl.BlockSpec((4, rows, HS), lambda i: (0, i, 0)),
            pl.BlockSpec((rows, width), lambda i: (i, 0)),
        ],
        out_shape=[
            jax.ShapeDtypeStruct((4, count, HS), BF16),
            jax.ShapeDtypeStruct((count, width), BF16),
        ],
        scratch_shapes=[pltpu.VMEM((width, 3 * HS), BF16)],
        compiler_params=pltpu.CompilerParams(vmem_limit_bytes=20 << 20),
        name="project",
    )(frames, gain, qkv_weight, out_weight, cotangent, pad2d)


def backward_body(
    len_ref, proj_ref, halo_ref, gain_ref, qkv_ref, out_ref, pad_ref, frames_hbm, normed_hbm, cot_hbm,
    near_ref, across_ref, ring0_ref, ring1_ref, ring2_ref, ring3_ref, keep_ref, send_ref,
    x_scr, grads_ref, mixed_ref, w_scr, frames_ref, normed_ref, cot_ref, sems,
):
    fetches = [
        pltpu.make_async_copy(source, target, sems.at[i])
        for i, (source, target) in enumerate(
            [(frames_hbm, frames_ref), (normed_hbm, normed_ref), (cot_hbm, cot_ref)]
        )
    ]
    for fetch in fetches:
        fetch.start()
    count = proj_ref.shape[1]
    tiles = count // 128 + 1
    shard = lax.axis_index("tm")
    first_block = shard * (count // 128) - 1
    normal_form, _ = normalised(halo_ref[0])
    normed = (normal_form * gain_ref[...]).astype(BF16)
    blocks = tiles + 1
    live_rows = [r.astype(F32) for r in pad_rows(pad_ref, first_block, blocks)]
    live_cols = as_columns(live_rows)
    halo_live = jnp.concatenate([live_cols[HALO:, 0:1], live_cols[:HALO, blocks - 1 : blocks]], axis=0)
    zeros = jnp.zeros((HALO, HS), BF16)
    for m in range(4):
        if m < 3:
            part = plain(normed, qkv_ref[m])
        else:
            part = jnp.where(halo_live == 1.0, rows_by_rows(halo_ref[1], out_ref[...]), 0.0)
        part = part.astype(BF16)
        x_scr[m, 0:HALO, :] = zeros
        x_scr[m, HALO : 2 * HALO, :] = part[:HALO]
        x_scr[m, 2 * HALO : 2 * HALO + count, :] = proj_ref[m]
        x_scr[m, 2 * HALO + count : 3 * HALO + count, :] = part[HALO:]
        x_scr[m, 3 * HALO + count :, :] = zeros

    ends = []
    total = 0
    for u in range(len_ref.shape[0]):
        total = total + len_ref[u]
        ends.append(total)

    def segment(positions):
        found = jnp.zeros(positions.shape, jnp.int32)
        for end in ends:
            found = found + jnp.where(positions >= end, 1, 0)
        return found.astype(F32)

    lane = lax.broadcasted_iota(jnp.int32, (1, 128), 1)
    codes = []
    for b in range(blocks):
        at = (first_block + b) * 128 + lane
        codes.append(jnp.where((live_rows[b] == 1.0) & (at >= 0), segment(at), -1.0))
    code_cols = as_columns(codes)

    keys = 192
    key_at = lax.broadcasted_iota(jnp.int32, (keys, 128), 0)
    query_at = lax.broadcasted_iota(jnp.int32, (keys, 128), 1)
    apart = key_at // CH - query_at // CH
    in_band = (apart >= 0) & (apart <= 2)
    same = key_at == query_at + CH

    place = lax.axis_index("mp")
    owners = [((place // 2 + k) % 4) * 2 + (place + s) % 2 for k in range(4) for s in range(2)]
    spans = [pl.ds(pl.multiple_of(owner * 128, 128), 128) for owner in owners]
    for m in range(3):
        for j, span in enumerate(spans):
            w_scr[j * 128 : (j + 1) * 128, m * HS : (m + 1) * HS] = qkv_ref[m, span, :]
    gain = jnp.concatenate([gain_ref[:, span] for span in spans], axis=1)
    ring_refs = (ring0_ref, ring1_ref, ring2_ref, ring3_ref)

    def input_rows(at, rows):
        incoming = rows_by_rows(grads_ref[at : at + rows, :], w_scr[...])
        frames = jnp.concatenate([frames_ref[at : at + rows, span] for span in spans], axis=1)
        normal_form, inverse = normalised(frames)
        scaled = incoming * gain
        mean_grad = jnp.mean(scaled, axis=-1, keepdims=True)
        mean_proj = jnp.mean(scaled * normal_form, axis=-1, keepdims=True)
        result = (inverse * (scaled - mean_grad - normal_form * mean_proj)).astype(BF16)
        to = at % (count // 2)
        for j in range(8):
            part = result[:, j * 128 : (j + 1) * 128]
            if at < count // 2:
                ring_refs[j // 2][j % 2, to : to + rows, :] = part
            else:
                (near_ref, across_ref)[j % 2][j // 2, to : to + rows, :] = part

    carry_k = carry_v = None
    for t in range(tiles):
        base = 128 * t
        q = x_scr[0, base + HALO : base + HALO + 128, :]
        g = x_scr[3, base + HALO : base + HALO + 128, :]
        k = x_scr[1, base + CH : base + CH + keys, :]
        v = x_scr[2, base + CH : base + CH + keys, :]
        query_seg = segment((first_block + t) * 128 + HALO + lane)
        code = jnp.concatenate([code_cols[CH:, t : t + 1], code_cols[: keys - 96, t + 1 : t + 2]], axis=0)
        allowed = in_band & ((code == query_seg) | same)
        scores = jnp.where(allowed, rows_by_rows(k, q) * SCALE, -1e30)
        weights = jnp.exp(scores - jnp.max(scores, axis=0, keepdims=True))
        probs = weights * (1.0 / jnp.sum(weights, axis=0, keepdims=True))
        rounded = probs.astype(BF16)
        prob_grad = rows_by_rows(v, g)
        centre = jnp.sum(probs * prob_grad, axis=0, keepdims=True)
        score_grad = (probs * (prob_grad - centre) * SCALE).astype(BF16)
        mixed = cols_by_cols(rounded, v).astype(BF16)
        query_grad = cols_by_cols(score_grad, k).astype(BF16)
        key_grad = plain(score_grad, q)
        value_grad = plain(rounded, g)
        live = jnp.concatenate([live_cols[HALO:, t : t + 1], live_cols[:HALO, t + 1 : t + 2]], axis=0)
        mixed = jnp.where(live == 1.0, mixed, jnp.zeros_like(mixed))
        lo, hi = (HALO if t == 0 else 0), (HALO if t == tiles - 1 else 128)
        at = base - HALO
        mixed_ref[at + lo : at + hi, :] = mixed[lo:hi]
        grads_ref[at + lo : at + hi, 0:HS] = query_grad[lo:hi]
        if t > 0:
            key_grad = jnp.concatenate([key_grad[:64] + carry_k, key_grad[64:]], axis=0)
            value_grad = jnp.concatenate([value_grad[:64] + carry_v, value_grad[64:]], axis=0)
        carry_k, carry_v = key_grad[128:], value_grad[128:]
        lo, hi = (96 if t == 0 else 0), (96 if t == tiles - 1 else 128)
        at = base - 96
        grads_ref[at + lo : at + hi, HS : 2 * HS] = key_grad[lo:hi].astype(BF16)
        grads_ref[at + lo : at + hi, 2 * HS : 3 * HS] = value_grad[lo:hi].astype(BF16)


        if t == 2:
            fetches[0].wait()
        if t >= 2 and t % 2 == 0:
            input_rows(base - 256, 256)

    fetches[1].wait()
    fetches[2].wait()
    core = shard % 2
    qkv = cols_by_cols(grads_ref[...], normed_ref[...]).astype(BF16)
    out = cols_by_cols(mixed_ref[...], cot_ref[...]).astype(BF16)
    full = jnp.concatenate([qkv, out], axis=0)
    for z in range(8):
        both = full[:, z * 128 : (z + 1) * 128].T
        low, high = both[:64], both[64:]
        keep = jnp.where(core == 0, low, high)
        send = jnp.where(core == 0, high, low)
        for m in range(4):
            keep_ref[z, m] = keep[:, m * HS : (m + 1) * HS]
            send_ref[z, m] = send[:, m * HS : (m + 1) * HS]


def backward(lengths, proj, halo, gain, qkv_weight, out_weight, pad2d, frames, normed, cotangent):
    count, width = frames.shape
    vmem = pl.BlockSpec(memory_space=pltpu.VMEM)
    half = count // 2
    shapes = [(4, half, 128)] * 2 + [(2, half, 128)] * 4 + [(8, 4, width // 16, HS)] * 2
    return pl.pallas_call(
        backward_body,
        in_specs=[pl.BlockSpec(memory_space=pltpu.SMEM)] + [vmem] * 6 + [pl.BlockSpec(memory_space=pl.ANY)] * 3,
        out_specs=[vmem] * len(shapes),
        out_shape=[jax.ShapeDtypeStruct(shape, BF16) for shape in shapes],
        scratch_shapes=[
            pltpu.VMEM((4, count + 4 * HALO, HS), BF16),
            pltpu.VMEM((count, 3 * HS), BF16),
            pltpu.VMEM((count, HS), BF16),
            pltpu.VMEM((width, 3 * HS), BF16),
            pltpu.VMEM((count, width), BF16),
            pltpu.VMEM((count, width), BF16),
            pltpu.VMEM((count, width), BF16),
            pltpu.SemaphoreType.DMA((3,)),
        ],
        compiler_params=pltpu.CompilerParams(vmem_limit_bytes=40 << 20),
        name="backward",
    )(lengths, proj, halo, gain, qkv_weight, out_weight, pad2d, frames, normed, cotangent)


def shifted(x, axis, by):
    size = lax.axis_size(axis)
    return lax.ppermute(x, axis, [(i, (i + by) % size) for i in range(size)])


def swapped(x, axis, bit):
    return lax.ppermute(x, axis, [(i, i ^ bit) for i in range(lax.axis_size(axis))])


def total(*parts):
    summed = parts[0].astype(F32)
    for part in parts[1:]:
        summed = summed + part.astype(F32)
    return summed


def on_device(frames, norm_gain, qkv_weight, out_weight, cotangent, pad_mask, utt_lengths):
    shards = lax.axis_size("tm")
    up = [(i, i + 1) for i in range(shards - 1)]
    down = [(i + 1, i) for i in range(shards - 1)]
    ends = jnp.stack([frames[-HALO:], cotangent[-HALO:]])
    starts = jnp.stack([frames[:HALO], cotangent[:HALO]])
    halo = jnp.concatenate([lax.ppermute(ends, "tm", up), lax.ppermute(starts, "tm", down)], axis=1)
    gain = norm_gain[None, :]
    pad2d = pad_mask.reshape(-1, 128)
    proj, normed = project(frames, gain, qkv_weight, out_weight, cotangent, pad2d)
    near, across, *ring, keep, send = backward(
        utt_lengths, proj, halo, gain, qkv_weight, out_weight, pad2d, frames, normed, cotangent
    )
    other = swapped(send, "tm", 1)
    across = swapped(across, "mp", 1)
    ring_in = [shifted(ring[k], "mp", 2 * k) for k in (2, 1, 3)]
    chip = total(keep, other).astype(BF16)
    same_core = [[c + 2 * z for z in range(shards // 2)] for c in range(2)]
    weights = lax.all_to_all(chip, "tm", 0, 0, tiled=True, axis_index_groups=same_core)
    col = [total(near[k], across[k]) for k in range(4)]
    col_in = [shifted(col[k].astype(BF16), "mp", 2 * k) for k in (2, 1, 3)]
    ring_in, _ = lax.optimization_barrier((ring_in, [c.astype(BF16) for c in col[1:]]))
    theirs = swapped(total(ring[0][1], *[r[1] for r in ring_in]).astype(BF16), "mp", 1)
    first_half = total(total(ring[0][0], *[r[0] for r in ring_in]), theirs).astype(BF16)
    second_half = total(col[0], *col_in).astype(BF16)
    frame_grad = jnp.concatenate([first_half, second_half], axis=0)
    qkv_grad = weights[:, :3].astype(F32).sum(axis=0)
    out_grad = weights[:, 3].astype(F32).sum(axis=0)
    return frame_grad, qkv_grad, out_grad.T


def solution(mesh):
    placed = (
        P(("batch", "tm"), None),
        P(),
        P(None, None, "mp"),
        P("mp", None),
        P(("batch", "tm"), None),
        P("batch"),
        P("batch"),
    )
    return jax.shard_map(
        on_device,
        mesh=mesh,
        in_specs=placed,
        out_specs=(P(("batch", "tm"), "mp"), P("batch", "tm", "mp"), P(("batch", "mp"), "tm")),
        check_vma=False,
    )
```

```python
import jax
import jax.numpy as jnp
from jax import lax
from jax.experimental import pallas as pl
from jax.experimental.pallas import tpu as pltpu
from jax.sharding import PartitionSpec as P

HS = 128
CH = 32
HALO = 64
EPSILON = 1e-05
SCALE = HS ** (-0.5)
F32 = jnp.float32
BF16 = jnp.bfloat16


def rows_by_rows(left, right):
    return lax.dot_general(left, right, (((1,), (1,)), ((), ())), preferred_element_type=F32)


def cols_by_cols(left, right):
    return lax.dot_general(left, right, (((0,), (0,)), ((), ())), preferred_element_type=F32)


def plain(left, right):
    return jnp.dot(left, right, preferred_element_type=F32)


def normalised(values):
    values = values.astype(F32)
    center = values - jnp.mean(values, axis=-1, keepdims=True)
    inverse = lax.rsqrt(jnp.mean(center * center, axis=-1, keepdims=True) + EPSILON)
    return center * inverse, inverse


def pad_rows(pad_ref, first, count):
    total = pad_ref.shape[0]
    return [pad_ref[pl.ds(jnp.clip(first + i, 0, total - 1), 1), :] for i in range(count)]


def as_columns(rows):
    height = -(-len(rows) // 8) * 8
    full = jnp.concatenate(rows + [jnp.zeros_like(rows[0])] * (height - len(rows)), axis=0)
    return full.T


def project_body(frames_ref, gain_ref, qkv_ref, out_ref, cot_ref, pad_ref, proj_ref, normed_ref, w_scr):
    step = pl.program_id(0)
    rows = frames_ref.shape[0]

    @pl.when(step == 0)
    def _():
        for m in range(3):
            w_scr[:, m * HS : (m + 1) * HS] = qkv_ref[m]

    normal_form, _ = normalised(frames_ref[...])
    normed = (normal_form * gain_ref[...]).astype(BF16)
    normed_ref[...] = normed
    qkv = plain(normed, w_scr[...]).astype(BF16)
    for m in range(3):
        proj_ref[m] = qkv[:, m * HS : (m + 1) * HS]
    per_step = rows // 128
    first = (lax.axis_index("tm") * pl.num_programs(0) + step) * per_step
    live = as_columns([r.astype(F32) for r in pad_rows(pad_ref, first, per_step)])
    live = jnp.concatenate([live[:, i : i + 1] for i in range(per_step)], axis=0)
    grads = rows_by_rows(cot_ref[...], out_ref[...])
    proj_ref[3] = jnp.where(live == 1.0, grads, 0.0).astype(BF16)


def project(frames, gain, qkv_weight, out_weight, cotangent, pad2d):
    count, width = frames.shape
    rows = 256
    whole = lambda *shape: pl.BlockSpec(shape, lambda i: (0,) * len(shape))
    return pl.pallas_call(
        project_body,
        grid=(count // rows,),
        in_specs=[
            pl.BlockSpec((rows, width), lambda i: (i, 0)),
            whole(1, width),
            whole(*qkv_weight.shape),
            whole(*out_weight.shape),
            pl.BlockSpec((rows, width), lambda i: (i, 0)),
            whole(*pad2d.shape),
        ],
        out_specs=[
            pl.BlockSpec((4, rows, HS), lambda i: (0, i, 0)),
            pl.BlockSpec((rows, width), lambda i: (i, 0)),
        ],
        out_shape=[
            jax.ShapeDtypeStruct((4, count, HS), BF16),
            jax.ShapeDtypeStruct((count, width), BF16),
        ],
        scratch_shapes=[pltpu.VMEM((width, 3 * HS), BF16)],
        compiler_params=pltpu.CompilerParams(vmem_limit_bytes=48 << 20),
        name="project",
    )(frames, gain, qkv_weight, out_weight, cotangent, pad2d)


def backward_body(
    len_ref, proj_ref, halo_ref, gain_ref, qkv_ref, out_ref, pad_ref, frames_hbm, normed_hbm, cot_hbm,
    near_ref, across_ref, ring0_ref, ring1_ref, ring2_ref, ring3_ref, keep_ref, send_ref,
    x_scr, grads_ref, mixed_ref, w_scr, frames_ref, normed_ref, cot_ref, sems,
):
    fetches = [
        pltpu.make_async_copy(source, target, sems.at[i])
        for i, (source, target) in enumerate(
            [(frames_hbm, frames_ref), (normed_hbm, normed_ref), (cot_hbm, cot_ref)]
        )
    ]
    for fetch in fetches:
        fetch.start()
    count = proj_ref.shape[1]
    tiles = count // 128 + 1
    shard = lax.axis_index("tm")
    first_block = shard * (count // 128) - 1
    normal_form, _ = normalised(halo_ref[0])
    normed = (normal_form * gain_ref[...]).astype(BF16)
    blocks = tiles + 1
    live_rows = [r.astype(F32) for r in pad_rows(pad_ref, first_block, blocks)]
    live_cols = as_columns(live_rows)
    halo_live = jnp.concatenate([live_cols[HALO:, 0:1], live_cols[:HALO, blocks - 1 : blocks]], axis=0)
    zeros = jnp.zeros((HALO, HS), BF16)
    for m in range(4):
        if m < 3:
            part = plain(normed, qkv_ref[m])
        else:
            part = jnp.where(halo_live == 1.0, rows_by_rows(halo_ref[1], out_ref[...]), 0.0)
        part = part.astype(BF16)
        x_scr[m, 0:HALO, :] = zeros
        x_scr[m, HALO : 2 * HALO, :] = part[:HALO]
        x_scr[m, 2 * HALO : 2 * HALO + count, :] = proj_ref[m]
        x_scr[m, 2 * HALO + count : 3 * HALO + count, :] = part[HALO:]
        x_scr[m, 3 * HALO + count :, :] = zeros

    ends = []
    total = 0
    for u in range(len_ref.shape[0]):
        total = total + len_ref[u]
        ends.append(total)

    def segment(positions):
        found = jnp.zeros(positions.shape, jnp.int32)
        for end in ends:
            found = found + jnp.where(positions >= end, 1, 0)
        return found.astype(F32)

    lane = lax.broadcasted_iota(jnp.int32, (1, 128), 1)
    codes = []
    for b in range(blocks):
        at = (first_block + b) * 128 + lane
        codes.append(jnp.where((live_rows[b] == 1.0) & (at >= 0), segment(at), -1.0))
    code_cols = as_columns(codes)

    keys = 192
    key_at = lax.broadcasted_iota(jnp.int32, (keys, 128), 0)
    query_at = lax.broadcasted_iota(jnp.int32, (keys, 128), 1)
    apart = key_at // CH - query_at // CH
    in_band = (apart >= 0) & (apart <= 2)
    same = key_at == query_at + CH

    place = lax.axis_index("mp")
    owners = [((place // 2 + k) % 4) * 2 + (place + s) % 2 for k in range(4) for s in range(2)]
    spans = [pl.ds(pl.multiple_of(owner * 128, 128), 128) for owner in owners]
    for m in range(3):
        for j, span in enumerate(spans):
            w_scr[j * 128 : (j + 1) * 128, m * HS : (m + 1) * HS] = qkv_ref[m, span, :]
    gain = jnp.concatenate([gain_ref[:, span] for span in spans], axis=1)
    ring_refs = (ring0_ref, ring1_ref, ring2_ref, ring3_ref)

    def input_rows(at, rows):
        incoming = rows_by_rows(grads_ref[at : at + rows, :], w_scr[...])
        frames = jnp.concatenate([frames_ref[at : at + rows, span] for span in spans], axis=1)
        normal_form, inverse = normalised(frames)
        scaled = incoming * gain
        mean_grad = jnp.mean(scaled, axis=-1, keepdims=True)
        mean_proj = jnp.mean(scaled * normal_form, axis=-1, keepdims=True)
        result = (inverse * (scaled - mean_grad - normal_form * mean_proj)).astype(BF16)
        to = at % (count // 2)
        for j in range(8):
            part = result[:, j * 128 : (j + 1) * 128]
            if at < count // 2:
                ring_refs[j // 2][j % 2, to : to + rows, :] = part
            else:
                (near_ref, across_ref)[j % 2][j // 2, to : to + rows, :] = part

    carry_k = carry_v = None
    for t in range(tiles):
        base = 128 * t
        q = x_scr[0, base + HALO : base + HALO + 128, :]
        g = x_scr[3, base + HALO : base + HALO + 128, :]
        k = x_scr[1, base + CH : base + CH + keys, :]
        v = x_scr[2, base + CH : base + CH + keys, :]
        query_seg = segment((first_block + t) * 128 + HALO + lane)
        code = jnp.concatenate([code_cols[CH:, t : t + 1], code_cols[: keys - 96, t + 1 : t + 2]], axis=0)
        allowed = in_band & ((code == query_seg) | same)
        scores = jnp.where(allowed, rows_by_rows(k, q) * SCALE, -1e30)
        weights = jnp.exp(scores - jnp.max(scores, axis=0, keepdims=True))
        probs = weights * (1.0 / jnp.sum(weights, axis=0, keepdims=True))
        rounded = probs.astype(BF16)
        prob_grad = rows_by_rows(v, g)
        centre = jnp.sum(probs * prob_grad, axis=0, keepdims=True)
        score_grad = (probs * (prob_grad - centre) * SCALE).astype(BF16)
        mixed = cols_by_cols(rounded, v).astype(BF16)
        query_grad = cols_by_cols(score_grad, k).astype(BF16)
        key_grad = plain(score_grad, q)
        value_grad = plain(rounded, g)
        live = jnp.concatenate([live_cols[HALO:, t : t + 1], live_cols[:HALO, t + 1 : t + 2]], axis=0)
        mixed = jnp.where(live == 1.0, mixed, jnp.zeros_like(mixed))
        lo, hi = (HALO if t == 0 else 0), (HALO if t == tiles - 1 else 128)
        at = base - HALO
        mixed_ref[at + lo : at + hi, :] = mixed[lo:hi]
        grads_ref[at + lo : at + hi, 0:HS] = query_grad[lo:hi]
        if t > 0:
            key_grad = jnp.concatenate([key_grad[:64] + carry_k, key_grad[64:]], axis=0)
            value_grad = jnp.concatenate([value_grad[:64] + carry_v, value_grad[64:]], axis=0)
        carry_k, carry_v = key_grad[128:], value_grad[128:]
        lo, hi = (96 if t == 0 else 0), (96 if t == tiles - 1 else 128)
        at = base - 96
        grads_ref[at + lo : at + hi, HS : 2 * HS] = key_grad[lo:hi].astype(BF16)
        grads_ref[at + lo : at + hi, 2 * HS : 3 * HS] = value_grad[lo:hi].astype(BF16)


        if t == 2:
            fetches[0].wait()
        if t >= 2 and t % 2 == 0:
            input_rows(base - 256, 256)

    fetches[1].wait()
    fetches[2].wait()
    core = shard % 2
    qkv = cols_by_cols(grads_ref[...], normed_ref[...]).astype(BF16)
    out = cols_by_cols(mixed_ref[...], cot_ref[...]).astype(BF16)
    full = jnp.concatenate([qkv, out], axis=0)
    for z in range(8):
        both = full[:, z * 128 : (z + 1) * 128].T
        low, high = both[:64], both[64:]
        keep = jnp.where(core == 0, low, high)
        send = jnp.where(core == 0, high, low)
        for m in range(4):
            keep_ref[z, m] = keep[:, m * HS : (m + 1) * HS]
            send_ref[z, m] = send[:, m * HS : (m + 1) * HS]


def backward(lengths, proj, halo, gain, qkv_weight, out_weight, pad2d, frames, normed, cotangent):
    count, width = frames.shape
    vmem = pl.BlockSpec(memory_space=pltpu.VMEM)
    half = count // 2
    shapes = [(4, half, 128)] * 2 + [(2, half, 128)] * 4 + [(8, 4, width // 16, HS)] * 2
    return pl.pallas_call(
        backward_body,
        in_specs=[pl.BlockSpec(memory_space=pltpu.SMEM)] + [vmem] * 6 + [pl.BlockSpec(memory_space=pl.ANY)] * 3,
        out_specs=[vmem] * len(shapes),
        out_shape=[jax.ShapeDtypeStruct(shape, BF16) for shape in shapes],
        scratch_shapes=[
            pltpu.VMEM((4, count + 4 * HALO, HS), BF16),
            pltpu.VMEM((count, 3 * HS), BF16),
            pltpu.VMEM((count, HS), BF16),
            pltpu.VMEM((width, 3 * HS), BF16),
            pltpu.VMEM((count, width), BF16),
            pltpu.VMEM((count, width), BF16),
            pltpu.VMEM((count, width), BF16),
            pltpu.SemaphoreType.DMA((3,)),
        ],
        compiler_params=pltpu.CompilerParams(vmem_limit_bytes=40 << 20),
        name="backward",
    )(lengths, proj, halo, gain, qkv_weight, out_weight, pad2d, frames, normed, cotangent)


def shifted(x, axis, by):
    size = lax.axis_size(axis)
    return lax.ppermute(x, axis, [(i, (i + by) % size) for i in range(size)])


def swapped(x, axis, bit):
    return lax.ppermute(x, axis, [(i, i ^ bit) for i in range(lax.axis_size(axis))])


def total(*parts):
    summed = parts[0].astype(F32)
    for part in parts[1:]:
        summed = summed + part.astype(F32)
    return summed


def on_device(frames, norm_gain, qkv_weight, out_weight, cotangent, pad_mask, utt_lengths):
    shards = lax.axis_size("tm")
    up = [(i, i + 1) for i in range(shards - 1)]
    down = [(i + 1, i) for i in range(shards - 1)]
    ends = jnp.stack([frames[-HALO:], cotangent[-HALO:]])
    starts = jnp.stack([frames[:HALO], cotangent[:HALO]])
    halo = jnp.concatenate([lax.ppermute(ends, "tm", up), lax.ppermute(starts, "tm", down)], axis=1)
    gain = norm_gain[None, :]
    pad2d = pad_mask.reshape(-1, 128)
    proj, normed = project(frames, gain, qkv_weight, out_weight, cotangent, pad2d)
    near, across, *ring, keep, send = backward(
        utt_lengths, proj, halo, gain, qkv_weight, out_weight, pad2d, frames, normed, cotangent
    )
    other = swapped(send, "tm", 1)
    across = swapped(across, "mp", 1)
    ring_in = [shifted(ring[k], "mp", 2 * k) for k in (2, 1, 3)]
    chip = total(keep, other).astype(BF16)
    same_core = [[c + 2 * z for z in range(shards // 2)] for c in range(2)]
    weights = lax.all_to_all(chip, "tm", 0, 0, tiled=True, axis_index_groups=same_core)
    (near, across, ring_in), _ = lax.optimization_barrier(((near, across, ring_in), chip))
    col = [total(near[k], across[k]) for k in range(4)]
    col_in = [shifted(col[k].astype(BF16), "mp", 2 * k) for k in (2, 1, 3)]
    ring_in, _ = lax.optimization_barrier((ring_in, [c.astype(BF16) for c in col[1:]]))
    theirs = swapped(total(ring[0][1], *[r[1] for r in ring_in]).astype(BF16), "mp", 1)
    first_half = total(total(ring[0][0], *[r[0] for r in ring_in]), theirs).astype(BF16)
    second_half = total(col[0], *col_in).astype(BF16)
    frame_grad = jnp.concatenate([first_half, second_half], axis=0)
    qkv_grad = weights[:, :3].astype(F32).sum(axis=0)
    out_grad = weights[:, 3].astype(F32).sum(axis=0)
    return frame_grad, qkv_grad, out_grad.T


def solution(mesh):
    placed = (
        P(("batch", "tm"), None),
        P(),
        P(None, None, "mp"),
        P("mp", None),
        P(("batch", "tm"), None),
        P("batch"),
        P("batch"),
    )
    return jax.shard_map(
        on_device,
        mesh=mesh,
        in_specs=placed,
        out_specs=(P(("batch", "tm"), "mp"), P("batch", "tm", "mp"), P(("batch", "mp"), "tm")),
        check_vma=False,
    )
```

```python
import jax
import jax.numpy as jnp
from jax import lax
from jax.experimental import pallas as pl
from jax.experimental.pallas import tpu as pltpu
from jax.sharding import PartitionSpec as P

HS = 128
CH = 32
HALO = 64
EPSILON = 1e-05
SCALE = HS ** (-0.5)
F32 = jnp.float32
BF16 = jnp.bfloat16


def rows_by_rows(left, right):
    return lax.dot_general(left, right, (((1,), (1,)), ((), ())), preferred_element_type=F32)


def cols_by_cols(left, right):
    return lax.dot_general(left, right, (((0,), (0,)), ((), ())), preferred_element_type=F32)


def plain(left, right):
    return jnp.dot(left, right, preferred_element_type=F32)


def normalised(values):
    values = values.astype(F32)
    mean = jnp.mean(values, axis=-1, keepdims=True)
    center = values - mean
    inverse = lax.rsqrt(jnp.mean(center * center, axis=-1, keepdims=True) + EPSILON)
    return center * inverse, inverse, mean


def pad_rows(pad_ref, first, count):
    total = pad_ref.shape[0]
    return [pad_ref[pl.ds(jnp.clip(first + i, 0, total - 1), 1), :] for i in range(count)]


def as_columns(rows):
    height = -(-len(rows) // 8) * 8
    full = jnp.concatenate(rows + [jnp.zeros_like(rows[0])] * (height - len(rows)), axis=0)
    return full.T


def project_body(
    frames_hbm, gain_ref, qkv_hbm, out_hbm, cot_hbm, pad_ref, proj_ref, stats_ref, normed_hbm,
    frames_ref, w_scr, out_ref, cot_ref, normed_ref, sems,
):
    count = frames_ref.shape[0]
    rows = count // 2
    halves = [pl.ds(0, rows), pl.ds(rows, rows)]
    moves = [(frames_hbm.at[span], frames_ref.at[span]) for span in halves]
    moves += [(qkv_hbm.at[m], w_scr.at[:, m * HS : (m + 1) * HS]) for m in range(3)]
    moves += [(out_hbm, out_ref), (cot_hbm, cot_ref)]
    moves += [(normed_ref.at[span], normed_hbm.at[span]) for span in halves]
    copies = [pltpu.make_async_copy(source, target, sems.at[i]) for i, (source, target) in enumerate(moves)]
    for i in (0, 2, 3, 4, 1, 5, 6):
        copies[i].start()
    lane = lax.broadcasted_iota(jnp.int32, (rows, 128), 1)

    def norm_rows(half):
        normal_form, inverse, mean = normalised(frames_ref[halves[half], :])
        stats_ref[halves[half], :] = jnp.where(lane == 0, mean, inverse)
        normed = (normal_form * gain_ref[...]).astype(BF16)
        normed_ref[halves[half], :] = normed
        return normed

    def project_rows(half, normed):
        qkv = plain(normed, w_scr[...]).astype(BF16)
        for m in range(3):
            proj_ref[m, halves[half], :] = qkv[:, m * HS : (m + 1) * HS]

    copies[0].wait()
    first = norm_rows(0)
    copies[7].start()
    for i in (2, 3, 4, 1):
        copies[i].wait()
    project_rows(0, first)
    second = norm_rows(1)
    for i in (5, 6):
        copies[i].wait()
    copies[8].start()
    blocks = count // 128
    live = as_columns([r.astype(F32) for r in pad_rows(pad_ref, lax.axis_index("tm") * blocks, blocks)])
    live = jnp.concatenate([live[:, i : i + 1] for i in range(blocks)], axis=0)
    project_rows(1, second)
    grads = rows_by_rows(cot_ref[...], out_ref[...])
    proj_ref[3] = jnp.where(live == 1.0, grads, 0.0).astype(BF16)
    copies[7].wait()
    copies[8].wait()


def project(frames, gain, qkv_weight, out_weight, cotangent, pad2d):
    count, width = frames.shape
    vmem = pl.BlockSpec(memory_space=pltpu.VMEM)
    hbm = pl.BlockSpec(memory_space=pl.ANY)
    return pl.pallas_call(
        project_body,
        in_specs=[hbm, vmem, hbm, hbm, hbm, vmem],
        out_specs=[vmem, vmem, hbm],
        out_shape=[
            jax.ShapeDtypeStruct((4, count, HS), BF16),
            jax.ShapeDtypeStruct((count, 128), F32),
            jax.ShapeDtypeStruct((count, width), BF16),
        ],
        scratch_shapes=[
            pltpu.VMEM((count, width), BF16),
            pltpu.VMEM((width, 3 * HS), BF16),
            pltpu.VMEM(out_weight.shape, BF16),
            pltpu.VMEM((count, width), BF16),
            pltpu.VMEM((count, width), BF16),
            pltpu.SemaphoreType.DMA((9,)),
        ],
        compiler_params=pltpu.CompilerParams(vmem_limit_bytes=48 << 20),
        name="project",
    )(frames, gain, qkv_weight, out_weight, cotangent, pad2d)


def backward_body(
    len_ref, proj_ref, stats_ref, halo_ref, gain_ref, qkv_ref, out_ref, pad_ref, frames_hbm, normed_hbm, cot_hbm,
    near_ref, across_ref, ring0_ref, ring1_ref, ring2_ref, ring3_ref, keep_ref, send_ref,
    x_scr, grads_ref, mixed_ref, w_scr, frames_ref, normed_ref, cot_ref, sems,
):
    fetches = [
        pltpu.make_async_copy(source, target, sems.at[i])
        for i, (source, target) in enumerate(
            [(frames_hbm, frames_ref), (normed_hbm, normed_ref), (cot_hbm, cot_ref)]
        )
    ]
    for fetch in fetches:
        fetch.start()
    count = proj_ref.shape[1]
    tiles = count // 128 + 1
    shard = lax.axis_index("tm")
    first_block = shard * (count // 128) - 1
    normal_form, _, _ = normalised(halo_ref[0])
    normed = (normal_form * gain_ref[...]).astype(BF16)
    blocks = tiles + 1
    live_rows = [r.astype(F32) for r in pad_rows(pad_ref, first_block, blocks)]
    live_cols = as_columns(live_rows)
    halo_live = jnp.concatenate([live_cols[HALO:, 0:1], live_cols[:HALO, blocks - 1 : blocks]], axis=0)
    zeros = jnp.zeros((HALO, HS), BF16)
    for m in range(4):
        if m < 3:
            part = plain(normed, qkv_ref[m])
        else:
            part = jnp.where(halo_live == 1.0, rows_by_rows(halo_ref[1], out_ref[...]), 0.0)
        part = part.astype(BF16)
        x_scr[m, 0:HALO, :] = zeros
        x_scr[m, HALO : 2 * HALO, :] = part[:HALO]
        x_scr[m, 2 * HALO : 2 * HALO + count, :] = proj_ref[m]
        x_scr[m, 2 * HALO + count : 3 * HALO + count, :] = part[HALO:]
        x_scr[m, 3 * HALO + count :, :] = zeros

    ends = []
    total = 0
    for u in range(len_ref.shape[0]):
        total = total + len_ref[u]
        ends.append(total)

    def segment(positions):
        found = jnp.zeros(positions.shape, jnp.int32)
        for end in ends:
            found = found + jnp.where(positions >= end, 1, 0)
        return found.astype(F32)

    lane = lax.broadcasted_iota(jnp.int32, (1, 128), 1)
    codes = []
    for b in range(blocks):
        at = (first_block + b) * 128 + lane
        codes.append(jnp.where((live_rows[b] == 1.0) & (at >= 0), segment(at), -1.0))
    code_cols = as_columns(codes)

    keys = 192
    key_at = lax.broadcasted_iota(jnp.int32, (keys, 128), 0)
    query_at = lax.broadcasted_iota(jnp.int32, (keys, 128), 1)
    apart = key_at // CH - query_at // CH
    in_band = (apart >= 0) & (apart <= 2)
    same = key_at == query_at + CH

    place = lax.axis_index("mp")
    owners = [jnp.bitwise_xor(place, j) for j in range(8)]
    spans = [pl.ds(pl.multiple_of(owner * 128, 128), 128) for owner in owners]
    for m in range(3):
        for j, span in enumerate(spans):
            w_scr[j * 128 : (j + 1) * 128, m * HS : (m + 1) * HS] = qkv_ref[m, span, :]
    gain = jnp.concatenate([gain_ref[:, span] for span in spans], axis=1)
    ring_refs = (ring0_ref, ring1_ref, ring2_ref, ring3_ref)

    def input_rows(at, rows):
        incoming = rows_by_rows(grads_ref[at : at + rows, :], w_scr[...])
        frames = jnp.concatenate([frames_ref[at : at + rows, span] for span in spans], axis=1)
        center = frames.astype(F32) - stats_ref[at : at + rows, 0:1]
        inverse = stats_ref[at : at + rows, 1:2]
        scaled = incoming * gain
        mean_grad = jnp.mean(scaled, axis=-1, keepdims=True)
        slope = jnp.mean(scaled * center, axis=-1, keepdims=True) * (inverse * inverse)
        result = (inverse * (scaled - mean_grad - center * slope)).astype(BF16)
        to = at % (count // 2)
        for j in range(8):
            part = result[:, j * 128 : (j + 1) * 128]
            if at < count // 2:
                ring_refs[j // 2][j % 2, to : to + rows, :] = part
            else:
                (near_ref, across_ref)[j % 2][j // 2, to : to + rows, :] = part

    carry = [None, None]

    def attention(tiles_now):
        q = [x_scr[0, 128 * t + HALO : 128 * t + HALO + 128, :] for t in tiles_now]
        g = [x_scr[3, 128 * t + HALO : 128 * t + HALO + 128, :] for t in tiles_now]
        k = [x_scr[1, 128 * t + CH : 128 * t + CH + keys, :] for t in tiles_now]
        v = [x_scr[2, 128 * t + CH : 128 * t + CH + keys, :] for t in tiles_now]
        n = range(len(tiles_now))
        scores = [rows_by_rows(k[i], q[i]) for i in n]
        prob_grad = [rows_by_rows(v[i], g[i]) for i in n]
        probs = []
        for i in n:
            t = tiles_now[i]
            query_seg = segment((first_block + t) * 128 + HALO + lane)
            code = jnp.concatenate([code_cols[CH:, t : t + 1], code_cols[: keys - 96, t + 1 : t + 2]], axis=0)
            allowed = in_band & ((code == query_seg) | same)
            masked = jnp.where(allowed, scores[i] * SCALE, -1e30)
            weights = jnp.exp(masked - jnp.max(masked, axis=0, keepdims=True))
            probs.append(weights * (1.0 / jnp.sum(weights, axis=0, keepdims=True)))
        rounded = [p.astype(BF16) for p in probs]
        score_grad = []
        for i in n:
            centre = jnp.sum(probs[i] * prob_grad[i], axis=0, keepdims=True)
            score_grad.append((probs[i] * (prob_grad[i] - centre) * SCALE).astype(BF16))
        value_grad = [plain(rounded[i], g[i]) for i in n]
        key_grad = [plain(score_grad[i], q[i]) for i in n]
        mixed = [cols_by_cols(rounded[i], v[i]).astype(BF16) for i in n]
        query_grad = [cols_by_cols(score_grad[i], k[i]).astype(BF16) for i in n]
        for i in n:
            t = tiles_now[i]
            base = 128 * t
            live = jnp.concatenate([live_cols[HALO:, t : t + 1], live_cols[:HALO, t + 1 : t + 2]], axis=0)
            shown = jnp.where(live == 1.0, mixed[i], jnp.zeros_like(mixed[i]))
            lo, hi = (HALO if t == 0 else 0), (HALO if t == tiles - 1 else 128)
            at = base - HALO
            mixed_ref[at + lo : at + hi, :] = shown[lo:hi]
            grads_ref[at + lo : at + hi, 0:HS] = query_grad[i][lo:hi]
            lo, hi = (96 if t == 0 else 0), (96 if t == tiles - 1 else 128)
            at = base - 96
            for m, grad in enumerate((key_grad[i], value_grad[i])):
                left = carry[m]
                carry[m] = grad[128:]
                if t > 0:
                    grad = jnp.concatenate([grad[:64] + left, grad[64:]], axis=0)
                grads_ref[at + lo : at + hi, (m + 1) * HS : (m + 2) * HS] = grad[lo:hi].astype(BF16)

    attention([0, 1, 2, 3, 4, 5, 6, 7, 8])
    fetches[0].wait()
    input_rows(0, 512)
    input_rows(512, 512)

    fetches[1].wait()
    fetches[2].wait()
    core = shard % 2
    qkv = cols_by_cols(grads_ref[...], normed_ref[...]).astype(BF16)
    out = cols_by_cols(mixed_ref[...], cot_ref[...]).astype(BF16)
    full = jnp.concatenate([qkv, out], axis=0)
    for z in range(8):
        both = full[:, z * 128 : (z + 1) * 128].T
        low, high = both[:64], both[64:]
        keep = jnp.where(core == 0, low, high)
        send = jnp.where(core == 0, high, low)
        for m in range(4):
            keep_ref[z, m] = keep[:, m * HS : (m + 1) * HS]
            send_ref[z, m] = send[:, m * HS : (m + 1) * HS]


def backward(lengths, proj, stats, halo, gain, qkv_weight, out_weight, pad2d, frames, normed, cotangent):
    count, width = frames.shape
    vmem = pl.BlockSpec(memory_space=pltpu.VMEM)
    half = count // 2
    shapes = [(4, half, 128)] * 2 + [(2, half, 128)] * 4 + [(8, 4, width // 16, HS)] * 2
    return pl.pallas_call(
        backward_body,
        in_specs=[pl.BlockSpec(memory_space=pltpu.SMEM)] + [vmem] * 7 + [pl.BlockSpec(memory_space=pl.ANY)] * 3,
        out_specs=[vmem] * len(shapes),
        out_shape=[jax.ShapeDtypeStruct(shape, BF16) for shape in shapes],
        scratch_shapes=[
            pltpu.VMEM((4, count + 4 * HALO, HS), BF16),
            pltpu.VMEM((count, 3 * HS), BF16),
            pltpu.VMEM((count, HS), BF16),
            pltpu.VMEM((width, 3 * HS), BF16),
            pltpu.VMEM((count, width), BF16),
            pltpu.VMEM((count, width), BF16),
            pltpu.VMEM((count, width), BF16),
            pltpu.SemaphoreType.DMA((3,)),
        ],
        compiler_params=pltpu.CompilerParams(vmem_limit_bytes=40 << 20),
        name="backward",
    )(lengths, proj, stats, halo, gain, qkv_weight, out_weight, pad2d, frames, normed, cotangent)


def swapped(x, axis, bit):
    return lax.ppermute(x, axis, [(i, i ^ bit) for i in range(lax.axis_size(axis))])


def total(*parts):
    summed = parts[0].astype(F32)
    for part in parts[1:]:
        summed = summed + part.astype(F32)
    return summed


def on_device(frames, norm_gain, qkv_weight, out_weight, cotangent, pad_mask, utt_lengths):
    shards = lax.axis_size("tm")
    up = [(i, i + 1) for i in range(shards - 1)]
    down = [(i + 1, i) for i in range(shards - 1)]
    ends = jnp.stack([frames[-HALO:], cotangent[-HALO:]])
    starts = jnp.stack([frames[:HALO], cotangent[:HALO]])
    halo = jnp.concatenate([lax.ppermute(ends, "tm", up), lax.ppermute(starts, "tm", down)], axis=1)
    gain = norm_gain[None, :]
    pad2d = pad_mask.reshape(-1, 128)
    proj, stats, normed = project(frames, gain, qkv_weight, out_weight, cotangent, pad2d)
    near, across, *ring, keep, send = backward(
        utt_lengths, proj, stats, halo, gain, qkv_weight, out_weight, pad2d, frames, normed, cotangent
    )
    other = swapped(send, "tm", 1)
    across = swapped(across, "mp", 1)
    ring_in = [swapped(ring[k], "mp", 2 * k) for k in (2, 1, 3)]
    chip = total(keep, other).astype(BF16)
    same_core = [[c + 2 * z for z in range(shards // 2)] for c in range(2)]
    weights = lax.all_to_all(chip, "tm", 0, 0, tiled=True, axis_index_groups=same_core)
    (near, across, ring_in), _ = lax.optimization_barrier(((near, across, ring_in), chip))
    col = [total(near[k], across[k]) for k in range(4)]
    col_in = [swapped(col[k].astype(BF16), "mp", 2 * k) for k in (2, 1, 3)]
    ring_in, _ = lax.optimization_barrier((ring_in, [c.astype(BF16) for c in col[1:]]))
    theirs = swapped(total(ring[0][1], *[r[1] for r in ring_in]).astype(BF16), "mp", 1)
    qkv_grad = weights[:, :3].astype(F32).sum(axis=0)
    out_grad = weights[:, 3].astype(F32).sum(axis=0)
    (theirs, col_in), _ = lax.optimization_barrier(((theirs, col_in), (qkv_grad, out_grad)))
    first_half = total(total(ring[0][0], *[r[0] for r in ring_in]), theirs).astype(BF16)
    second_half = total(col[0], *col_in).astype(BF16)
    frame_grad = jnp.concatenate([first_half, second_half], axis=0)
    return frame_grad, qkv_grad, out_grad.T


def solution(mesh):
    placed = (
        P(("batch", "tm"), None),
        P(),
        P(None, None, "mp"),
        P("mp", None),
        P(("batch", "tm"), None),
        P("batch"),
        P("batch"),
    )
    return jax.shard_map(
        on_device,
        mesh=mesh,
        in_specs=placed,
        out_specs=(P(("batch", "tm"), "mp"), P("batch", "tm", "mp"), P(("batch", "mp"), "tm")),
        check_vma=False,
    )
```

```python
import jax
import jax.numpy as jnp
from jax import lax
from jax.experimental import pallas as pl
from jax.experimental.pallas import tpu as pltpu
from jax.sharding import PartitionSpec as P

HS = 128
CH = 32
HALO = 64
EPSILON = 1e-05
SCALE = HS ** (-0.5)
F32 = jnp.float32
BF16 = jnp.bfloat16


def rows_by_rows(left, right):
    return lax.dot_general(left, right, (((1,), (1,)), ((), ())), preferred_element_type=F32)


def cols_by_cols(left, right):
    return lax.dot_general(left, right, (((0,), (0,)), ((), ())), preferred_element_type=F32)


def plain(left, right):
    return jnp.dot(left, right, preferred_element_type=F32)


def normalised(values):
    values = values.astype(F32)
    mean = jnp.mean(values, axis=-1, keepdims=True)
    center = values - mean
    inverse = lax.rsqrt(jnp.mean(center * center, axis=-1, keepdims=True) + EPSILON)
    return center * inverse, inverse, mean


def pad_rows(pad_ref, first, count):
    total = pad_ref.shape[0]
    return [pad_ref[pl.ds(jnp.clip(first + i, 0, total - 1), 1), :] for i in range(count)]


def as_columns(rows):
    height = -(-len(rows) // 8) * 8
    full = jnp.concatenate(rows + [jnp.zeros_like(rows[0])] * (height - len(rows)), axis=0)
    return full.T


def project_body(
    frames_hbm, gain_ref, qkv_hbm, out_hbm, cot_hbm, pad_ref, proj_ref, stats_ref, normed_hbm,
    frames_ref, w_scr, out_ref, cot_ref, normed_ref, sems,
):
    count = frames_ref.shape[0]
    rows = count // 2
    halves = [pl.ds(0, rows), pl.ds(rows, rows)]
    moves = [(frames_hbm.at[span], frames_ref.at[span]) for span in halves]
    moves += [(qkv_hbm.at[m], w_scr.at[:, m * HS : (m + 1) * HS]) for m in range(3)]
    moves += [(out_hbm, out_ref), (cot_hbm, cot_ref)]
    moves += [(normed_ref.at[span], normed_hbm.at[span]) for span in halves]
    copies = [pltpu.make_async_copy(source, target, sems.at[i]) for i, (source, target) in enumerate(moves)]
    for i in (0, 2, 3, 4, 1, 5, 6):
        copies[i].start()
    lane = lax.broadcasted_iota(jnp.int32, (rows, 128), 1)

    def norm_rows(half):
        normal_form, inverse, mean = normalised(frames_ref[halves[half], :])
        stats_ref[halves[half], :] = jnp.where(lane == 0, mean, inverse)
        normed = (normal_form * gain_ref[...]).astype(BF16)
        normed_ref[halves[half], :] = normed
        return normed

    def project_rows(half, normed):
        qkv = plain(normed, w_scr[...]).astype(BF16)
        for m in range(3):
            proj_ref[m, halves[half], :] = qkv[:, m * HS : (m + 1) * HS]

    copies[0].wait()
    first = norm_rows(0)
    copies[7].start()
    for i in (2, 3, 4, 1):
        copies[i].wait()
    project_rows(0, first)
    second = norm_rows(1)
    for i in (5, 6):
        copies[i].wait()
    copies[8].start()
    blocks = count // 128
    live = as_columns([r.astype(F32) for r in pad_rows(pad_ref, lax.axis_index("tm") * blocks, blocks)])
    live = jnp.concatenate([live[:, i : i + 1] for i in range(blocks)], axis=0)
    project_rows(1, second)
    grads = rows_by_rows(cot_ref[...], out_ref[...])
    proj_ref[3] = jnp.where(live == 1.0, grads, 0.0).astype(BF16)
    copies[7].wait()
    copies[8].wait()


def project(frames, gain, qkv_weight, out_weight, cotangent, pad2d):
    count, width = frames.shape
    vmem = pl.BlockSpec(memory_space=pltpu.VMEM)
    hbm = pl.BlockSpec(memory_space=pl.ANY)
    return pl.pallas_call(
        project_body,
        in_specs=[hbm, vmem, hbm, hbm, hbm, vmem],
        out_specs=[vmem, vmem, hbm],
        out_shape=[
            jax.ShapeDtypeStruct((4, count, HS), BF16),
            jax.ShapeDtypeStruct((count, 128), F32),
            jax.ShapeDtypeStruct((count, width), BF16),
        ],
        scratch_shapes=[
            pltpu.VMEM((count, width), BF16),
            pltpu.VMEM((width, 3 * HS), BF16),
            pltpu.VMEM(out_weight.shape, BF16),
            pltpu.VMEM((count, width), BF16),
            pltpu.VMEM((count, width), BF16),
            pltpu.SemaphoreType.DMA((9,)),
        ],
        compiler_params=pltpu.CompilerParams(vmem_limit_bytes=48 << 20),
        name="project",
    )(frames, gain, qkv_weight, out_weight, cotangent, pad2d)


def backward_body(
    len_ref, proj_ref, stats_ref, halo_ref, gain_ref, qkv_ref, out_ref, pad_ref, frames_hbm, normed_hbm, cot_hbm,
    near_ref, across_ref, ring0_ref, ring1_ref, ring2_ref, ring3_ref, keep_ref, send_ref,
    x_scr, grads_ref, mixed_ref, w_scr, frames_ref, normed_ref, cot_ref, sems,
):
    fetches = [
        pltpu.make_async_copy(source, target, sems.at[i])
        for i, (source, target) in enumerate(
            [(frames_hbm, frames_ref), (normed_hbm, normed_ref), (cot_hbm, cot_ref)]
        )
    ]
    for fetch in fetches:
        fetch.start()
    count = proj_ref.shape[1]
    tiles = count // 128 + 1
    shard = lax.axis_index("tm")
    first_block = shard * (count // 128) - 1
    normal_form, _, _ = normalised(halo_ref[0])
    normed = (normal_form * gain_ref[...]).astype(BF16)
    blocks = tiles + 1
    live_rows = [r.astype(F32) for r in pad_rows(pad_ref, first_block, blocks)]
    live_cols = as_columns(live_rows)
    halo_live = jnp.concatenate([live_cols[HALO:, 0:1], live_cols[:HALO, blocks - 1 : blocks]], axis=0)
    zeros = jnp.zeros((HALO, HS), BF16)
    for m in range(4):
        if m < 3:
            part = plain(normed, qkv_ref[m])
        else:
            part = jnp.where(halo_live == 1.0, rows_by_rows(halo_ref[1], out_ref[...]), 0.0)
        part = part.astype(BF16)
        x_scr[m, 0:HALO, :] = zeros
        x_scr[m, HALO : 2 * HALO, :] = part[:HALO]
        x_scr[m, 2 * HALO : 2 * HALO + count, :] = proj_ref[m]
        x_scr[m, 2 * HALO + count : 3 * HALO + count, :] = part[HALO:]
        x_scr[m, 3 * HALO + count :, :] = zeros

    ends = []
    total = 0
    for u in range(len_ref.shape[0]):
        total = total + len_ref[u]
        ends.append(total)

    def segment(positions):
        found = jnp.zeros(positions.shape, jnp.int32)
        for end in ends:
            found = found + jnp.where(positions >= end, 1, 0)
        return found.astype(F32)

    lane = lax.broadcasted_iota(jnp.int32, (1, 128), 1)
    codes = []
    for b in range(blocks):
        at = (first_block + b) * 128 + lane
        codes.append(jnp.where((live_rows[b] == 1.0) & (at >= 0), segment(at), -1.0))
    code_cols = as_columns(codes)

    keys = 192
    key_at = lax.broadcasted_iota(jnp.int32, (keys, 128), 0)
    query_at = lax.broadcasted_iota(jnp.int32, (keys, 128), 1)
    apart = key_at // CH - query_at // CH
    in_band = (apart >= 0) & (apart <= 2)
    same = key_at == query_at + CH

    place = lax.axis_index("mp")
    owners = [jnp.bitwise_xor(place, j) for j in range(8)]
    spans = [pl.ds(pl.multiple_of(owner * 128, 128), 128) for owner in owners]
    for m in range(3):
        for j, span in enumerate(spans):
            w_scr[j * 128 : (j + 1) * 128, m * HS : (m + 1) * HS] = qkv_ref[m, span, :]
    gain = jnp.concatenate([gain_ref[:, span] for span in spans], axis=1)
    ring_refs = (ring0_ref, ring1_ref, ring2_ref, ring3_ref)

    def input_rows(at, rows):
        incoming = rows_by_rows(grads_ref[at : at + rows, :], w_scr[...])
        frames = jnp.concatenate([frames_ref[at : at + rows, span] for span in spans], axis=1)
        center = frames.astype(F32) - stats_ref[at : at + rows, 0:1]
        inverse = stats_ref[at : at + rows, 1:2]
        scaled = incoming * gain
        mean_grad = jnp.mean(scaled, axis=-1, keepdims=True)
        slope = jnp.mean(scaled * center, axis=-1, keepdims=True) * (inverse * inverse)
        result = (inverse * (scaled - mean_grad - center * slope)).astype(BF16)
        to = at % (count // 2)
        for j in range(8):
            part = result[:, j * 128 : (j + 1) * 128]
            if at < count // 2:
                ring_refs[j // 2][j % 2, to : to + rows, :] = part
            else:
                (near_ref, across_ref)[j % 2][j // 2, to : to + rows, :] = part

    carry = [None, None]

    def attention(tiles_now):
        q = [x_scr[0, 128 * t + HALO : 128 * t + HALO + 128, :] for t in tiles_now]
        g = [x_scr[3, 128 * t + HALO : 128 * t + HALO + 128, :] for t in tiles_now]
        k = [x_scr[1, 128 * t + CH : 128 * t + CH + keys, :] for t in tiles_now]
        v = [x_scr[2, 128 * t + CH : 128 * t + CH + keys, :] for t in tiles_now]
        n = range(len(tiles_now))
        scores = [rows_by_rows(k[i], q[i]) for i in n]
        prob_grad = [rows_by_rows(v[i], g[i]) for i in n]
        probs = []
        for i in n:
            t = tiles_now[i]
            query_seg = segment((first_block + t) * 128 + HALO + lane)
            code = jnp.concatenate([code_cols[CH:, t : t + 1], code_cols[: keys - 96, t + 1 : t + 2]], axis=0)
            allowed = in_band & ((code == query_seg) | same)
            masked = jnp.where(allowed, scores[i] * SCALE, -1e30)
            weights = jnp.exp(masked - jnp.max(masked, axis=0, keepdims=True))
            probs.append(weights * (1.0 / jnp.sum(weights, axis=0, keepdims=True)))
        rounded = [p.astype(BF16) for p in probs]
        score_grad = []
        for i in n:
            centre = jnp.sum(probs[i] * prob_grad[i], axis=0, keepdims=True)
            score_grad.append((probs[i] * (prob_grad[i] - centre) * SCALE).astype(BF16))
        value_grad = [plain(rounded[i], g[i]) for i in n]
        key_grad = [plain(score_grad[i], q[i]) for i in n]
        mixed = [cols_by_cols(rounded[i], v[i]).astype(BF16) for i in n]
        query_grad = [cols_by_cols(score_grad[i], k[i]).astype(BF16) for i in n]
        for i in n:
            t = tiles_now[i]
            base = 128 * t
            live = jnp.concatenate([live_cols[HALO:, t : t + 1], live_cols[:HALO, t + 1 : t + 2]], axis=0)
            shown = jnp.where(live == 1.0, mixed[i], jnp.zeros_like(mixed[i]))
            lo, hi = (HALO if t == 0 else 0), (HALO if t == tiles - 1 else 128)
            at = base - HALO
            mixed_ref[at + lo : at + hi, :] = shown[lo:hi]
            grads_ref[at + lo : at + hi, 0:HS] = query_grad[i][lo:hi]
            lo, hi = (96 if t == 0 else 0), (96 if t == tiles - 1 else 128)
            at = base - 96
            for m, grad in enumerate((key_grad[i], value_grad[i])):
                left = carry[m]
                carry[m] = grad[128:]
                if t > 0:
                    grad = jnp.concatenate([grad[:64] + left, grad[64:]], axis=0)
                grads_ref[at + lo : at + hi, (m + 1) * HS : (m + 2) * HS] = grad[lo:hi].astype(BF16)

    attention([0, 1, 2, 3, 4, 5, 6, 7, 8])
    fetches[0].wait()
    input_rows(0, 512)
    input_rows(512, 512)

    fetches[1].wait()
    fetches[2].wait()
    core = shard % 2
    qkv = cols_by_cols(grads_ref[...], normed_ref[...]).astype(BF16)
    out = cols_by_cols(mixed_ref[...], cot_ref[...]).astype(BF16)
    full = jnp.concatenate([qkv, out], axis=0)
    for z in range(8):
        both = full[:, z * 128 : (z + 1) * 128].T
        low, high = both[:64], both[64:]
        keep = jnp.where(core == 0, low, high)
        send = jnp.where(core == 0, high, low)
        for m in range(4):
            keep_ref[z, m] = keep[:, m * HS : (m + 1) * HS]
            send_ref[z, m] = send[:, m * HS : (m + 1) * HS]


def backward(lengths, proj, stats, halo, gain, qkv_weight, out_weight, pad2d, frames, normed, cotangent):
    count, width = frames.shape
    vmem = pl.BlockSpec(memory_space=pltpu.VMEM)
    half = count // 2
    shapes = [(4, half, 128)] * 2 + [(2, half, 128)] * 4 + [(8, 4, width // 16, HS)] * 2
    return pl.pallas_call(
        backward_body,
        in_specs=[pl.BlockSpec(memory_space=pltpu.SMEM)] + [vmem] * 7 + [pl.BlockSpec(memory_space=pl.ANY)] * 3,
        out_specs=[vmem] * len(shapes),
        out_shape=[jax.ShapeDtypeStruct(shape, BF16) for shape in shapes],
        scratch_shapes=[
            pltpu.VMEM((4, count + 4 * HALO, HS), BF16),
            pltpu.VMEM((count, 3 * HS), BF16),
            pltpu.VMEM((count, HS), BF16),
            pltpu.VMEM((width, 3 * HS), BF16),
            pltpu.VMEM((count, width), BF16),
            pltpu.VMEM((count, width), BF16),
            pltpu.VMEM((count, width), BF16),
            pltpu.SemaphoreType.DMA((3,)),
        ],
        compiler_params=pltpu.CompilerParams(vmem_limit_bytes=40 << 20),
        name="backward",
    )(lengths, proj, stats, halo, gain, qkv_weight, out_weight, pad2d, frames, normed, cotangent)


def swapped(x, axis, bit):
    return lax.ppermute(x, axis, [(i, i ^ bit) for i in range(lax.axis_size(axis))])


def total(*parts):
    summed = parts[0].astype(F32)
    for part in parts[1:]:
        summed = summed + part.astype(F32)
    return summed


def on_device(frames, norm_gain, qkv_weight, out_weight, cotangent, pad_mask, utt_lengths):
    shards = lax.axis_size("tm")
    up = [(i, i + 1) for i in range(shards - 1)]
    down = [(i + 1, i) for i in range(shards - 1)]
    ends = jnp.stack([frames[-HALO:], cotangent[-HALO:]])
    starts = jnp.stack([frames[:HALO], cotangent[:HALO]])
    halo = jnp.concatenate([lax.ppermute(ends, "tm", up), lax.ppermute(starts, "tm", down)], axis=1)
    gain = norm_gain[None, :]
    pad2d = pad_mask.reshape(-1, 128)
    proj, stats, normed = project(frames, gain, qkv_weight, out_weight, cotangent, pad2d)
    near, across, *ring, keep, send = backward(
        utt_lengths, proj, stats, halo, gain, qkv_weight, out_weight, pad2d, frames, normed, cotangent
    )
    other = swapped(send, "tm", 1)
    across = swapped(across, "mp", 1)
    ring_in = [swapped(ring[k], "mp", 2 * k) for k in (2, 1, 3)]
    chip = total(keep, other).astype(BF16)
    same_core = [[c + 2 * z for z in range(shards // 2)] for c in range(2)]
    weights = lax.all_to_all(chip, "tm", 0, 0, tiled=True, axis_index_groups=same_core)
    (near, across, ring_in), _ = lax.optimization_barrier(((near, across, ring_in), chip))
    col = [total(near[k], across[k]) for k in range(4)]
    col_in = [swapped(col[k].astype(BF16), "mp", 2 * k) for k in (2, 1, 3)]
    ring_in, _ = lax.optimization_barrier((ring_in, [c.astype(BF16) for c in col[1:]]))
    theirs = swapped(total(ring[0][1], *[r[1] for r in ring_in]).astype(BF16), "mp", 1)
    qkv_grad = weights[:, :3].astype(F32).sum(axis=0)
    out_grad = weights[:, 3].astype(F32).sum(axis=0)
    first_half = total(total(ring[0][0], *[r[0] for r in ring_in]), theirs).astype(BF16)
    second_half = total(col[0], *col_in).astype(BF16)
    frame_grad = jnp.concatenate([first_half, second_half], axis=0)
    return frame_grad, qkv_grad, out_grad.T


def solution(mesh):
    placed = (
        P(("batch", "tm"), None),
        P(),
        P(None, None, "mp"),
        P("mp", None),
        P(("batch", "tm"), None),
        P("batch"),
        P("batch"),
    )
    return jax.shard_map(
        on_device,
        mesh=mesh,
        in_specs=placed,
        out_specs=(P(("batch", "tm"), "mp"), P("batch", "tm", "mp"), P(("batch", "mp"), "tm")),
        check_vma=False,
    )
```

```python
import jax
import jax.numpy as jnp
from jax import lax
from jax.experimental import pallas as pl
from jax.experimental.pallas import tpu as pltpu
from jax.sharding import PartitionSpec as P

HS = 128
CH = 32
HALO = 64
EPSILON = 1e-05
SCALE = HS ** (-0.5)
F32 = jnp.float32
BF16 = jnp.bfloat16


def rows_by_rows(left, right):
    return lax.dot_general(left, right, (((1,), (1,)), ((), ())), preferred_element_type=F32)


def cols_by_cols(left, right):
    return lax.dot_general(left, right, (((0,), (0,)), ((), ())), preferred_element_type=F32)


def plain(left, right):
    return jnp.dot(left, right, preferred_element_type=F32)


def normalised(values):
    values = values.astype(F32)
    mean = jnp.mean(values, axis=-1, keepdims=True)
    center = values - mean
    inverse = lax.rsqrt(jnp.mean(center * center, axis=-1, keepdims=True) + EPSILON)
    return center * inverse, inverse, mean


def pad_rows(pad_ref, first, count):
    total = pad_ref.shape[0]
    return [pad_ref[pl.ds(jnp.clip(first + i, 0, total - 1), 1), :] for i in range(count)]


def as_columns(rows):
    height = -(-len(rows) // 8) * 8
    full = jnp.concatenate(rows + [jnp.zeros_like(rows[0])] * (height - len(rows)), axis=0)
    return full.T


def project_body(
    frames_hbm, gain_ref, qkv_hbm, out_hbm, cot_hbm, pad_ref, proj_ref, stats_ref, normed_hbm,
    frames_ref, w_scr, out_ref, cot_ref, normed_ref, sems,
):
    count = frames_ref.shape[0]
    rows = count // 2
    halves = [pl.ds(0, rows), pl.ds(rows, rows)]
    moves = [(frames_hbm.at[span], frames_ref.at[span]) for span in halves]
    moves += [(qkv_hbm.at[m], w_scr.at[:, m * HS : (m + 1) * HS]) for m in range(3)]
    moves += [(out_hbm, out_ref), (cot_hbm, cot_ref)]
    moves += [(normed_ref.at[span], normed_hbm.at[span]) for span in halves]
    copies = [pltpu.make_async_copy(source, target, sems.at[i]) for i, (source, target) in enumerate(moves)]
    for i in (0, 2, 3, 4, 1, 5, 6):
        copies[i].start()
    lane = lax.broadcasted_iota(jnp.int32, (rows, 128), 1)

    def norm_rows(half):
        normal_form, inverse, mean = normalised(frames_ref[halves[half], :])
        stats_ref[halves[half], :] = jnp.where(lane == 0, mean, inverse)
        normed = (normal_form * gain_ref[...]).astype(BF16)
        normed_ref[halves[half], :] = normed
        return normed

    def project_rows(half, normed):
        qkv = plain(normed, w_scr[...]).astype(BF16)
        for m in range(3):
            proj_ref[m, halves[half], :] = qkv[:, m * HS : (m + 1) * HS]

    copies[0].wait()
    first = norm_rows(0)
    copies[7].start()
    for i in (2, 3, 4, 1):
        copies[i].wait()
    project_rows(0, first)
    second = norm_rows(1)
    for i in (5, 6):
        copies[i].wait()
    copies[8].start()
    blocks = count // 128
    live = as_columns([r.astype(F32) for r in pad_rows(pad_ref, lax.axis_index("tm") * blocks, blocks)])
    live = jnp.concatenate([live[:, i : i + 1] for i in range(blocks)], axis=0)
    project_rows(1, second)
    grads = rows_by_rows(cot_ref[...], out_ref[...])
    proj_ref[3] = jnp.where(live == 1.0, grads, 0.0).astype(BF16)
    copies[7].wait()
    copies[8].wait()


def project(frames, gain, qkv_weight, out_weight, cotangent, pad2d):
    count, width = frames.shape
    vmem = pl.BlockSpec(memory_space=pltpu.VMEM)
    hbm = pl.BlockSpec(memory_space=pl.ANY)
    return pl.pallas_call(
        project_body,
        in_specs=[hbm, vmem, hbm, hbm, hbm, vmem],
        out_specs=[vmem, vmem, hbm],
        out_shape=[
            jax.ShapeDtypeStruct((4, count, HS), BF16),
            jax.ShapeDtypeStruct((count, 128), F32),
            jax.ShapeDtypeStruct((count, width), BF16),
        ],
        scratch_shapes=[
            pltpu.VMEM((count, width), BF16),
            pltpu.VMEM((width, 3 * HS), BF16),
            pltpu.VMEM(out_weight.shape, BF16),
            pltpu.VMEM((count, width), BF16),
            pltpu.VMEM((count, width), BF16),
            pltpu.SemaphoreType.DMA((9,)),
        ],
        compiler_params=pltpu.CompilerParams(vmem_limit_bytes=48 << 20),
        name="project",
    )(frames, gain, qkv_weight, out_weight, cotangent, pad2d)


def backward_body(
    len_ref, proj_ref, stats_ref, halo_ref, gain_ref, qkv_ref, out_ref, pad_ref, frames_hbm, normed_hbm, cot_hbm,
    near_ref, across_ref, ring0_ref, ring1_ref, ring2_ref, ring3_ref, keep_ref, send_ref,
    x_scr, grads_ref, mixed_ref, w_scr, frames_ref, normed_ref, cot_ref, sems,
):
    fetches = [
        pltpu.make_async_copy(source, target, sems.at[i])
        for i, (source, target) in enumerate(
            [(frames_hbm, frames_ref), (normed_hbm, normed_ref), (cot_hbm, cot_ref)]
        )
    ]
    for fetch in fetches:
        fetch.start()
    count = proj_ref.shape[1]
    tiles = count // 128 + 1
    shard = lax.axis_index("tm")
    first_block = shard * (count // 128) - 1
    normal_form, _, _ = normalised(halo_ref[0])
    normed = (normal_form * gain_ref[...]).astype(BF16)
    blocks = tiles + 1
    live_rows = [r.astype(F32) for r in pad_rows(pad_ref, first_block, blocks)]
    live_cols = as_columns(live_rows)
    halo_live = jnp.concatenate([live_cols[HALO:, 0:1], live_cols[:HALO, blocks - 1 : blocks]], axis=0)
    zeros = jnp.zeros((HALO, HS), BF16)
    for m in range(4):
        if m < 3:
            part = plain(normed, qkv_ref[m])
        else:
            part = jnp.where(halo_live == 1.0, rows_by_rows(halo_ref[1], out_ref[...]), 0.0)
        part = part.astype(BF16)
        x_scr[m, 0:HALO, :] = zeros
        x_scr[m, HALO : 2 * HALO, :] = part[:HALO]
        x_scr[m, 2 * HALO : 2 * HALO + count, :] = proj_ref[m]
        x_scr[m, 2 * HALO + count : 3 * HALO + count, :] = part[HALO:]
        x_scr[m, 3 * HALO + count :, :] = zeros

    ends = []
    total = 0
    for u in range(len_ref.shape[0]):
        total = total + len_ref[u]
        ends.append(total)

    def segment(positions):
        found = jnp.zeros(positions.shape, jnp.int32)
        for end in ends:
            found = found + jnp.where(positions >= end, 1, 0)
        return found.astype(F32)

    lane = lax.broadcasted_iota(jnp.int32, (1, 128), 1)
    codes = []
    for b in range(blocks):
        at = (first_block + b) * 128 + lane
        codes.append(jnp.where((live_rows[b] == 1.0) & (at >= 0), segment(at), -1.0))
    code_cols = as_columns(codes)

    keys = 192
    key_at = lax.broadcasted_iota(jnp.int32, (keys, 128), 0)
    query_at = lax.broadcasted_iota(jnp.int32, (keys, 128), 1)
    apart = key_at // CH - query_at // CH
    in_band = (apart >= 0) & (apart <= 2)
    same = key_at == query_at + CH

    place = lax.axis_index("mp")
    owners = [jnp.bitwise_xor(place, j) for j in range(8)]
    spans = [pl.ds(pl.multiple_of(owner * 128, 128), 128) for owner in owners]
    for m in range(3):
        for j, span in enumerate(spans):
            w_scr[j * 128 : (j + 1) * 128, m * HS : (m + 1) * HS] = qkv_ref[m, span, :]
    gain = jnp.concatenate([gain_ref[:, span] for span in spans], axis=1)
    ring_refs = (ring0_ref, ring1_ref, ring2_ref, ring3_ref)

    def input_rows(at, rows):
        incoming = rows_by_rows(grads_ref[at : at + rows, :], w_scr[...])
        frames = jnp.concatenate([frames_ref[at : at + rows, span] for span in spans], axis=1)
        center = frames.astype(F32) - stats_ref[at : at + rows, 0:1]
        inverse = stats_ref[at : at + rows, 1:2]
        scaled = incoming * gain
        mean_grad = jnp.mean(scaled, axis=-1, keepdims=True)
        slope = jnp.mean(scaled * center, axis=-1, keepdims=True) * (inverse * inverse)
        result = (inverse * (scaled - mean_grad - center * slope)).astype(BF16)
        split = ring0_ref.shape[1]
        for j in range(8):
            part = result[:, j * 128 : (j + 1) * 128]
            if at < split:
                ring_refs[j // 2][j % 2, at : at + rows, :] = part
            else:
                (near_ref, across_ref)[j % 2][j // 2, at - split : at - split + rows, :] = part

    carry = [None, None]

    def attention(tiles_now):
        q = [x_scr[0, 128 * t + HALO : 128 * t + HALO + 128, :] for t in tiles_now]
        g = [x_scr[3, 128 * t + HALO : 128 * t + HALO + 128, :] for t in tiles_now]
        k = [x_scr[1, 128 * t + CH : 128 * t + CH + keys, :] for t in tiles_now]
        v = [x_scr[2, 128 * t + CH : 128 * t + CH + keys, :] for t in tiles_now]
        n = range(len(tiles_now))
        scores = [rows_by_rows(k[i], q[i]) for i in n]
        prob_grad = [rows_by_rows(v[i], g[i]) for i in n]
        probs = []
        for i in n:
            t = tiles_now[i]
            query_seg = segment((first_block + t) * 128 + HALO + lane)
            code = jnp.concatenate([code_cols[CH:, t : t + 1], code_cols[: keys - 96, t + 1 : t + 2]], axis=0)
            allowed = in_band & ((code == query_seg) | same)
            masked = jnp.where(allowed, scores[i] * SCALE, -1e30)
            weights = jnp.exp(masked - jnp.max(masked, axis=0, keepdims=True))
            probs.append(weights * (1.0 / jnp.sum(weights, axis=0, keepdims=True)))
        rounded = [p.astype(BF16) for p in probs]
        score_grad = []
        for i in n:
            centre = jnp.sum(probs[i] * prob_grad[i], axis=0, keepdims=True)
            score_grad.append((probs[i] * (prob_grad[i] - centre) * SCALE).astype(BF16))
        value_grad = [plain(rounded[i], g[i]) for i in n]
        key_grad = [plain(score_grad[i], q[i]) for i in n]
        mixed = [cols_by_cols(rounded[i], v[i]).astype(BF16) for i in n]
        query_grad = [cols_by_cols(score_grad[i], k[i]).astype(BF16) for i in n]
        for i in n:
            t = tiles_now[i]
            base = 128 * t
            live = jnp.concatenate([live_cols[HALO:, t : t + 1], live_cols[:HALO, t + 1 : t + 2]], axis=0)
            shown = jnp.where(live == 1.0, mixed[i], jnp.zeros_like(mixed[i]))
            lo, hi = (HALO if t == 0 else 0), (HALO if t == tiles - 1 else 128)
            at = base - HALO
            mixed_ref[at + lo : at + hi, :] = shown[lo:hi]
            grads_ref[at + lo : at + hi, 0:HS] = query_grad[i][lo:hi]
            lo, hi = (96 if t == 0 else 0), (96 if t == tiles - 1 else 128)
            at = base - 96
            for m, grad in enumerate((key_grad[i], value_grad[i])):
                left = carry[m]
                carry[m] = grad[128:]
                if t > 0:
                    grad = jnp.concatenate([grad[:64] + left, grad[64:]], axis=0)
                grads_ref[at + lo : at + hi, (m + 1) * HS : (m + 2) * HS] = grad[lo:hi].astype(BF16)

    attention([0, 1, 2, 3, 4, 5, 6, 7, 8])
    fetches[0].wait()
    input_rows(0, ring0_ref.shape[1])
    input_rows(ring0_ref.shape[1], near_ref.shape[1])

    fetches[1].wait()
    fetches[2].wait()
    core, zl = shard % 2, (shard // 2) % 2
    qkv = cols_by_cols(grads_ref[...], normed_ref[...]).astype(BF16)
    out = cols_by_cols(mixed_ref[...], cot_ref[...]).astype(BF16)
    full = jnp.concatenate([qkv, out], axis=0)
    for z in range(8):
        both = full[:, z * 128 : (z + 1) * 128].T
        low, high = both[:64], both[64:]
        keep = jnp.where(core == 0, low, high)
        send = jnp.where(core == 0, high, low)
        side = jnp.bitwise_xor(zl, z % 2)
        for m in range(4):
            keep_ref[side, z // 2, m] = keep[:, m * HS : (m + 1) * HS]
            send_ref[side, z // 2, m] = send[:, m * HS : (m + 1) * HS]


def backward(lengths, proj, stats, halo, gain, qkv_weight, out_weight, pad2d, frames, normed, cotangent):
    count, width = frames.shape
    vmem = pl.BlockSpec(memory_space=pltpu.VMEM)
    split = count * 3 // 8
    shapes = [(4, count - split, 128)] * 2 + [(2, split, 128)] * 4 + [(2, 4, 4, width // 16, HS)] * 2
    return pl.pallas_call(
        backward_body,
        in_specs=[pl.BlockSpec(memory_space=pltpu.SMEM)] + [vmem] * 7 + [pl.BlockSpec(memory_space=pl.ANY)] * 3,
        out_specs=[vmem] * len(shapes),
        out_shape=[jax.ShapeDtypeStruct(shape, BF16) for shape in shapes],
        scratch_shapes=[
            pltpu.VMEM((4, count + 4 * HALO, HS), BF16),
            pltpu.VMEM((count, 3 * HS), BF16),
            pltpu.VMEM((count, HS), BF16),
            pltpu.VMEM((width, 3 * HS), BF16),
            pltpu.VMEM((count, width), BF16),
            pltpu.VMEM((count, width), BF16),
            pltpu.VMEM((count, width), BF16),
            pltpu.SemaphoreType.DMA((3,)),
        ],
        compiler_params=pltpu.CompilerParams(vmem_limit_bytes=40 << 20),
        name="backward",
    )(lengths, proj, stats, halo, gain, qkv_weight, out_weight, pad2d, frames, normed, cotangent)


def swapped(x, axis, bit):
    return lax.ppermute(x, axis, [(i, i ^ bit) for i in range(lax.axis_size(axis))])


def total(*parts):
    summed = parts[0].astype(F32)
    for part in parts[1:]:
        summed = summed + part.astype(F32)
    return summed


def on_device(frames, norm_gain, qkv_weight, out_weight, cotangent, pad_mask, utt_lengths):
    shards = lax.axis_size("tm")
    up = [(i, i + 1) for i in range(shards - 1)]
    down = [(i + 1, i) for i in range(shards - 1)]
    ends = jnp.stack([frames[-HALO:], cotangent[-HALO:]])
    starts = jnp.stack([frames[:HALO], cotangent[:HALO]])
    halo = jnp.concatenate([lax.ppermute(ends, "tm", up), lax.ppermute(starts, "tm", down)], axis=1)
    gain = norm_gain[None, :]
    pad2d = pad_mask.reshape(-1, 128)
    proj, stats, normed = project(frames, gain, qkv_weight, out_weight, cotangent, pad2d)
    near, across, *ring, keep, send = backward(
        utt_lengths, proj, stats, halo, gain, qkv_weight, out_weight, pad2d, frames, normed, cotangent
    )
    other = swapped(send, "tm", 1)
    across = swapped(across, "mp", 1)
    ring_in = [swapped(ring[k], "mp", 2 * k) for k in (2, 1, 3)]
    stay, cross = total(keep[0], other[0]).astype(BF16), total(keep[1], other[1]).astype(BF16)
    pair = total(stay, swapped(cross, "tm", 2)).astype(BF16)
    groups = [[c + 4 * z for z in range(shards // 4)] for c in range(4)]
    weights = lax.all_to_all(pair, "tm", 0, 0, tiled=True, axis_index_groups=groups)
    (near, across, ring_in), _ = lax.optimization_barrier(((near, across, ring_in), pair))
    col = [total(near[k], across[k]) for k in range(4)]
    col_in = [swapped(col[k].astype(BF16), "mp", 2 * k) for k in (2, 1, 3)]
    ring_in, _ = lax.optimization_barrier((ring_in, [c.astype(BF16) for c in col[1:]]))
    theirs = swapped(total(ring[0][1], *[r[1] for r in ring_in]).astype(BF16), "mp", 1)
    first_half = total(total(ring[0][0], *[r[0] for r in ring_in]), theirs).astype(BF16)
    weights, _ = lax.optimization_barrier((weights, first_half))
    qkv_grad = weights[:, :3].astype(F32).sum(axis=0)
    out_grad = weights[:, 3].astype(F32).sum(axis=0)
    col_in, _ = lax.optimization_barrier((col_in, (qkv_grad, out_grad)))
    second_half = total(col[0], *col_in).astype(BF16)
    frame_grad = jnp.concatenate([first_half, second_half], axis=0)
    return frame_grad, qkv_grad, out_grad.T


def solution(mesh):
    placed = (
        P(("batch", "tm"), None),
        P(),
        P(None, None, "mp"),
        P("mp", None),
        P(("batch", "tm"), None),
        P("batch"),
        P("batch"),
    )
    return jax.shard_map(
        on_device,
        mesh=mesh,
        in_specs=placed,
        out_specs=(P(("batch", "tm"), "mp"), P("batch", "tm", "mp"), P(("batch", "mp"), "tm")),
        check_vma=False,
    )
```

```python
import jax
import jax.numpy as jnp
from jax import lax
from jax.experimental import pallas as pl
from jax.experimental.pallas import tpu as pltpu
from jax.sharding import PartitionSpec as P

HS = 128
CH = 32
HALO = 64
EPSILON = 1e-05
SCALE = HS ** (-0.5)
F32 = jnp.float32
BF16 = jnp.bfloat16


def rows_by_rows(left, right):
    return lax.dot_general(left, right, (((1,), (1,)), ((), ())), preferred_element_type=F32)


def cols_by_cols(left, right):
    return lax.dot_general(left, right, (((0,), (0,)), ((), ())), preferred_element_type=F32)


def plain(left, right):
    return jnp.dot(left, right, preferred_element_type=F32)


def normalised(values):
    values = values.astype(F32)
    mean = jnp.mean(values, axis=-1, keepdims=True)
    center = values - mean
    inverse = lax.rsqrt(jnp.mean(center * center, axis=-1, keepdims=True) + EPSILON)
    return center * inverse, inverse, mean


def pad_rows(pad_ref, first, count):
    total = pad_ref.shape[0]
    return [pad_ref[pl.ds(jnp.clip(first + i, 0, total - 1), 1), :] for i in range(count)]


def as_columns(rows):
    height = -(-len(rows) // 8) * 8
    full = jnp.concatenate(rows + [jnp.zeros_like(rows[0])] * (height - len(rows)), axis=0)
    return full.T


def project_body(
    frames_hbm, gain_ref, qkv_hbm, out_hbm, cot_hbm, pad_ref, proj_ref, stats_ref, normed_hbm,
    frames_ref, w_scr, out_ref, cot_ref, normed_ref, sems,
):
    count = frames_ref.shape[0]
    rows = count // 2
    halves = [pl.ds(0, rows), pl.ds(rows, rows)]
    moves = [(frames_hbm.at[span], frames_ref.at[span]) for span in halves]
    moves += [(qkv_hbm.at[m], w_scr.at[:, m * HS : (m + 1) * HS]) for m in range(3)]
    moves += [(out_hbm, out_ref), (cot_hbm, cot_ref)]
    moves += [(normed_ref.at[span], normed_hbm.at[span]) for span in halves]
    copies = [pltpu.make_async_copy(source, target, sems.at[i]) for i, (source, target) in enumerate(moves)]
    for i in (0, 2, 3, 4, 1, 5, 6):
        copies[i].start()
    lane = lax.broadcasted_iota(jnp.int32, (rows, 128), 1)

    def norm_rows(half):
        normal_form, inverse, mean = normalised(frames_ref[halves[half], :])
        stats_ref[halves[half], :] = jnp.where(lane == 0, mean, inverse)
        normed = (normal_form * gain_ref[...]).astype(BF16)
        normed_ref[halves[half], :] = normed
        return normed

    def project_rows(half, normed):
        qkv = plain(normed, w_scr[...]).astype(BF16)
        for m in range(3):
            proj_ref[m, halves[half], :] = qkv[:, m * HS : (m + 1) * HS]

    copies[0].wait()
    first = norm_rows(0)
    copies[7].start()
    for i in (2, 3, 4, 1):
        copies[i].wait()
    project_rows(0, first)
    second = norm_rows(1)
    for i in (5, 6):
        copies[i].wait()
    copies[8].start()
    blocks = count // 128
    live = as_columns([r.astype(F32) for r in pad_rows(pad_ref, lax.axis_index("tm") * blocks, blocks)])
    live = jnp.concatenate([live[:, i : i + 1] for i in range(blocks)], axis=0)
    project_rows(1, second)
    grads = rows_by_rows(cot_ref[...], out_ref[...])
    proj_ref[3] = jnp.where(live == 1.0, grads, 0.0).astype(BF16)
    copies[7].wait()
    copies[8].wait()


def project(frames, gain, qkv_weight, out_weight, cotangent, pad2d):
    count, width = frames.shape
    vmem = pl.BlockSpec(memory_space=pltpu.VMEM)
    hbm = pl.BlockSpec(memory_space=pl.ANY)
    return pl.pallas_call(
        project_body,
        in_specs=[hbm, vmem, hbm, hbm, hbm, vmem],
        out_specs=[vmem, vmem, hbm],
        out_shape=[
            jax.ShapeDtypeStruct((4, count, HS), BF16),
            jax.ShapeDtypeStruct((count, 128), F32),
            jax.ShapeDtypeStruct((count, width), BF16),
        ],
        scratch_shapes=[
            pltpu.VMEM((count, width), BF16),
            pltpu.VMEM((width, 3 * HS), BF16),
            pltpu.VMEM(out_weight.shape, BF16),
            pltpu.VMEM((count, width), BF16),
            pltpu.VMEM((count, width), BF16),
            pltpu.SemaphoreType.DMA((9,)),
        ],
        compiler_params=pltpu.CompilerParams(vmem_limit_bytes=48 << 20),
        name="project",
    )(frames, gain, qkv_weight, out_weight, cotangent, pad2d)


def backward_body(
    len_ref, proj_ref, stats_ref, halo_ref, gain_ref, qkv_ref, out_ref, pad_ref, frames_hbm, normed_hbm, cot_hbm,
    near_ref, across_ref, ring0_ref, ring1_ref, ring2_ref, ring3_ref, keep_ref, send_ref,
    x_scr, grads_ref, mixed_ref, w_scr, frames_ref, normed_ref, cot_ref, sems,
):
    fetches = [
        pltpu.make_async_copy(source, target, sems.at[i])
        for i, (source, target) in enumerate(
            [(frames_hbm, frames_ref), (normed_hbm, normed_ref), (cot_hbm, cot_ref)]
        )
    ]
    for fetch in fetches:
        fetch.start()
    count = proj_ref.shape[1]
    tiles = count // 128 + 1
    shard = lax.axis_index("tm")
    first_block = shard * (count // 128) - 1
    normal_form, _, _ = normalised(halo_ref[0])
    normed = (normal_form * gain_ref[...]).astype(BF16)
    blocks = tiles + 1
    live_rows = [r.astype(F32) for r in pad_rows(pad_ref, first_block, blocks)]
    live_cols = as_columns(live_rows)
    halo_live = jnp.concatenate([live_cols[HALO:, 0:1], live_cols[:HALO, blocks - 1 : blocks]], axis=0)
    zeros = jnp.zeros((HALO, HS), BF16)
    for m in range(4):
        if m < 3:
            part = plain(normed, qkv_ref[m])
        else:
            part = jnp.where(halo_live == 1.0, rows_by_rows(halo_ref[1], out_ref[...]), 0.0)
        part = part.astype(BF16)
        x_scr[m, 0:HALO, :] = zeros
        x_scr[m, HALO : 2 * HALO, :] = part[:HALO]
        x_scr[m, 2 * HALO : 2 * HALO + count, :] = proj_ref[m]
        x_scr[m, 2 * HALO + count : 3 * HALO + count, :] = part[HALO:]
        x_scr[m, 3 * HALO + count :, :] = zeros

    ends = []
    total = 0
    for u in range(len_ref.shape[0]):
        total = total + len_ref[u]
        ends.append(total)

    def segment(positions):
        found = jnp.zeros(positions.shape, jnp.int32)
        for end in ends:
            found = found + jnp.where(positions >= end, 1, 0)
        return found.astype(F32)

    lane = lax.broadcasted_iota(jnp.int32, (1, 128), 1)
    codes = []
    for b in range(blocks):
        at = (first_block + b) * 128 + lane
        codes.append(jnp.where((live_rows[b] == 1.0) & (at >= 0), segment(at), -1.0))
    code_cols = as_columns(codes)

    keys = 192
    key_at = lax.broadcasted_iota(jnp.int32, (keys, 128), 0)
    query_at = lax.broadcasted_iota(jnp.int32, (keys, 128), 1)
    apart = key_at // CH - query_at // CH
    in_band = (apart >= 0) & (apart <= 2)
    same = key_at == query_at + CH

    place = lax.axis_index("mp")
    owners = [jnp.bitwise_xor(place, j) for j in range(8)]
    spans = [pl.ds(pl.multiple_of(owner * 128, 128), 128) for owner in owners]
    for m in range(3):
        for j, span in enumerate(spans):
            w_scr[j * 128 : (j + 1) * 128, m * HS : (m + 1) * HS] = qkv_ref[m, span, :]
    gain = jnp.concatenate([gain_ref[:, span] for span in spans], axis=1)
    ring_refs = (ring0_ref, ring1_ref, ring2_ref, ring3_ref)

    def input_rows(at, rows):
        incoming = rows_by_rows(grads_ref[at : at + rows, :], w_scr[...])
        frames = jnp.concatenate([frames_ref[at : at + rows, span] for span in spans], axis=1)
        center = frames.astype(F32) - stats_ref[at : at + rows, 0:1]
        inverse = stats_ref[at : at + rows, 1:2]
        scaled = incoming * gain
        mean_grad = jnp.mean(scaled, axis=-1, keepdims=True)
        slope = jnp.mean(scaled * center, axis=-1, keepdims=True) * (inverse * inverse)
        result = (inverse * (scaled - mean_grad - center * slope)).astype(BF16)
        to = at % (count // 2)
        for j in range(8):
            part = result[:, j * 128 : (j + 1) * 128]
            if at < count // 2:
                ring_refs[j // 2][j % 2, to : to + rows, :] = part
            else:
                (near_ref, across_ref)[j % 2][j // 2, to : to + rows, :] = part

    carry = [None, None]

    def attention(tiles_now):
        q = [x_scr[0, 128 * t + HALO : 128 * t + HALO + 128, :] for t in tiles_now]
        g = [x_scr[3, 128 * t + HALO : 128 * t + HALO + 128, :] for t in tiles_now]
        k = [x_scr[1, 128 * t + CH : 128 * t + CH + keys, :] for t in tiles_now]
        v = [x_scr[2, 128 * t + CH : 128 * t + CH + keys, :] for t in tiles_now]
        n = range(len(tiles_now))
        scores = [rows_by_rows(k[i], q[i]) for i in n]
        prob_grad = [rows_by_rows(v[i], g[i]) for i in n]
        probs = []
        for i in n:
            t = tiles_now[i]
            query_seg = segment((first_block + t) * 128 + HALO + lane)
            code = jnp.concatenate([code_cols[CH:, t : t + 1], code_cols[: keys - 96, t + 1 : t + 2]], axis=0)
            allowed = in_band & ((code == query_seg) | same)
            masked = jnp.where(allowed, scores[i] * SCALE, -1e30)
            weights = jnp.exp(masked - jnp.max(masked, axis=0, keepdims=True))
            probs.append(weights * (1.0 / jnp.sum(weights, axis=0, keepdims=True)))
        rounded = [p.astype(BF16) for p in probs]
        score_grad = []
        for i in n:
            centre = jnp.sum(probs[i] * prob_grad[i], axis=0, keepdims=True)
            score_grad.append((probs[i] * (prob_grad[i] - centre) * SCALE).astype(BF16))
        value_grad = [plain(rounded[i], g[i]) for i in n]
        key_grad = [plain(score_grad[i], q[i]) for i in n]
        mixed = [cols_by_cols(rounded[i], v[i]).astype(BF16) for i in n]
        query_grad = [cols_by_cols(score_grad[i], k[i]).astype(BF16) for i in n]
        for i in n:
            t = tiles_now[i]
            base = 128 * t
            live = jnp.concatenate([live_cols[HALO:, t : t + 1], live_cols[:HALO, t + 1 : t + 2]], axis=0)
            shown = jnp.where(live == 1.0, mixed[i], jnp.zeros_like(mixed[i]))
            lo, hi = (HALO if t == 0 else 0), (HALO if t == tiles - 1 else 128)
            at = base - HALO
            mixed_ref[at + lo : at + hi, :] = shown[lo:hi]
            grads_ref[at + lo : at + hi, 0:HS] = query_grad[i][lo:hi]
            lo, hi = (96 if t == 0 else 0), (96 if t == tiles - 1 else 128)
            at = base - 96
            for m, grad in enumerate((key_grad[i], value_grad[i])):
                left = carry[m]
                carry[m] = grad[128:]
                if t > 0:
                    grad = jnp.concatenate([grad[:64] + left, grad[64:]], axis=0)
                grads_ref[at + lo : at + hi, (m + 1) * HS : (m + 2) * HS] = grad[lo:hi].astype(BF16)

    attention([0, 1, 2, 3, 4, 5, 6, 7, 8])
    fetches[0].wait()
    input_rows(0, 512)
    input_rows(512, 512)

    fetches[1].wait()
    fetches[2].wait()
    core, zl = shard % 2, (shard // 2) % 2
    qkv = cols_by_cols(grads_ref[...], normed_ref[...]).astype(BF16)
    out = cols_by_cols(mixed_ref[...], cot_ref[...]).astype(BF16)
    full = jnp.concatenate([qkv, out], axis=0)
    for z in range(8):
        both = full[:, z * 128 : (z + 1) * 128].T
        low, high = both[:64], both[64:]
        keep = jnp.where(core == 0, low, high)
        send = jnp.where(core == 0, high, low)
        side = jnp.bitwise_xor(zl, z % 2)
        for m in range(4):
            keep_ref[side, z // 2, m] = keep[:, m * HS : (m + 1) * HS]
            send_ref[side, z // 2, m] = send[:, m * HS : (m + 1) * HS]


def backward(lengths, proj, stats, halo, gain, qkv_weight, out_weight, pad2d, frames, normed, cotangent):
    count, width = frames.shape
    vmem = pl.BlockSpec(memory_space=pltpu.VMEM)
    half = count // 2
    shapes = [(4, half, 128)] * 2 + [(2, half, 128)] * 4 + [(2, 4, 4, width // 16, HS)] * 2
    return pl.pallas_call(
        backward_body,
        in_specs=[pl.BlockSpec(memory_space=pltpu.SMEM)] + [vmem] * 7 + [pl.BlockSpec(memory_space=pl.ANY)] * 3,
        out_specs=[vmem] * len(shapes),
        out_shape=[jax.ShapeDtypeStruct(shape, BF16) for shape in shapes],
        scratch_shapes=[
            pltpu.VMEM((4, count + 4 * HALO, HS), BF16),
            pltpu.VMEM((count, 3 * HS), BF16),
            pltpu.VMEM((count, HS), BF16),
            pltpu.VMEM((width, 3 * HS), BF16),
            pltpu.VMEM((count, width), BF16),
            pltpu.VMEM((count, width), BF16),
            pltpu.VMEM((count, width), BF16),
            pltpu.SemaphoreType.DMA((3,)),
        ],
        compiler_params=pltpu.CompilerParams(vmem_limit_bytes=40 << 20),
        name="backward",
    )(lengths, proj, stats, halo, gain, qkv_weight, out_weight, pad2d, frames, normed, cotangent)


def swapped(x, axis, bit):
    return lax.ppermute(x, axis, [(i, i ^ bit) for i in range(lax.axis_size(axis))])


def total(*parts):
    summed = parts[0].astype(F32)
    for part in parts[1:]:
        summed = summed + part.astype(F32)
    return summed


def on_device(frames, norm_gain, qkv_weight, out_weight, cotangent, pad_mask, utt_lengths):
    shards = lax.axis_size("tm")
    up = [(i, i + 1) for i in range(shards - 1)]
    down = [(i + 1, i) for i in range(shards - 1)]
    ends = jnp.stack([frames[-HALO:], cotangent[-HALO:]])
    starts = jnp.stack([frames[:HALO], cotangent[:HALO]])
    halo = jnp.concatenate([lax.ppermute(ends, "tm", up), lax.ppermute(starts, "tm", down)], axis=1)
    gain = norm_gain[None, :]
    pad2d = pad_mask.reshape(-1, 128)
    proj, stats, normed = project(frames, gain, qkv_weight, out_weight, cotangent, pad2d)
    near, across, *ring, keep, send = backward(
        utt_lengths, proj, stats, halo, gain, qkv_weight, out_weight, pad2d, frames, normed, cotangent
    )
    other = swapped(send, "tm", 1)
    across = swapped(across, "mp", 1)
    ring_in = [swapped(ring[k], "mp", 2 * k) for k in (2, 1, 3)]
    stay, cross = total(keep[0], other[0]).astype(BF16), total(keep[1], other[1]).astype(BF16)
    pair = total(stay, swapped(cross, "tm", 2)).astype(BF16)
    groups = [[c + 4 * z for z in range(shards // 4)] for c in range(4)]
    weights = lax.all_to_all(pair, "tm", 0, 0, tiled=True, axis_index_groups=groups)
    (near, across, ring_in), _ = lax.optimization_barrier(((near, across, ring_in), pair))
    col = [total(near[k], across[k]) for k in range(4)]
    col_in = [swapped(col[k].astype(BF16), "mp", 2 * k) for k in (2, 1, 3)]
    ring_in, _ = lax.optimization_barrier((ring_in, [c.astype(BF16) for c in col[1:]]))
    both = lax.optimization_barrier(total(ring[0], *ring_in))
    theirs = swapped(both[1].astype(BF16), "mp", 1)
    qkv_grad = weights[:, :3].astype(F32).sum(axis=0)
    out_grad = weights[:, 3].astype(F32).sum(axis=0)
    (theirs, col_in), _ = lax.optimization_barrier(((theirs, col_in), (qkv_grad, out_grad)))
    first_half = total(both[0], theirs).astype(BF16)
    second_half = total(col[0], *col_in).astype(BF16)
    frame_grad = jnp.concatenate([first_half, second_half], axis=0)
    return frame_grad, qkv_grad, out_grad.T


def solution(mesh):
    placed = (
        P(("batch", "tm"), None),
        P(),
        P(None, None, "mp"),
        P("mp", None),
        P(("batch", "tm"), None),
        P("batch"),
        P("batch"),
    )
    return jax.shard_map(
        on_device,
        mesh=mesh,
        in_specs=placed,
        out_specs=(P(("batch", "tm"), "mp"), P("batch", "tm", "mp"), P(("batch", "mp"), "tm")),
        check_vma=False,
    )
```

```python
import jax
import jax.numpy as jnp
from jax import lax
from jax.experimental import pallas as pl
from jax.experimental.pallas import tpu as pltpu
from jax.sharding import PartitionSpec as P

HS = 128
CH = 32
HALO = 64
EPSILON = 1e-05
SCALE = HS ** (-0.5)
F32 = jnp.float32
BF16 = jnp.bfloat16


def rows_by_rows(left, right):
    return lax.dot_general(left, right, (((1,), (1,)), ((), ())), preferred_element_type=F32)


def cols_by_cols(left, right):
    return lax.dot_general(left, right, (((0,), (0,)), ((), ())), preferred_element_type=F32)


def plain(left, right):
    return jnp.dot(left, right, preferred_element_type=F32)


def normalised(values):
    values = values.astype(F32)
    mean = jnp.mean(values, axis=-1, keepdims=True)
    center = values - mean
    inverse = lax.rsqrt(jnp.mean(center * center, axis=-1, keepdims=True) + EPSILON)
    return center * inverse, inverse, mean


def pad_rows(pad_ref, first, count):
    total = pad_ref.shape[0]
    return [pad_ref[pl.ds(jnp.clip(first + i, 0, total - 1), 1), :] for i in range(count)]


def as_columns(rows):
    height = -(-len(rows) // 8) * 8
    full = jnp.concatenate(rows + [jnp.zeros_like(rows[0])] * (height - len(rows)), axis=0)
    return full.T


def project_body(
    frames_hbm, gain_hbm, qkv_hbm, out_hbm, cot_hbm, pad_hbm,
    proj_ref, stats_ref, first_ref, last_ref, normed_hbm,
    frames_ref, w_scr, out_ref, cot_ref, normed_ref, gain_ref, pad_ref, sems,
):
    count = frames_ref.shape[0]
    rows = count // 2
    halves = [pl.ds(0, rows), pl.ds(rows, rows)]
    moves = [(frames_hbm.at[span], frames_ref.at[span]) for span in halves]
    moves += [(qkv_hbm.at[m], w_scr.at[:, m * HS : (m + 1) * HS]) for m in range(3)]
    moves += [(out_hbm, out_ref), (cot_hbm, cot_ref)]
    moves += [(normed_ref.at[span], normed_hbm.at[span]) for span in halves]
    moves += [(gain_hbm, gain_ref), (pad_hbm, pad_ref)]
    copies = [pltpu.make_async_copy(source, target, sems.at[i]) for i, (source, target) in enumerate(moves)]
    for i in (9, 0, 2, 3, 4, 1, 5, 10, 6):
        copies[i].start()
    lane = lax.broadcasted_iota(jnp.int32, (rows, 128), 1)

    def norm_rows(half):
        normal_form, inverse, mean = normalised(frames_ref[halves[half], :])
        stats_ref[halves[half], :] = jnp.where(lane == 0, mean, inverse)
        normed = (normal_form * gain_ref[...]).astype(BF16)
        normed_ref[halves[half], :] = normed
        return normed

    def project_rows(half, normed):
        qkv = plain(normed, w_scr[...]).astype(BF16)
        for m in range(3):
            proj_ref[m, halves[half], :] = qkv[:, m * HS : (m + 1) * HS]

    copies[9].wait()
    copies[0].wait()
    first = norm_rows(0)
    copies[7].start()
    for i in (2, 3, 4, 1):
        copies[i].wait()
    project_rows(0, first)
    second = norm_rows(1)
    for i in (5, 10, 6):
        copies[i].wait()
    copies[8].start()
    blocks = count // 128
    live = as_columns([r.astype(F32) for r in pad_rows(pad_ref, lax.axis_index("tm") * blocks, blocks)])
    live = jnp.concatenate([live[:, i : i + 1] for i in range(blocks)], axis=0)
    project_rows(1, second)
    grads = rows_by_rows(cot_ref[...], out_ref[...])
    proj_ref[3] = jnp.where(live == 1.0, grads, 0.0).astype(BF16)
    first_ref[...] = proj_ref[:, :HALO, :]
    last_ref[...] = proj_ref[:, count - HALO :, :]
    copies[7].wait()
    copies[8].wait()


def project(frames, gain, qkv_weight, out_weight, cotangent, pad2d):
    count, width = frames.shape
    vmem = pl.BlockSpec(memory_space=pltpu.VMEM)
    hbm = pl.BlockSpec(memory_space=pl.ANY)
    return pl.pallas_call(
        project_body,
        in_specs=[hbm] * 6,
        out_specs=[vmem, vmem, vmem, vmem, hbm],
        out_shape=[
            jax.ShapeDtypeStruct((4, count, HS), BF16),
            jax.ShapeDtypeStruct((count, 128), F32),
            jax.ShapeDtypeStruct((4, HALO, HS), BF16),
            jax.ShapeDtypeStruct((4, HALO, HS), BF16),
            jax.ShapeDtypeStruct((count, width), BF16),
        ],
        scratch_shapes=[
            pltpu.VMEM((count, width), BF16),
            pltpu.VMEM((width, 3 * HS), BF16),
            pltpu.VMEM(out_weight.shape, BF16),
            pltpu.VMEM((count, width), BF16),
            pltpu.VMEM((count, width), BF16),
            pltpu.VMEM(gain.shape, F32),
            pltpu.VMEM(pad2d.shape, jnp.int32),
            pltpu.SemaphoreType.DMA((11,)),
        ],
        compiler_params=pltpu.CompilerParams(vmem_limit_bytes=54 << 20),
        name="project",
    )(frames, gain, qkv_weight, out_weight, cotangent, pad2d)


def backward_body(
    len_ref, proj_ref, stats_ref, below_ref, above_ref, gain_ref, qkv_ref, pad_ref, frames_hbm, normed_hbm, cot_hbm,
    near_ref, across_ref, ring0_ref, ring1_ref, ring2_ref, ring3_ref, keep_ref, send_ref,
    x_scr, grads_ref, mixed_ref, w_scr, frames_ref, normed_ref, cot_ref, sems,
):
    fetches = [
        pltpu.make_async_copy(source, target, sems.at[i])
        for i, (source, target) in enumerate(
            [(frames_hbm, frames_ref), (normed_hbm, normed_ref), (cot_hbm, cot_ref)]
        )
    ]
    for fetch in fetches:
        fetch.start()
    count = proj_ref.shape[1]
    tiles = count // 128 + 1
    shard = lax.axis_index("tm")
    first_block = shard * (count // 128) - 1
    blocks = tiles + 1
    live_rows = [r.astype(F32) for r in pad_rows(pad_ref, first_block, blocks)]
    live_cols = as_columns(live_rows)
    zeros = jnp.zeros((HALO, HS), BF16)
    for m in range(4):
        x_scr[m, 0:HALO, :] = zeros
        x_scr[m, HALO : 2 * HALO, :] = below_ref[m]
        x_scr[m, 2 * HALO : 2 * HALO + count, :] = proj_ref[m]
        x_scr[m, 2 * HALO + count : 3 * HALO + count, :] = above_ref[m]
        x_scr[m, 3 * HALO + count :, :] = zeros

    ends = []
    total = 0
    for u in range(len_ref.shape[0]):
        total = total + len_ref[u]
        ends.append(total)

    def segment(positions):
        found = jnp.zeros(positions.shape, jnp.int32)
        for end in ends:
            found = found + jnp.where(positions >= end, 1, 0)
        return found.astype(F32)

    lane = lax.broadcasted_iota(jnp.int32, (1, 128), 1)
    codes = []
    for b in range(blocks):
        at = (first_block + b) * 128 + lane
        codes.append(jnp.where((live_rows[b] == 1.0) & (at >= 0), segment(at), -1.0))
    code_cols = as_columns(codes)

    keys = 192
    key_at = lax.broadcasted_iota(jnp.int32, (keys, 128), 0)
    query_at = lax.broadcasted_iota(jnp.int32, (keys, 128), 1)
    apart = key_at // CH - query_at // CH
    in_band = (apart >= 0) & (apart <= 2)
    same = key_at == query_at + CH

    place = lax.axis_index("mp")
    owners = [jnp.bitwise_xor(place, j) for j in range(8)]
    spans = [pl.ds(pl.multiple_of(owner * 128, 128), 128) for owner in owners]
    for m in range(3):
        for j, span in enumerate(spans):
            w_scr[j * 128 : (j + 1) * 128, m * HS : (m + 1) * HS] = qkv_ref[m, span, :]
    gain = jnp.concatenate([gain_ref[:, span] for span in spans], axis=1)
    ring_refs = (ring0_ref, ring1_ref, ring2_ref, ring3_ref)

    def input_rows(at, rows):
        incoming = rows_by_rows(grads_ref[at : at + rows, :], w_scr[...])
        frames = jnp.concatenate([frames_ref[at : at + rows, span] for span in spans], axis=1)
        center = frames.astype(F32) - stats_ref[at : at + rows, 0:1]
        inverse = stats_ref[at : at + rows, 1:2]
        scaled = incoming * gain
        mean_grad = jnp.mean(scaled, axis=-1, keepdims=True)
        slope = jnp.mean(scaled * center, axis=-1, keepdims=True) * (inverse * inverse)
        result = (inverse * (scaled - mean_grad - center * slope)).astype(BF16)
        to = at % (count // 2)
        for j in range(8):
            part = result[:, j * 128 : (j + 1) * 128]
            if at < count // 2:
                ring_refs[j // 2][j % 2, to : to + rows, :] = part
            else:
                (near_ref, across_ref)[j % 2][j // 2, to : to + rows, :] = part

    carry = [None, None]

    def attention(tiles_now):
        q = [x_scr[0, 128 * t + HALO : 128 * t + HALO + 128, :] for t in tiles_now]
        g = [x_scr[3, 128 * t + HALO : 128 * t + HALO + 128, :] for t in tiles_now]
        k = [x_scr[1, 128 * t + CH : 128 * t + CH + keys, :] for t in tiles_now]
        v = [x_scr[2, 128 * t + CH : 128 * t + CH + keys, :] for t in tiles_now]
        n = range(len(tiles_now))
        scores = [rows_by_rows(k[i], q[i]) for i in n]
        prob_grad = [rows_by_rows(v[i], g[i]) for i in n]
        probs = []
        for i in n:
            t = tiles_now[i]
            query_seg = segment((first_block + t) * 128 + HALO + lane)
            code = jnp.concatenate([code_cols[CH:, t : t + 1], code_cols[: keys - 96, t + 1 : t + 2]], axis=0)
            allowed = in_band & ((code == query_seg) | same)
            masked = jnp.where(allowed, scores[i] * SCALE, -1e30)
            weights = jnp.exp(masked - jnp.max(masked, axis=0, keepdims=True))
            probs.append(weights * (1.0 / jnp.sum(weights, axis=0, keepdims=True)))
        rounded = [p.astype(BF16) for p in probs]
        score_grad = []
        for i in n:
            centre = jnp.sum(probs[i] * prob_grad[i], axis=0, keepdims=True)
            score_grad.append((probs[i] * (prob_grad[i] - centre) * SCALE).astype(BF16))
        value_grad = [plain(rounded[i], g[i]) for i in n]
        key_grad = [plain(score_grad[i], q[i]) for i in n]
        mixed = [cols_by_cols(rounded[i], v[i]).astype(BF16) for i in n]
        query_grad = [cols_by_cols(score_grad[i], k[i]).astype(BF16) for i in n]
        for i in n:
            t = tiles_now[i]
            base = 128 * t
            live = jnp.concatenate([live_cols[HALO:, t : t + 1], live_cols[:HALO, t + 1 : t + 2]], axis=0)
            shown = jnp.where(live == 1.0, mixed[i], jnp.zeros_like(mixed[i]))
            lo, hi = (HALO if t == 0 else 0), (HALO if t == tiles - 1 else 128)
            at = base - HALO
            mixed_ref[at + lo : at + hi, :] = shown[lo:hi]
            grads_ref[at + lo : at + hi, 0:HS] = query_grad[i][lo:hi]
            lo, hi = (96 if t == 0 else 0), (96 if t == tiles - 1 else 128)
            at = base - 96
            for m, grad in enumerate((key_grad[i], value_grad[i])):
                left = carry[m]
                carry[m] = grad[128:]
                if t > 0:
                    grad = jnp.concatenate([grad[:64] + left, grad[64:]], axis=0)
                grads_ref[at + lo : at + hi, (m + 1) * HS : (m + 2) * HS] = grad[lo:hi].astype(BF16)

    attention([0, 1, 2, 3, 4, 5, 6, 7, 8])
    fetches[0].wait()
    input_rows(0, 512)
    input_rows(512, 512)

    fetches[1].wait()
    fetches[2].wait()
    core, zl = shard % 2, (shard // 2) % 2
    qkv = cols_by_cols(grads_ref[...], normed_ref[...]).astype(BF16)
    out = cols_by_cols(mixed_ref[...], cot_ref[...]).astype(BF16)
    full = jnp.concatenate([qkv, out], axis=0)
    for z in range(8):
        both = full[:, z * 128 : (z + 1) * 128].T
        low, high = both[:64], both[64:]
        keep = jnp.where(core == 0, low, high)
        send = jnp.where(core == 0, high, low)
        side = jnp.bitwise_xor(zl, z % 2)
        for m in range(4):
            keep_ref[side, z // 2, m] = keep[:, m * HS : (m + 1) * HS]
            send_ref[side, z // 2, m] = send[:, m * HS : (m + 1) * HS]


def backward(lengths, proj, stats, below, above, gain, qkv_weight, pad2d, frames, normed, cotangent):
    count, width = frames.shape
    vmem = pl.BlockSpec(memory_space=pltpu.VMEM)
    half = count // 2
    shapes = [(4, half, 128)] * 2 + [(2, half, 128)] * 4 + [(2, 4, 4, width // 16, HS)] * 2
    return pl.pallas_call(
        backward_body,
        in_specs=[pl.BlockSpec(memory_space=pltpu.SMEM)] + [vmem] * 7 + [pl.BlockSpec(memory_space=pl.ANY)] * 3,
        out_specs=[vmem] * len(shapes),
        out_shape=[jax.ShapeDtypeStruct(shape, BF16) for shape in shapes],
        scratch_shapes=[
            pltpu.VMEM((4, count + 4 * HALO, HS), BF16),
            pltpu.VMEM((count, 3 * HS), BF16),
            pltpu.VMEM((count, HS), BF16),
            pltpu.VMEM((width, 3 * HS), BF16),
            pltpu.VMEM((count, width), BF16),
            pltpu.VMEM((count, width), BF16),
            pltpu.VMEM((count, width), BF16),
            pltpu.SemaphoreType.DMA((3,)),
        ],
        compiler_params=pltpu.CompilerParams(vmem_limit_bytes=40 << 20),
        name="backward",
    )(lengths, proj, stats, below, above, gain, qkv_weight, pad2d, frames, normed, cotangent)


def swapped(x, axis, bit):
    return lax.ppermute(x, axis, [(i, i ^ bit) for i in range(lax.axis_size(axis))])


def total(*parts):
    summed = parts[0].astype(F32)
    for part in parts[1:]:
        summed = summed + part.astype(F32)
    return summed


def on_device(frames, norm_gain, qkv_weight, out_weight, cotangent, pad_mask, utt_lengths):
    shards = lax.axis_size("tm")
    up = [(i, i + 1) for i in range(shards - 1)]
    down = [(i + 1, i) for i in range(shards - 1)]
    gain = norm_gain[None, :]
    pad2d = pad_mask.reshape(-1, 128)
    proj, stats, first, last, normed = project(frames, gain, qkv_weight, out_weight, cotangent, pad2d)
    below, above = lax.ppermute(last, "tm", up), lax.ppermute(first, "tm", down)
    near, across, *ring, keep, send = backward(
        utt_lengths, proj, stats, below, above, gain, qkv_weight, pad2d, frames, normed, cotangent
    )
    other = swapped(send, "tm", 1)
    across = swapped(across, "mp", 1)
    ring_in = [swapped(ring[k], "mp", 2 * k) for k in (2, 1, 3)]
    stay, cross = total(keep[0], other[0]).astype(BF16), total(keep[1], other[1]).astype(BF16)
    pair = total(stay, swapped(cross, "tm", 2)).astype(BF16)
    groups = [[c + 4 * z for z in range(shards // 4)] for c in range(4)]
    weights = lax.all_to_all(pair, "tm", 0, 0, tiled=True, axis_index_groups=groups)
    (near, across, ring_in), _ = lax.optimization_barrier(((near, across, ring_in), pair))
    col = [total(near[k], across[k]) for k in range(4)]
    col_in = [swapped(col[k].astype(BF16), "mp", 2 * k) for k in (2, 1, 3)]
    ring_in, _ = lax.optimization_barrier((ring_in, [c.astype(BF16) for c in col[1:]]))
    both = lax.optimization_barrier(total(ring[0], *ring_in))
    theirs = swapped(both[1].astype(BF16), "mp", 1)
    qkv_grad = weights[:, :3].astype(F32).sum(axis=0)
    out_grad = weights[:, 3].astype(F32).sum(axis=0)
    (theirs, col_in), _ = lax.optimization_barrier(((theirs, col_in), (qkv_grad, out_grad)))
    first_half = total(both[0], theirs).astype(BF16)
    second_half = total(col[0], *col_in).astype(BF16)
    frame_grad = jnp.concatenate([first_half, second_half], axis=0)
    return frame_grad, qkv_grad, out_grad.T


def solution(mesh):
    placed = (
        P(("batch", "tm"), None),
        P(),
        P(None, None, "mp"),
        P("mp", None),
        P(("batch", "tm"), None),
        P("batch"),
        P("batch"),
    )
    return jax.shard_map(
        on_device,
        mesh=mesh,
        in_specs=placed,
        out_specs=(P(("batch", "tm"), "mp"), P("batch", "tm", "mp"), P(("batch", "mp"), "tm")),
        check_vma=False,
    )
```

```python
import jax
import jax.numpy as jnp
from jax import lax
from jax.experimental import pallas as pl
from jax.experimental.pallas import tpu as pltpu
from jax.sharding import PartitionSpec as P

HS = 128
CH = 32
HALO = 64
EPSILON = 1e-05
SCALE = HS ** (-0.5)
F32 = jnp.float32
BF16 = jnp.bfloat16


def rows_by_rows(left, right):
    return lax.dot_general(left, right, (((1,), (1,)), ((), ())), preferred_element_type=F32)


def cols_by_cols(left, right):
    return lax.dot_general(left, right, (((0,), (0,)), ((), ())), preferred_element_type=F32)


def plain(left, right):
    return jnp.dot(left, right, preferred_element_type=F32)


def normalised(values):
    values = values.astype(F32)
    mean = jnp.mean(values, axis=-1, keepdims=True)
    center = values - mean
    inverse = lax.rsqrt(jnp.mean(center * center, axis=-1, keepdims=True) + EPSILON)
    return center * inverse, inverse, mean


def pad_rows(pad_ref, first, count):
    total = pad_ref.shape[0]
    return [pad_ref[pl.ds(jnp.clip(first + i, 0, total - 1), 1), :] for i in range(count)]


def as_columns(rows):
    height = -(-len(rows) // 8) * 8
    full = jnp.concatenate(rows + [jnp.zeros_like(rows[0])] * (height - len(rows)), axis=0)
    return full.T


def project_body(
    frames_hbm, gain_ref, qkv_hbm, out_hbm, cot_hbm, pad_ref, proj_ref, stats_ref, normed_hbm,
    frames_ref, w_scr, out_ref, cot_ref, normed_ref, sems,
):
    count = frames_ref.shape[0]
    rows = count // 2
    halves = [pl.ds(0, rows), pl.ds(rows, rows)]
    moves = [(frames_hbm.at[span], frames_ref.at[span]) for span in halves]
    moves += [(qkv_hbm.at[m], w_scr.at[:, m * HS : (m + 1) * HS]) for m in range(3)]
    moves += [(out_hbm, out_ref), (cot_hbm, cot_ref)]
    moves += [(normed_ref.at[span], normed_hbm.at[span]) for span in halves]
    copies = [pltpu.make_async_copy(source, target, sems.at[i]) for i, (source, target) in enumerate(moves)]
    for i in (0, 2, 3, 4, 1, 5, 6):
        copies[i].start()
    lane = lax.broadcasted_iota(jnp.int32, (rows, 128), 1)

    def norm_rows(half):
        normal_form, inverse, mean = normalised(frames_ref[halves[half], :])
        stats_ref[halves[half], :] = jnp.where(lane == 0, mean, inverse)
        normed = (normal_form * gain_ref[...]).astype(BF16)
        normed_ref[halves[half], :] = normed
        return normed

    def project_rows(half, normed):
        qkv = plain(normed, w_scr[...]).astype(BF16)
        for m in range(3):
            proj_ref[m, halves[half], :] = qkv[:, m * HS : (m + 1) * HS]

    copies[0].wait()
    first = norm_rows(0)
    copies[7].start()
    for i in (2, 3, 4, 1):
        copies[i].wait()
    project_rows(0, first)
    second = norm_rows(1)
    for i in (5, 6):
        copies[i].wait()
    copies[8].start()
    blocks = count // 128
    live = as_columns([r.astype(F32) for r in pad_rows(pad_ref, lax.axis_index("tm") * blocks, blocks)])
    live = jnp.concatenate([live[:, i : i + 1] for i in range(blocks)], axis=0)
    project_rows(1, second)
    grads = rows_by_rows(cot_ref[...], out_ref[...])
    proj_ref[3] = jnp.where(live == 1.0, grads, 0.0).astype(BF16)
    copies[7].wait()
    copies[8].wait()


def project(frames, gain, qkv_weight, out_weight, cotangent, pad2d):
    count, width = frames.shape
    vmem = pl.BlockSpec(memory_space=pltpu.VMEM)
    hbm = pl.BlockSpec(memory_space=pl.ANY)
    return pl.pallas_call(
        project_body,
        in_specs=[hbm, vmem, hbm, hbm, hbm, vmem],
        out_specs=[vmem, vmem, hbm],
        out_shape=[
            jax.ShapeDtypeStruct((4, count, HS), BF16),
            jax.ShapeDtypeStruct((count, 128), F32),
            jax.ShapeDtypeStruct((count, width), BF16),
        ],
        scratch_shapes=[
            pltpu.VMEM((count, width), BF16),
            pltpu.VMEM((width, 3 * HS), BF16),
            pltpu.VMEM(out_weight.shape, BF16),
            pltpu.VMEM((count, width), BF16),
            pltpu.VMEM((count, width), BF16),
            pltpu.SemaphoreType.DMA((9,)),
        ],
        compiler_params=pltpu.CompilerParams(vmem_limit_bytes=48 << 20),
        name="project",
    )(frames, gain, qkv_weight, out_weight, cotangent, pad2d)


def backward_body(
    len_ref, proj_ref, stats_ref, halo_ref, gain_ref, qkv_ref, out_ref, pad_ref, frames_hbm, normed_hbm, cot_hbm,
    near_ref, across_ref, ring0_ref, ring1_ref, ring2_ref, ring3_ref, keep_ref, send_ref,
    x_scr, grads_ref, mixed_ref, w_scr, frames_ref, normed_ref, cot_ref, sems,
):
    fetches = [
        pltpu.make_async_copy(source, target, sems.at[i])
        for i, (source, target) in enumerate(
            [(frames_hbm, frames_ref), (normed_hbm, normed_ref), (cot_hbm, cot_ref)]
        )
    ]
    for fetch in fetches:
        fetch.start()
    count = proj_ref.shape[1]
    tiles = count // 128 + 1
    shard = lax.axis_index("tm")
    first_block = shard * (count // 128) - 1
    normal_form, _, _ = normalised(halo_ref[0])
    normed = (normal_form * gain_ref[...]).astype(BF16)
    blocks = tiles + 1
    live_rows = [r.astype(F32) for r in pad_rows(pad_ref, first_block, blocks)]
    live_cols = as_columns(live_rows)
    halo_live = jnp.concatenate([live_cols[HALO:, 0:1], live_cols[:HALO, blocks - 1 : blocks]], axis=0)
    zeros = jnp.zeros((HALO, HS), BF16)
    for m in range(4):
        if m < 3:
            part = plain(normed, qkv_ref[m])
        else:
            part = jnp.where(halo_live == 1.0, rows_by_rows(halo_ref[1], out_ref[...]), 0.0)
        part = part.astype(BF16)
        x_scr[m, 0:HALO, :] = zeros
        x_scr[m, HALO : 2 * HALO, :] = part[:HALO]
        x_scr[m, 2 * HALO : 2 * HALO + count, :] = proj_ref[m]
        x_scr[m, 2 * HALO + count : 3 * HALO + count, :] = part[HALO:]
        x_scr[m, 3 * HALO + count :, :] = zeros

    ends = []
    total = 0
    for u in range(len_ref.shape[0]):
        total = total + len_ref[u]
        ends.append(total)

    def segment(positions):
        found = jnp.zeros(positions.shape, jnp.int32)
        for end in ends:
            found = found + jnp.where(positions >= end, 1, 0)
        return found.astype(F32)

    lane = lax.broadcasted_iota(jnp.int32, (1, 128), 1)
    codes = []
    for b in range(blocks):
        at = (first_block + b) * 128 + lane
        codes.append(jnp.where((live_rows[b] == 1.0) & (at >= 0), segment(at), -1.0))
    code_cols = as_columns(codes)

    keys = 192
    key_at = lax.broadcasted_iota(jnp.int32, (keys, 128), 0)
    query_at = lax.broadcasted_iota(jnp.int32, (keys, 128), 1)
    apart = key_at // CH - query_at // CH
    in_band = (apart >= 0) & (apart <= 2)
    same = key_at == query_at + CH

    place = lax.axis_index("mp")
    owners = [jnp.bitwise_xor(place, j) for j in range(8)]
    spans = [pl.ds(pl.multiple_of(owner * 128, 128), 128) for owner in owners]
    for m in range(3):
        for j, span in enumerate(spans):
            w_scr[j * 128 : (j + 1) * 128, m * HS : (m + 1) * HS] = qkv_ref[m, span, :]
    gain = jnp.concatenate([gain_ref[:, span] for span in spans], axis=1)
    ring_refs = (ring0_ref, ring1_ref, ring2_ref, ring3_ref)

    def input_rows(at, rows):
        incoming = rows_by_rows(grads_ref[at : at + rows, :], w_scr[...])
        frames = jnp.concatenate([frames_ref[at : at + rows, span] for span in spans], axis=1)
        center = frames.astype(F32) - stats_ref[at : at + rows, 0:1]
        inverse = stats_ref[at : at + rows, 1:2]
        scaled = incoming * gain
        mean_grad = jnp.mean(scaled, axis=-1, keepdims=True)
        slope = jnp.mean(scaled * center, axis=-1, keepdims=True) * (inverse * inverse)
        result = (inverse * (scaled - mean_grad - center * slope)).astype(BF16)
        split = ring0_ref.shape[1]
        for j in range(8):
            part = result[:, j * 128 : (j + 1) * 128]
            if at < split:
                ring_refs[j // 2][j % 2, at : at + rows, :] = part
            else:
                (near_ref, across_ref)[j % 2][j // 2, at - split : at - split + rows, :] = part

    carry = [None, None]

    def attention(tiles_now):
        q = [x_scr[0, 128 * t + HALO : 128 * t + HALO + 128, :] for t in tiles_now]
        g = [x_scr[3, 128 * t + HALO : 128 * t + HALO + 128, :] for t in tiles_now]
        k = [x_scr[1, 128 * t + CH : 128 * t + CH + keys, :] for t in tiles_now]
        v = [x_scr[2, 128 * t + CH : 128 * t + CH + keys, :] for t in tiles_now]
        n = range(len(tiles_now))
        scores = [rows_by_rows(k[i], q[i]) for i in n]
        prob_grad = [rows_by_rows(v[i], g[i]) for i in n]
        probs = []
        for i in n:
            t = tiles_now[i]
            query_seg = segment((first_block + t) * 128 + HALO + lane)
            code = jnp.concatenate([code_cols[CH:, t : t + 1], code_cols[: keys - 96, t + 1 : t + 2]], axis=0)
            allowed = in_band & ((code == query_seg) | same)
            masked = jnp.where(allowed, scores[i] * SCALE, -1e30)
            weights = jnp.exp(masked - jnp.max(masked, axis=0, keepdims=True))
            probs.append(weights * (1.0 / jnp.sum(weights, axis=0, keepdims=True)))
        rounded = [p.astype(BF16) for p in probs]
        score_grad = []
        for i in n:
            centre = jnp.sum(probs[i] * prob_grad[i], axis=0, keepdims=True)
            score_grad.append((probs[i] * (prob_grad[i] - centre) * SCALE).astype(BF16))
        value_grad = [plain(rounded[i], g[i]) for i in n]
        key_grad = [plain(score_grad[i], q[i]) for i in n]
        mixed = [cols_by_cols(rounded[i], v[i]).astype(BF16) for i in n]
        query_grad = [cols_by_cols(score_grad[i], k[i]).astype(BF16) for i in n]
        for i in n:
            t = tiles_now[i]
            base = 128 * t
            live = jnp.concatenate([live_cols[HALO:, t : t + 1], live_cols[:HALO, t + 1 : t + 2]], axis=0)
            shown = jnp.where(live == 1.0, mixed[i], jnp.zeros_like(mixed[i]))
            lo, hi = (HALO if t == 0 else 0), (HALO if t == tiles - 1 else 128)
            at = base - HALO
            mixed_ref[at + lo : at + hi, :] = shown[lo:hi]
            grads_ref[at + lo : at + hi, 0:HS] = query_grad[i][lo:hi]
            lo, hi = (96 if t == 0 else 0), (96 if t == tiles - 1 else 128)
            at = base - 96
            for m, grad in enumerate((key_grad[i], value_grad[i])):
                left = carry[m]
                carry[m] = grad[128:]
                if t > 0:
                    grad = jnp.concatenate([grad[:64] + left, grad[64:]], axis=0)
                grads_ref[at + lo : at + hi, (m + 1) * HS : (m + 2) * HS] = grad[lo:hi].astype(BF16)

    attention([0, 1, 2, 3, 4, 5, 6, 7, 8])
    fetches[0].wait()
    input_rows(0, ring0_ref.shape[1])
    input_rows(ring0_ref.shape[1], near_ref.shape[1])

    fetches[1].wait()
    fetches[2].wait()
    core, zl = shard % 2, (shard // 2) % 2
    qkv = cols_by_cols(grads_ref[...], normed_ref[...]).astype(BF16)
    out = cols_by_cols(mixed_ref[...], cot_ref[...]).astype(BF16)
    full = jnp.concatenate([qkv, out], axis=0)
    for z in range(8):
        both = full[:, z * 128 : (z + 1) * 128].T
        low, high = both[:64], both[64:]
        keep = jnp.where(core == 0, low, high)
        send = jnp.where(core == 0, high, low)
        side = jnp.bitwise_xor(zl, z % 2)
        for m in range(4):
            keep_ref[side, z // 2, m] = keep[:, m * HS : (m + 1) * HS]
            send_ref[side, z // 2, m] = send[:, m * HS : (m + 1) * HS]


def backward(lengths, proj, stats, halo, gain, qkv_weight, out_weight, pad2d, frames, normed, cotangent):
    count, width = frames.shape
    vmem = pl.BlockSpec(memory_space=pltpu.VMEM)
    split = count * 7 // 16
    shapes = [(4, count - split, 128)] * 2 + [(2, split, 128)] * 4 + [(2, 4, 4, width // 16, HS)] * 2
    return pl.pallas_call(
        backward_body,
        in_specs=[pl.BlockSpec(memory_space=pltpu.SMEM)] + [vmem] * 7 + [pl.BlockSpec(memory_space=pl.ANY)] * 3,
        out_specs=[vmem] * len(shapes),
        out_shape=[jax.ShapeDtypeStruct(shape, BF16) for shape in shapes],
        scratch_shapes=[
            pltpu.VMEM((4, count + 4 * HALO, HS), BF16),
            pltpu.VMEM((count, 3 * HS), BF16),
            pltpu.VMEM((count, HS), BF16),
            pltpu.VMEM((width, 3 * HS), BF16),
            pltpu.VMEM((count, width), BF16),
            pltpu.VMEM((count, width), BF16),
            pltpu.VMEM((count, width), BF16),
            pltpu.SemaphoreType.DMA((3,)),
        ],
        compiler_params=pltpu.CompilerParams(vmem_limit_bytes=40 << 20),
        name="backward",
    )(lengths, proj, stats, halo, gain, qkv_weight, out_weight, pad2d, frames, normed, cotangent)


def swapped(x, axis, bit):
    return lax.ppermute(x, axis, [(i, i ^ bit) for i in range(lax.axis_size(axis))])


def total(*parts):
    summed = parts[0].astype(F32)
    for part in parts[1:]:
        summed = summed + part.astype(F32)
    return summed


def on_device(frames, norm_gain, qkv_weight, out_weight, cotangent, pad_mask, utt_lengths):
    shards = lax.axis_size("tm")
    up = [(i, i + 1) for i in range(shards - 1)]
    down = [(i + 1, i) for i in range(shards - 1)]
    ends = jnp.stack([frames[-HALO:], cotangent[-HALO:]])
    starts = jnp.stack([frames[:HALO], cotangent[:HALO]])
    halo = jnp.concatenate([lax.ppermute(ends, "tm", up), lax.ppermute(starts, "tm", down)], axis=1)
    gain = norm_gain[None, :]
    pad2d = pad_mask.reshape(-1, 128)
    proj, stats, normed = project(frames, gain, qkv_weight, out_weight, cotangent, pad2d)
    near, across, *ring, keep, send = backward(
        utt_lengths, proj, stats, halo, gain, qkv_weight, out_weight, pad2d, frames, normed, cotangent
    )
    other = swapped(send, "tm", 1)
    across = swapped(across, "mp", 1)
    ring_in = [swapped(ring[k], "mp", 2 * k) for k in (2, 1, 3)]
    stay, cross = total(keep[0], other[0]).astype(BF16), total(keep[1], other[1]).astype(BF16)
    pair = total(stay, swapped(cross, "tm", 2)).astype(BF16)
    groups = [[c + 4 * z for z in range(shards // 4)] for c in range(4)]
    weights = lax.all_to_all(pair, "tm", 0, 0, tiled=True, axis_index_groups=groups)
    (near, across, ring_in), _ = lax.optimization_barrier(((near, across, ring_in), pair))
    col = [total(near[k], across[k]) for k in range(4)]
    col_in = [swapped(col[k].astype(BF16), "mp", 2 * k) for k in (2, 1, 3)]
    ring_in, _ = lax.optimization_barrier((ring_in, [c.astype(BF16) for c in col[1:]]))
    both = lax.optimization_barrier(total(ring[0], *ring_in))
    theirs = swapped(both[1].astype(BF16), "mp", 1)
    qkv_grad = weights[:, :3].astype(F32).sum(axis=0)
    out_grad = weights[:, 3].astype(F32).sum(axis=0)
    (theirs, col_in), _ = lax.optimization_barrier(((theirs, col_in), (qkv_grad, out_grad)))
    first_half = total(both[0], theirs).astype(BF16)
    second_half = total(col[0], *col_in).astype(BF16)
    frame_grad = jnp.concatenate([first_half, second_half], axis=0)
    return frame_grad, qkv_grad, out_grad.T


def solution(mesh):
    placed = (
        P(("batch", "tm"), None),
        P(),
        P(None, None, "mp"),
        P("mp", None),
        P(("batch", "tm"), None),
        P("batch"),
        P("batch"),
    )
    return jax.shard_map(
        on_device,
        mesh=mesh,
        in_specs=placed,
        out_specs=(P(("batch", "tm"), "mp"), P("batch", "tm", "mp"), P(("batch", "mp"), "tm")),
        check_vma=False,
    )
```
